32 devices in a mesh: seq: 2 (over y), dp: 16 (over z, x, core).
Axes of the slice: x: 2, y: 2, z: 4, core: 2. Of those that a mesh axis runs over, the one named last changes fastest.
Arguments:
- incoming_activations: bfloat16 [16, 2048, 768], P('dp', 'seq'), may hold values from -6 to 6
- upstream_derivative: bfloat16 [16, 2048, 768], P('dp', 'seq'), may hold values from -6 to 6
- grid_coordinates: int32 [16, 2048], P('dp'), may hold values from 0 to 511, as said below
- word_segment_ids: int32 [16, 2048], P('dp'), may hold values from 0 to 7, never falling along the last dimension, each value on 1 to 384 neighbouring positions
- asking_matrix: bfloat16 [768, 768], P(('seq', 'dp')), may hold values from -0.21875 to 0.21875
- asking_shift: bfloat16 [768], P(('seq', 'dp')), may hold values from -4 to 4
- lookup_matrix: bfloat16 [768, 768], P(('seq', 'dp')), may hold values from -0.21875 to 0.21875
- content_matrix: bfloat16 [768, 768], P(('seq', 'dp')), may hold values from -0.21875 to 0.21875
- content_shift: bfloat16 [768], P(('seq', 'dp')), may hold values from -4 to 4
- mixing_result_matrix: bfloat16 [768, 768], P(('seq', 'dp')), may hold values from -3.5 to 3.5
- mixing_result_shift: bfloat16 [768], P(('seq', 'dp')), may hold values from -4 to 4
- post_mixing_scaling: bfloat16 [768], P(('seq', 'dp')), may hold values from 0.5 to 1.5
- post_mixing_offset: bfloat16 [768], P(('seq', 'dp')), may hold values from -4 to 4
- expand_matrix: bfloat16 [768, 3072], P(('seq', 'dp')), may hold values from -0.21875 to 0.21875
- expand_shift: bfloat16 [3072], P(('seq', 'dp')), may hold values from -4 to 4
- contract_matrix: bfloat16 [3072, 768], P(('seq', 'dp')), may hold values from -0.109375 to 0.109375
- contract_shift: bfloat16 [768], P(('seq', 'dp')), may hold values from -4 to 4
- post_perceptron_scaling: bfloat16 [768], P(('seq', 'dp')), may hold values from 0.5 to 1.5
- post_perceptron_offset: bfloat16 [768], P(('seq', 'dp')), may hold values from -4 to 4
- pair_gate_scores: float32 [12, 512, 512], P(None, ('seq', 'dp')), may hold values from -6 to 6
- gate_random_jitter: float32 [12, 512, 512], P(None, ('seq', 'dp')), may hold values from -6 to 6
- softening_scale: float32 [12], replicated, may hold values from 0.5 to 2
Outputs:
- layer_out: bfloat16 [16, 2048, 768], P('dp', 'seq')
- input_grad: float32 [16, 2048, 768], P('dp', 'seq')
- grad_query_weight: float32 [768, 768], P(('seq', 'dp'))
- grad_query_bias: float32 [768], P(('seq', 'dp'))
- grad_key_weight: float32 [768, 768], P(('seq', 'dp'))
- grad_value_weight: float32 [768, 768], P(('seq', 'dp'))
- grad_value_bias: float32 [768], P(('seq', 'dp'))
- grad_output_weight: float32 [768, 768], P(('seq', 'dp'))
- grad_output_bias: float32 [768], P(('seq', 'dp'))
- grad_first_gain: float32 [768], P(('seq', 'dp'))
- grad_first_shift: float32 [768], P(('seq', 'dp'))
- grad_inner_weight: float32 [768, 3072], P(('seq', 'dp'))
- grad_inner_bias: float32 [3072], P(('seq', 'dp'))
- grad_outer_weight: float32 [3072, 768], P(('seq', 'dp'))
- grad_outer_bias: float32 [768], P(('seq', 'dp'))
- grad_second_gain: float32 [768], P(('seq', 'dp'))
- grad_second_shift: float32 [768], P(('seq', 'dp'))
- mask_logits_gradient: float32 [12, 512, 512], P(None, ('seq', 'dp'))
The draws below stay inside these ranges and needn't reach their ends.
Inputs may be any that keep to these rules, and one draw needn't show every extreme that they name: `grid_coordinates`: in each sequence the positions count up by one from a start of the sequence's own, modulo 512. `word_segment_ids`: in each sequence the numbers never fall and every number appears on consecutive positions, at most 384 of them, one on exactly that many.
All inputs are finite; a program needn't handle non-finite values.
Results may differ from the reference program's by a relative error of at most 0.015.
Values may be sent and summed in bfloat16 or wider, within the bound.
No kernel may reach another device: no remote copies, remote signals or barrier semaphores. Data moves between devices by JAX's collectives and lax.ppermute only.
A program may use at most 320 MiB of HBM per device.

```python
import math
import jax
import jax.numpy as jnp
import numpy as np
from jax import lax

D = 768
FOCUS_COUNT = 12
HD = 64
FF = 3072
POS = 512
LEN = 2048
BLK = 256
SEQS = 16


def draw_grid_coordinates(key, part):
    offsets = jax.random.randint(key, (SEQS, 1), 0, POS)
    steps_along = jnp.arange(LEN, dtype=jnp.int32)[None, :]
    return ((offsets + steps_along) % POS).astype(jnp.int32)


def steps_of(key, shape, pieces, least, high):
    loudness, own = 1.0, jax.random.fold_in(key, 6)
    for axis_at, parts in pieces:
        heights = jnp.exp(jax.random.uniform(jax.random.fold_in(own, axis_at), (parts,), jnp.float32, least / len(pieces), high / len(pieces)))
        loudness = loudness * jnp.repeat(heights, shape[axis_at] // parts).reshape([-1 if axis == axis_at else 1 for axis in range(len(shape))])
    return loudness


def profile(amount, total, limit, lean):
    weights = [(1 << 20) // math.isqrt(rank ** lean) + 1 for rank in range(2, amount + 1)]
    surplus, given = total - limit - (amount - 1), [1] * (amount - 1)
    while surplus > 0:
        candidates = [i for i in range(amount - 1) if given[i] < limit]
        mass, left = sum([weights[i] for i in candidates]), surplus
        for i in candidates:
            addition = min(limit - given[i], max(1, left * weights[i] // mass), surplus)
            given[i] = given[i] + addition
            surplus = surplus - addition
    return np.array([limit] + given)


def ragged(key, amount, total, reach, lean):
    if amount == 2:
        one = jax.random.randint(key, (), max(1, total - reach), min(reach, total - 1) + 1)
        return jnp.stack([one, total - one])
    lengths = jnp.asarray(profile(amount, total, reach, lean), jnp.int32)
    twos = (amount - 1) // 2
    giver, receiver = lengths[1:1 + 2 * twos:2], lengths[2:2 + 2 * twos:2]
    room = jnp.minimum(giver - 1, reach - receiver)
    moved = jax.random.randint(jax.random.fold_in(key, 1), (twos,), 0, 1 << 20) % (room + 1)
    lengths = lengths.at[1:1 + 2 * twos:2].set(giver - moved).at[2:2 + 2 * twos:2].set(receiver + moved)
    return lengths[jax.random.permutation(jax.random.fold_in(key, 2), amount)]


def centred(rng, dims, width, reach, shards=(), kind=jnp.bfloat16):
    result = width * jax.random.normal(rng, dims, jnp.float32)
    if shards:
        result = result * steps_of(rng, dims, shards, -0.22, 0.18)
    return jnp.clip(result, -reach, reach).astype(kind)


def setup_inputs(seed: int = 0) -> dict:
    streams_of = jax.random.split(jax.random.key(seed), 23)
    return {
        "incoming_activations": centred(streams_of[0], (SEQS, LEN, D), 1.0, 6.0, ((0, 16), (1, 2))),
        "upstream_derivative": centred(streams_of[1], (SEQS, LEN, D), 1.0, 6.0, ((0, 16), (1, 2))),
        "grid_coordinates": draw_grid_coordinates(jax.random.fold_in(streams_of[22], 71), 0),
        "word_segment_ids": jax.vmap(lambda own: jnp.searchsorted(jnp.cumsum(ragged(own, LEN // BLK, LEN, BLK + BLK // 2, 0)), jnp.arange(LEN), side="right"))(jax.random.split(streams_of[3], SEQS)).reshape((SEQS, LEN)).astype(jnp.int32),
        "asking_matrix": centred(streams_of[4], (D, D), D ** -0.5, 0.21875, ((0, 32),)),
        "asking_shift": centred(streams_of[5], (D,), 0.3, 4.0, ((0, 32),)),
        "lookup_matrix": centred(streams_of[6], (D, D), D ** -0.5, 0.21875, ((0, 32),)),
        "content_matrix": centred(streams_of[7], (D, D), D ** -0.5, 0.21875, ((0, 32),)),
        "content_shift": centred(streams_of[8], (D,), 0.3, 4.0, ((0, 32),)),
        "mixing_result_matrix": centred(streams_of[9], (D, D), (max(1, D // 256)) ** -0.5, 3.5, ((0, 32),)),
        "mixing_result_shift": centred(streams_of[10], (D,), 0.3, 4.0, ((0, 32),)),
        "post_mixing_scaling": jnp.clip(1.0 + 0.1 * jax.random.normal(streams_of[11], (D,), jnp.float32), 0.5, 1.5).astype(jnp.bfloat16),
        "post_mixing_offset": centred(streams_of[12], (D,), 0.3, 4.0, ((0, 32),)),
        "expand_matrix": centred(streams_of[13], (D, FF), D ** -0.5, 0.21875, ((0, 32),)),
        "expand_shift": centred(streams_of[14], (FF,), 0.3, 4.0, ((0, 32),)),
        "contract_matrix": centred(streams_of[15], (FF, D), FF ** -0.5, 0.109375, ((0, 32),)),
        "contract_shift": centred(streams_of[16], (D,), 0.3, 4.0, ((0, 32),)),
        "post_perceptron_scaling": jnp.clip(1.0 + 0.1 * jax.random.normal(streams_of[17], (D,), jnp.float32), 0.5, 1.5).astype(jnp.bfloat16),
        "post_perceptron_offset": centred(streams_of[18], (D,), 0.3, 4.0, ((0, 32),)),
        "pair_gate_scores": centred(streams_of[19], (FOCUS_COUNT, POS, POS), 1.0, 6.0, ((1, 32),), jnp.float32),
        "gate_random_jitter": centred(streams_of[20], (FOCUS_COUNT, POS, POS), 1.0, 6.0, ((1, 32),), jnp.float32),
        "softening_scale": jnp.clip(jnp.exp(jax.random.uniform(streams_of[21], (FOCUS_COUNT,), jnp.float32, math.log(0.5), math.log(2.0))), 0.5, 2.0),
    }


EPSILON = 1e-06
NEGATIVE = -1e+30
HIGHEST = lax.Precision.HIGHEST

@jax.custom_vjp
def lower_accuracy_cast(v):
    return lax.optimization_barrier(v.astype(jnp.bfloat16)).astype(jnp.float32)

@jax.custom_vjp
def low_back(v):
    return v

def low_keep(v):
    return (lower_accuracy_cast(v), None)

def low_pass(kept, grad):
    return (grad,)

def back_keep(v):
    return (v, None)

def back_low(kept, grad):
    return (lower_accuracy_cast(grad),)
lower_accuracy_cast.defvjp(low_keep, low_pass)
low_back.defvjp(back_keep, back_low)

def matmul(left_side, right_side):
    return jnp.dot(left_side, right_side, precision=HIGHEST)

def layer_norm(values, norm_gain, norm_shift):
    center = values - lax.optimization_barrier(jnp.mean(values, axis=-1, keepdims=True))
    rstdev = lax.rsqrt(lax.optimization_barrier(jnp.mean(center * center, axis=-1, keepdims=True)) + EPSILON)
    return center * rstdev * norm_gain + norm_shift

def attend(query_rows, key_rows, value_rows, location_gate_grid, seq_positions, seq_blocks):
    length = query_rows.shape[0]
    query_heads = query_rows.reshape(length, FOCUS_COUNT, HD)
    key_heads = key_rows.reshape(length, FOCUS_COUNT, HD)
    value_heads = value_rows.reshape(length, FOCUS_COUNT, HD)
    logits = jnp.einsum('qhd,khd->hqk', query_heads, key_heads, precision=HIGHEST) * (1.0 / math.sqrt(HD))
    logits = logits + 4.0 * location_gate_grid[:, seq_positions[:, None], seq_positions[None, :]]
    logits = low_back(logits)
    allowed = seq_blocks[None, :] <= seq_blocks[:, None]
    logits = jnp.where(allowed[None], logits, NEGATIVE)
    softmax_low = lower_accuracy_cast(jax.nn.softmax(logits, axis=-1))
    mixture = jnp.einsum('hqk,khd->qhd', softmax_low, value_heads, precision=HIGHEST)
    return mixture.reshape(length, FOCUS_COUNT * HD)
checked_attend = jax.checkpoint(attend)

def apply_encoder_unit(encoder_settings, activation_vector, location_ids_bundled, segment_ids_bundled, gate_random_jitter, softening_scale):
    asking_matrix, asking_shift, lookup_matrix, content_matrix, content_shift, mixing_result_matrix, mixing_result_shift, post_mixing_scaling, post_mixing_offset, expand_matrix, expand_shift, contract_matrix, contract_shift, post_perceptron_scaling, post_perceptron_offset, pair_gate_scores = encoder_settings
    location_gate_grid = lower_accuracy_cast(jax.nn.sigmoid((pair_gate_scores + gate_random_jitter) / softening_scale[:, None, None]))
    seq_count, length, model_width = activation_vector.shape
    token_rows = activation_vector.reshape(seq_count * length, model_width)
    queries = low_back(lower_accuracy_cast(matmul(token_rows, asking_matrix) + asking_shift))
    key_rows = low_back(lower_accuracy_cast(matmul(token_rows, lookup_matrix)))
    value_rows = low_back(lower_accuracy_cast(matmul(token_rows, content_matrix) + content_shift))

    def one_sequence(members):
        return checked_attend(members[0], members[1], members[2], location_gate_grid, members[3], members[4])
    attended = lax.map(one_sequence, (queries.reshape(activation_vector.shape), key_rows.reshape(activation_vector.shape), value_rows.reshape(activation_vector.shape), location_ids_bundled, segment_ids_bundled))
    attended = low_back(lower_accuracy_cast(attended.reshape(seq_count * length, model_width)))
    projected = low_back(matmul(attended, mixing_result_matrix) + mixing_result_shift)
    first_out = layer_norm(token_rows + projected, post_mixing_scaling, post_mixing_offset)
    inner_pre = low_back(matmul(lower_accuracy_cast(first_out), expand_matrix) + expand_shift)
    active = lower_accuracy_cast(jax.nn.gelu(inner_pre))
    outer_pre = low_back(matmul(active, contract_matrix) + contract_shift)
    second = layer_norm(first_out + outer_pre, post_perceptron_scaling, post_perceptron_offset)
    return second.reshape(activation_vector.shape)

def reference(incoming_activations, upstream_derivative, grid_coordinates, word_segment_ids, asking_matrix, asking_shift, lookup_matrix, content_matrix, content_shift, mixing_result_matrix, mixing_result_shift, post_mixing_scaling, post_mixing_offset, expand_matrix, expand_shift, contract_matrix, contract_shift, post_perceptron_scaling, post_perceptron_offset, pair_gate_scores, gate_random_jitter, softening_scale):
    encoder_settings = tuple((item.astype(jnp.float32) for item in (asking_matrix, asking_shift, lookup_matrix, content_matrix, content_shift, mixing_result_matrix, mixing_result_shift, post_mixing_scaling, post_mixing_offset, expand_matrix, expand_shift, contract_matrix, contract_shift, post_perceptron_scaling, post_perceptron_offset, pair_gate_scores)))
    group_size = math.gcd(SEQS, max(1, 4096 // LEN))
    step_count = SEQS // group_size

    def regroup(array):
        return array.reshape((step_count, group_size) + array.shape[1:])

    def one_group(running, members):
        activation_vector, grad_out, location_ids_bundled, segment_ids_bundled = members

        def local_forward(present_settings, present_activation):
            return apply_encoder_unit(present_settings, present_activation, location_ids_bundled, segment_ids_bundled, gate_random_jitter, softening_scale)
        output, pull = jax.vjp(local_forward, encoder_settings, activation_vector)
        grad_params, grad_hidden = pull(grad_out)
        running = jax.tree.map(jnp.add, running, grad_params)
        return (running, (output.astype(jnp.bfloat16), grad_hidden))
    zeros = tuple((jnp.zeros(item.shape, jnp.float32) for item in encoder_settings))
    totals, (outputs, grads_in) = lax.scan(one_group, zeros, (regroup(incoming_activations.astype(jnp.float32)), regroup(upstream_derivative.astype(jnp.float32)), regroup(grid_coordinates), regroup(word_segment_ids)))
    layer_out = outputs.reshape(SEQS, LEN, D)
    input_grad = grads_in.reshape(SEQS, LEN, D)
    return (layer_out, input_grad, totals[0], totals[1], totals[2], totals[3], totals[4], totals[5], totals[6], totals[7], totals[8], totals[9], totals[10], totals[11], totals[12], totals[13], totals[14], totals[15])
```

```python
import functools
import math

import jax
import jax.numpy as jnp
from jax import lax
from jax.experimental import pallas as pl
from jax.experimental.pallas import tpu as pltpu
from jax.sharding import PartitionSpec as P

EPSILON = 1e-06
LOG2E = math.log2(math.e)
MASKED = -1e30
TILE = 256
NT = (((1,), (1,)), ((), ()))
NN = (((1,), (0,)), ((), ()))


def dot(a, b, dims=NN):
    return lax.dot_general(a, b, dims, preferred_element_type=jnp.float32)


def local_row(block, seq_index, half_blocks):
    return ((block // half_blocks) ^ seq_index) * (half_blocks * TILE) + (block % half_blocks) * TILE


def split_pair(rows):
    lane = lax.broadcasted_iota(jnp.int32, rows.shape, 1)
    zero = jnp.zeros_like(rows)
    return jnp.where(lane < 64, rows, zero), jnp.where(lane < 64, zero, rows)


def attend_kernel(half_blocks, scale, s_ref, nk_ref, qkv_ref, tab_ref, end_ref, att_ref, o32_ref, lse_ref, vt_ref, st_ref, acc_ref):
    block = pl.program_id(1)
    seq_index = s_ref[0]
    table_blocks = tab_ref.shape[1] // TILE

    @pl.when(block == 0)
    def _():
        vt = qkv_ref[:, 256:384].astype(jnp.float32).T
        sub = lax.broadcasted_iota(jnp.int32, vt.shape, 0)
        vt_ref[0] = jnp.where(sub < 64, vt, 1.0).astype(jnp.bfloat16)
        vt_ref[1] = jnp.where(sub < 64, 1.0, vt).astype(jnp.bfloat16)

    here = pl.multiple_of(local_row(block, seq_index, half_blocks), TILE)
    queries = split_pair(qkv_ref[pl.ds(here, TILE), 0:128])
    row_end = end_ref[0:1, :]
    sub = lax.broadcasted_iota(jnp.int32, (TILE, TILE), 0)
    count = nk_ref[block]

    def score(j, peaks):
        there = pl.multiple_of(local_row(j, seq_index, half_blocks), TILE)
        keys = qkv_ref[pl.ds(there, TILE), 128:256]
        allowed = sub < row_end - j * TILE
        out = []
        for h in range(2):
            part = tab_ref[h, pl.ds(pl.multiple_of((j % table_blocks) * TILE, TILE), TILE), :]
            x = jnp.where(allowed, dot(keys, queries[h], NT) * scale + part, MASKED)
            st_ref[h, pl.ds(pl.multiple_of(j * TILE, TILE), TILE), :] = x
            out.append(jnp.maximum(peaks[h], jnp.max(x.reshape(TILE // 8, 8, TILE), axis=0)))
        return tuple(out)

    start = jnp.full((8, TILE), MASKED, jnp.float32)
    peaks = lax.fori_loop(0, count, score, (start, start))
    peak = [jnp.max(p, axis=0, keepdims=True) for p in peaks]
    acc_ref[...] = jnp.zeros_like(acc_ref)

    def mix(j, carry):
        there = pl.multiple_of(local_row(j, seq_index, half_blocks), TILE)
        for h in range(2):
            x = st_ref[h, pl.ds(pl.multiple_of(j * TILE, TILE), TILE), :]
            p = jnp.exp2(x - peak[h]).astype(jnp.bfloat16)
            acc_ref[h] += dot(vt_ref[h, :, pl.ds(there, TILE)], p)
        return carry

    lax.fori_loop(0, count, mix, 0)
    out0 = acc_ref[0, 0:64, :] / acc_ref[0, 64:128, :]
    out1 = acc_ref[1, 64:128, :] / acc_ref[1, 0:64, :]
    out = jnp.concatenate([out0, out1], axis=0).T
    o32_ref[...] = out
    att_ref[...] = out.astype(jnp.bfloat16)
    lse0 = peak[0] + jnp.log2(acc_ref[0, 64:65, :])
    lse1 = peak[1] + jnp.log2(acc_ref[1, 0:1, :])
    lse_ref[0] = jnp.concatenate([lse0, lse1, jnp.zeros((6, TILE), jnp.float32)], axis=0)


def attend(qkv, tables, row_end, counts, seq_index, score_scale):
    rows = qkv.shape[0]
    pairs = qkv.shape[1] // 384
    blocks = rows // TILE
    half = blocks // 2
    tsize = tables.shape[1]
    spec = pltpu.PrefetchScalarGridSpec(
        num_scalar_prefetch=2,
        grid=(pairs, blocks),
        in_specs=[
            pl.BlockSpec((rows, 384), lambda p, g, s, n: (0, p)),
            pl.BlockSpec((2, tsize, TILE), lambda p, g, s, n: (p, 0, g % (tsize // TILE))),
            pl.BlockSpec((1, TILE), lambda p, g, s, n: (0, g)),
        ],
        out_specs=[
            pl.BlockSpec((TILE, 128), lambda p, g, s, n: (((g // half) ^ s[0]) * half + g % half, p)),
            pl.BlockSpec((TILE, 128), lambda p, g, s, n: (((g // half) ^ s[0]) * half + g % half, p)),
            pl.BlockSpec((1, 8, TILE), lambda p, g, s, n: (p, 0, g)),
        ],
        scratch_shapes=[
            pltpu.VMEM((2, 128, rows), jnp.bfloat16),
            pltpu.VMEM((2, rows, TILE), jnp.float32),
            pltpu.VMEM((2, 128, TILE), jnp.float32),
        ],
    )
    return pl.pallas_call(
        functools.partial(attend_kernel, half, score_scale * LOG2E),
        grid_spec=spec,
        out_shape=[
            jax.ShapeDtypeStruct((rows, pairs * 128), jnp.bfloat16),
            jax.ShapeDtypeStruct((rows, pairs * 128), jnp.float32),
            jax.ShapeDtypeStruct((pairs, 8, rows), jnp.float32),
        ],
        compiler_params=pltpu.CompilerParams(dimension_semantics=("arbitrary", "arbitrary"), vmem_limit_bytes=40 << 20),
        name="attend",
    )(seq_index, counts, qkv, tables, row_end)


def attend_back_kernel(half_blocks, scale, score_scale, s_ref, nk_ref, qkv_ref, grad_ref, o32_ref, tab_ref, end_ref, lse_ref,
                       dqkv_ref, gtab_ref, kt_ref, dk_ref, dv_ref, dq_ref):
    block = pl.program_id(1)
    seq_index = s_ref[0]
    table_blocks = tab_ref.shape[1] // TILE

    @pl.when(block == 0)
    def _():
        kt = qkv_ref[:, 128:256].astype(jnp.float32).T
        sub = lax.broadcasted_iota(jnp.int32, kt.shape, 0)
        kt_ref[0] = jnp.where(sub < 64, kt, 0.0).astype(jnp.bfloat16)
        kt_ref[1] = jnp.where(sub < 64, 0.0, kt).astype(jnp.bfloat16)
        dk_ref[...] = jnp.zeros_like(dk_ref)
        dv_ref[...] = jnp.zeros_like(dv_ref)
        gtab_ref[...] = jnp.zeros_like(gtab_ref)

    here = pl.multiple_of(local_row(block, seq_index, half_blocks), TILE)
    queries = split_pair(qkv_ref[pl.ds(here, TILE), 0:128])
    grads = split_pair(grad_ref[...])
    row_end = end_ref[0:1, :]
    inner = (grad_ref[...].astype(jnp.float32) * o32_ref[...]).T
    delta = [jnp.sum(inner[0:64], axis=0, keepdims=True), jnp.sum(inner[64:128], axis=0, keepdims=True)]
    lse = [lse_ref[0, 0:1, :], lse_ref[0, 1:2, :]]
    q_stack = jnp.concatenate(queries, axis=0)
    g_stack = jnp.concatenate(grads, axis=0)
    sub = lax.broadcasted_iota(jnp.int32, (TILE, TILE), 0)
    dq_ref[...] = jnp.zeros_like(dq_ref)
    lane0 = pl.multiple_of((block % table_blocks) * TILE, TILE)

    def step(j, carry):
        there = pl.multiple_of(local_row(j, seq_index, half_blocks), TILE)
        keys = qkv_ref[pl.ds(there, TILE), 128:256]
        values = qkv_ref[pl.ds(there, TILE), 256:384]
        allowed = sub < row_end - j * TILE
        trow = pl.multiple_of((j % table_blocks) * TILE, TILE)
        probs, scores = [], []
        for h in range(2):
            part = tab_ref[h, pl.ds(trow, TILE), :]
            x = dot(keys, queries[h], NT) * scale + part - lse[h]
            p = jnp.exp2(jnp.where(allowed, x, MASKED))
            d = p * (dot(values, grads[h], NT) - delta[h])
            gtab_ref[h, pl.ds(trow, TILE), pl.ds(lane0, TILE)] += d
            probs.append(p.astype(jnp.bfloat16))
            scores.append(d.astype(jnp.bfloat16))
        dv_ref[pl.ds(there, TILE), :] += dot(jnp.concatenate(probs, axis=1), g_stack)
        dk_ref[pl.ds(there, TILE), :] += dot(jnp.concatenate(scores, axis=1), q_stack)
        kt = jnp.concatenate([kt_ref[0, :, pl.ds(there, TILE)], kt_ref[1, :, pl.ds(there, TILE)]], axis=1)
        dq_ref[...] += dot(kt, jnp.concatenate(scores, axis=0))
        return carry

    lax.fori_loop(0, nk_ref[block], step, 0)
    dqkv_ref[pl.ds(here, TILE), 0:128] = (dq_ref[...] * score_scale).T.astype(jnp.bfloat16)

    @pl.when(block == pl.num_programs(1) - 1)
    def _():
        dqkv_ref[:, 128:256] = (dk_ref[...] * score_scale).astype(jnp.bfloat16)
        dqkv_ref[:, 256:384] = dv_ref[...].astype(jnp.bfloat16)


def attend_back(qkv, grads, o32, tables, row_end, lse, counts, seq_index, score_scale):
    rows = qkv.shape[0]
    pairs = qkv.shape[1] // 384
    blocks = rows // TILE
    half = blocks // 2
    tsize = tables.shape[1]
    row_map = lambda p, g, s, n: (((g // half) ^ s[0]) * half + g % half, p)
    spec = pltpu.PrefetchScalarGridSpec(
        num_scalar_prefetch=2,
        grid=(pairs, blocks),
        in_specs=[
            pl.BlockSpec((rows, 384), lambda p, g, s, n: (0, p)),
            pl.BlockSpec((TILE, 128), row_map),
            pl.BlockSpec((TILE, 128), row_map),
            pl.BlockSpec((2, tsize, TILE), lambda p, g, s, n: (p, 0, g % (tsize // TILE))),
            pl.BlockSpec((1, TILE), lambda p, g, s, n: (0, g)),
            pl.BlockSpec((1, 8, TILE), lambda p, g, s, n: (p, 0, g)),
        ],
        out_specs=[
            pl.BlockSpec((rows, 384), lambda p, g, s, n: (0, p)),
            pl.BlockSpec((2, tsize, tsize), lambda p, g, s, n: (p, 0, 0)),
        ],
        scratch_shapes=[
            pltpu.VMEM((2, 128, rows), jnp.bfloat16),
            pltpu.VMEM((rows, 128), jnp.float32),
            pltpu.VMEM((rows, 128), jnp.float32),
            pltpu.VMEM((128, TILE), jnp.float32),
        ],
    )
    return pl.pallas_call(
        functools.partial(attend_back_kernel, half, score_scale * LOG2E, score_scale),
        grid_spec=spec,
        out_shape=[
            jax.ShapeDtypeStruct((rows, pairs * 384), jnp.bfloat16),
            jax.ShapeDtypeStruct((2 * pairs, tsize, tsize), jnp.float32),
        ],
        compiler_params=pltpu.CompilerParams(dimension_semantics=("arbitrary", "arbitrary"), vmem_limit_bytes=40 << 20),
        name="attend_back",
    )(seq_index, counts, qkv, grads, o32, tables, row_end, lse)


def matmul(left_side, right_side):
    return jnp.dot(left_side, right_side, preferred_element_type=jnp.float32)


def contract_rows(left_side, right_side):
    return jnp.einsum("rd,re->de", left_side, right_side, preferred_element_type=jnp.float32)


def times_transpose(left_side, right_side):
    return jnp.einsum("re,de->rd", left_side, right_side, preferred_element_type=jnp.float32)


def norm_forward(values, norm_gain, norm_shift):
    center = values - jnp.mean(values, axis=-1, keepdims=True)
    rstdev = lax.rsqrt(jnp.mean(center * center, axis=-1, keepdims=True) + EPSILON)
    normed = center * rstdev
    return (normed * norm_gain + norm_shift, normed, rstdev)


def norm_backward(gradient, normed, rstdev, norm_gain):
    scaled = gradient * norm_gain
    back = rstdev * (
        scaled
        - jnp.mean(scaled, axis=-1, keepdims=True)
        - normed * jnp.mean(scaled * normed, axis=-1, keepdims=True)
    )
    return (back, jnp.sum(gradient * normed, axis=0), jnp.sum(gradient, axis=0))

def swap_seq(value):
    return lax.ppermute(value, "seq", [(0, 1), (1, 0)])


def pair_up(mine, theirs, seq_index):
    first = seq_index == 0
    return jnp.stack([jnp.where(first, mine, theirs), jnp.where(first, theirs, mine)])


def flip_bit(value, axis, bit):
    count = lax.axis_size(axis)
    return lax.ppermute(value, axis, [(i, i ^ bit) for i in range(count)])


def gather_small(value):
    gathered = value[None]
    bit = 1
    for axis in ("dp", "seq"):
        bit = 1
        while bit < lax.axis_size(axis):
            other = flip_bit(gathered, axis, bit)
            low = (lax.axis_index(axis) & bit) == 0
            gathered = jnp.concatenate(
                [jnp.where(low, gathered, other), jnp.where(low, other, gathered)], axis=0
            )
            bit *= 2
    return gathered


def sum_small(value):
    for axis in ("dp", "seq"):
        bit = 1
        while bit < lax.axis_size(axis):
            value = value + flip_bit(value, axis, bit)
            bit *= 2
    return value


def body(
    incoming_activations,
    upstream_derivative,
    grid_coordinates,
    word_segment_ids,
    asking_matrix,
    asking_shift,
    lookup_matrix,
    content_matrix,
    content_shift,
    mixing_result_matrix,
    mixing_result_shift,
    post_mixing_scaling,
    post_mixing_offset,
    expand_matrix,
    expand_shift,
    contract_matrix,
    contract_shift,
    post_perceptron_scaling,
    post_perceptron_offset,
    pair_gate_scores,
    gate_random_jitter,
    softening_scale,
):
    f32, bf16 = jnp.float32, jnp.bfloat16
    heads = softening_scale.shape[0]
    width = incoming_activations.shape[2]
    rows = incoming_activations.shape[1]
    inner = expand_matrix.shape[1]
    tsize = pair_gate_scores.shape[2]
    head_size = width // heads
    score_scale = 1.0 / math.sqrt(head_size)
    half_width, half_heads = width // 2, heads // 2
    pairs = half_heads // 2
    seq_index = lax.axis_index("seq")
    dp_index = lax.axis_index("dp")
    dp_size = lax.axis_size("dp")
    inputs = incoming_activations[0]
    share = asking_matrix.shape[0]

    other_inputs = swap_seq(inputs)
    vectors = gather_small(
        jnp.concatenate(
            [
                asking_shift,
                content_shift,
                mixing_result_shift,
                post_mixing_scaling,
                post_mixing_offset,
                contract_shift,
                post_perceptron_scaling,
                post_perceptron_offset,
                expand_shift,
            ]
        )
    )

    def vector(index, size=share):
        return vectors[:, index * share : index * share + size].reshape(-1).astype(f32)

    def pack_heads(parts):
        return jnp.stack([part.reshape(share, 2, pairs, 128) for part in parts], axis=3).reshape(
            share, 2, 3 * half_width
        )

    packed = pack_heads((asking_matrix, lookup_matrix, content_matrix))
    kept = lax.dynamic_index_in_dim(packed, seq_index, 1, keepdims=False)
    sent = lax.dynamic_index_in_dim(packed, 1 - seq_index, 1, keepdims=False)
    heads_matrix = lax.all_gather(
        pair_up(kept, swap_seq(sent), seq_index), "dp", axis=1, tiled=True
    ).reshape(width, 3 * half_width)

    smoothed_gate = jax.nn.sigmoid(
        (pair_gate_scores + gate_random_jitter) / softening_scale[:, None, None]
    )
    mask_rows = tsize // (2 * dp_size)
    mask_low = smoothed_gate.astype(bf16).reshape(2, half_heads, mask_rows, tsize)
    kept = lax.dynamic_index_in_dim(mask_low, seq_index, 0, keepdims=False)
    sent = lax.dynamic_index_in_dim(mask_low, 1 - seq_index, 0, keepdims=False)
    own_mask = lax.all_gather(
        pair_up(kept, swap_seq(sent), seq_index).transpose(1, 0, 2, 3), "dp", axis=2, tiled=True
    ).reshape(half_heads, tsize, tsize)

    layer_matrix = lax.all_gather(
        jnp.concatenate(
            [mixing_result_matrix, expand_matrix, contract_matrix.reshape(share, inner)], axis=1
        ),
        ("seq", "dp"),
        axis=0,
        tiled=True,
    )
    output_matrix = layer_matrix[:, :width]
    inner_matrix = layer_matrix[:, width : width + inner]
    outer_matrix = layer_matrix[:, width + inner :].reshape(inner, width)

    segments = word_segment_ids[0]
    values_range = jnp.arange(8, dtype=jnp.int32)[:, None]
    segment_ends = jnp.sum((segments[None, :] <= values_range).astype(jnp.int32), axis=1)
    row_end = jnp.sum(
        jnp.where(segments[None, :] == values_range, segment_ends[:, None], 0), axis=0
    )
    counts = (row_end.reshape(-1, TILE)[:, -1] + (TILE - 1)) // TILE
    row_end = row_end[None]
    seq_scalar = seq_index[None].astype(jnp.int32)
    start = grid_coordinates[0, 0]
    turned = (jnp.arange(tsize, dtype=jnp.int32) + start) % tsize
    turn = (turned[:, None] == jnp.arange(tsize, dtype=jnp.int32)[None, :]).astype(bf16)
    tables = jnp.einsum("hab,cb->hca", own_mask, turn, preferred_element_type=f32).astype(bf16)
    tables = jnp.einsum("hca,da->hcd", tables, turn, preferred_element_type=f32) * (4.0 * LOG2E)

    own_columns = lambda index: lax.dynamic_slice_in_dim(
        vector(index), seq_index * half_width, half_width
    ).reshape(pairs, 128)
    query_shift, value_shift = own_columns(0), own_columns(1)
    heads_shift = jnp.stack([query_shift, jnp.zeros_like(query_shift), value_shift], axis=1)
    both_inputs = jnp.concatenate([inputs, other_inputs], axis=0)
    heads_rows = (matmul(both_inputs, heads_matrix) + heads_shift.reshape(-1)).astype(bf16)
    own_attended, own_attended_wide, logsum = attend(
        heads_rows, tables, row_end, counts, seq_scalar, score_scale
    )
    their_attended = swap_seq(own_attended[rows:])
    attended = pair_up(own_attended[:rows], their_attended, seq_index)
    attended = jnp.concatenate([attended[0], attended[1]], axis=1)

    first_scale, first_offset = vector(3), vector(4)
    second_scale, second_offset = vector(6), vector(7)
    projected = matmul(attended, output_matrix) + vector(2)
    first_out, first_normed, first_rstdev = norm_forward(
        inputs.astype(f32) + projected, first_scale, first_offset
    )
    first_low = first_out.astype(bf16)
    inner_pre = matmul(first_low, inner_matrix) + vector(8, expand_shift.shape[0])
    active_low = jax.nn.gelu(inner_pre).astype(bf16)
    outer_pre = matmul(active_low, outer_matrix) + vector(5)
    second, second_normed, second_rstdev = norm_forward(
        first_out + outer_pre, second_scale, second_offset
    )
    layer_out = second.astype(bf16)

    grad_out = upstream_derivative[0].astype(f32)
    grad_sum, grad_second_gain, grad_second_shift = norm_backward(
        grad_out, second_normed, second_rstdev, second_scale
    )
    grad_outer_low = grad_sum.astype(bf16)
    grad_active = times_transpose(grad_outer_low, outer_matrix)
    unused_value, gelu_pull = jax.vjp(jax.nn.gelu, inner_pre)
    grad_inner_low = gelu_pull(grad_active)[0].astype(bf16)
    grad_first = grad_sum + times_transpose(grad_inner_low, inner_matrix)
    grad_summed, grad_first_gain, grad_first_shift = norm_backward(
        grad_first, first_normed, first_rstdev, first_scale
    )
    grad_proj_low = grad_summed.astype(bf16)
    grad_attended = times_transpose(grad_proj_low, output_matrix).astype(bf16)
    grad_halves = grad_attended.reshape(rows, 2, half_width)
    own_grad = lax.dynamic_index_in_dim(grad_halves, seq_index, 1, keepdims=False)
    sent_grad = lax.dynamic_index_in_dim(grad_halves, 1 - seq_index, 1, keepdims=False)
    grads_all = jnp.concatenate([own_grad, swap_seq(sent_grad)], axis=0)

    grad_outer_weight = contract_rows(active_low, grad_outer_low).astype(bf16)
    grad_inner_weight = contract_rows(first_low, grad_inner_low).astype(bf16)
    grad_output_weight = contract_rows(attended, grad_proj_low).astype(bf16)
    layer_grad = lax.psum_scatter(
        jnp.concatenate(
            [grad_output_weight, grad_inner_weight, grad_outer_weight.reshape(width, inner)], axis=1
        ),
        ("seq", "dp"),
        scatter_dimension=0,
        tiled=True,
    ).astype(f32)

    grad_heads, grad_tables = attend_back(
        heads_rows, grads_all, own_attended_wide, tables, row_end, logsum, counts, seq_scalar, score_scale
    )
    grad_input_parts = times_transpose(grad_heads, heads_matrix)
    their_part = swap_seq(grad_input_parts[rows:].astype(bf16))
    input_grad = grad_summed + grad_input_parts[:rows] + their_part.astype(f32)
    grad_heads_weight = contract_rows(both_inputs, grad_heads).astype(bf16)

    grad_tables = jnp.einsum(
        "da,hcd->hac", turn, grad_tables.astype(bf16), preferred_element_type=f32
    ).astype(bf16)
    grad_mask = jnp.einsum("hac,cb->hab", grad_tables, turn, preferred_element_type=f32).astype(bf16)
    mask_sum = lax.psum_scatter(
        grad_mask.reshape(half_heads, 2, tsize // 2, tsize), "dp", scatter_dimension=2, tiled=True
    ).astype(f32)
    heads_sum = lax.psum_scatter(
        grad_heads_weight.reshape(2, half_width, 3 * half_width), "dp", scatter_dimension=1, tiled=True
    ).astype(f32)
    kept = lax.dynamic_index_in_dim(mask_sum, seq_index, 1, keepdims=False)
    sent = lax.dynamic_index_in_dim(mask_sum, 1 - seq_index, 1, keepdims=False)
    mask_grad = pair_up(kept, swap_seq(sent), seq_index).reshape(heads, mask_rows, tsize)
    mask_logits_gradient = (
        4.0 * mask_grad * smoothed_gate * (1.0 - smoothed_gate) / softening_scale[:, None, None]
    )
    kept = lax.dynamic_index_in_dim(heads_sum, seq_index, 0, keepdims=False)
    sent = lax.dynamic_index_in_dim(heads_sum, 1 - seq_index, 0, keepdims=False)
    heads_grad = pair_up(kept, swap_seq(sent), seq_index).reshape(2, share, pairs, 3, 128)
    heads_grad = heads_grad.transpose(3, 1, 0, 2, 4).reshape(3, share, width)

    head_bias = jnp.sum(grad_heads.astype(f32), axis=0).reshape(pairs, 3, 128)

    def spread(part):
        return lax.dynamic_update_slice_in_dim(
            jnp.zeros((width,), f32), part.reshape(half_width), seq_index * half_width, 0
        )

    sums = sum_small(
        jnp.concatenate(
            [
                spread(head_bias[:, 0]),
                spread(head_bias[:, 2]),
                jnp.sum(grad_proj_low.astype(f32), axis=0),
                grad_first_gain,
                grad_first_shift,
                jnp.sum(grad_outer_low.astype(f32), axis=0),
                grad_second_gain,
                grad_second_shift,
                jnp.sum(grad_inner_low.astype(f32), axis=0),
            ]
        )
    )
    owner = seq_index * dp_size + dp_index

    def piece(index, size=share):
        return lax.dynamic_slice_in_dim(sums, index * width + owner * size, size)

    return (
        layer_out[None],
        input_grad[None],
        heads_grad[0],
        piece(0),
        heads_grad[1],
        heads_grad[2],
        piece(1),
        layer_grad[:, :width],
        piece(2),
        piece(3),
        piece(4),
        layer_grad[:, width : width + inner],
        piece(8, expand_shift.shape[0]),
        layer_grad[:, width + inner :].reshape(contract_matrix.shape),
        piece(5),
        piece(6),
        piece(7),
        mask_logits_gradient,
    )


def solution(mesh):
    return jax.shard_map(
        body,
        mesh=mesh,
        in_specs=(
            P("dp", "seq", None),
            P("dp", "seq", None),
            P("dp", None),
            P("dp", None),
            P(("seq", "dp"), None),
            P(("seq", "dp")),
            P(("seq", "dp"), None),
            P(("seq", "dp"), None),
            P(("seq", "dp")),
            P(("seq", "dp"), None),
            P(("seq", "dp")),
            P(("seq", "dp")),
            P(("seq", "dp")),
            P(("seq", "dp"), None),
            P(("seq", "dp")),
            P(("seq", "dp"), None),
            P(("seq", "dp")),
            P(("seq", "dp")),
            P(("seq", "dp")),
            P(None, ("seq", "dp"), None),
            P(None, ("seq", "dp"), None),
            P(),
        ),
        out_specs=(
            P("dp", "seq", None),
            P("dp", "seq", None),
            P(("seq", "dp"), None),
            P(("seq", "dp")),
            P(("seq", "dp"), None),
            P(("seq", "dp"), None),
            P(("seq", "dp")),
            P(("seq", "dp"), None),
            P(("seq", "dp")),
            P(("seq", "dp")),
            P(("seq", "dp")),
            P(("seq", "dp"), None),
            P(("seq", "dp")),
            P(("seq", "dp"), None),
            P(("seq", "dp")),
            P(("seq", "dp")),
            P(("seq", "dp")),
            P(None, ("seq", "dp"), None),
        ),
        check_vma=False,
    )
```

```python
import functools
import math

import jax
import jax.numpy as jnp
from jax import lax
from jax.experimental import pallas as pl
from jax.experimental.pallas import tpu as pltpu
from jax.sharding import PartitionSpec as P

EPSILON = 1e-06
LOG2E = math.log2(math.e)
MASKED = -1e30
TILE = 256
NT = (((1,), (1,)), ((), ()))
NN = (((1,), (0,)), ((), ()))
TN = (((0,), (0,)), ((), ()))


def dot(a, b, dims=NN):
    return lax.dot_general(a, b, dims, preferred_element_type=jnp.float32)


def local_row(block, seq_index, half_blocks):
    return ((block // half_blocks) ^ seq_index) * (half_blocks * TILE) + (block % half_blocks) * TILE


def split_pair(rows):
    lane = lax.broadcasted_iota(jnp.int32, rows.shape, 1)
    zero = jnp.zeros_like(rows)
    return jnp.where(lane < 64, rows, zero), jnp.where(lane < 64, zero, rows)


CHUNK = 512
BACK = 512


def chunk_row(block, seq_index, half_blocks):
    return pl.multiple_of(local_row(block, seq_index, half_blocks), TILE)


def attend_kernel(half_blocks, scale, s_ref, nk_ref, full_ref, qkv_ref, tab_ref, end_ref, att_ref, o32_ref, lse_ref, vt_ref, st_ref, acc_ref):
    seq_index = s_ref[0]
    table_size = tab_ref.shape[1]
    per = CHUNK // TILE
    pick = split_pair(jnp.ones((128, 128), jnp.bfloat16))
    reach = jnp.zeros((1, 1), jnp.float32)
    for half in pick:
        longest = []
        for at in (0, 128):
            part = qkv_ref[:, at : at + 128].astype(jnp.float32)
            squares = dot((part * part).astype(jnp.bfloat16), half, NT)
            longest.append(jnp.max(squares, keepdims=True))
        reach = jnp.maximum(reach, jnp.sqrt(longest[0]) * jnp.sqrt(longest[1]) * scale)
    small = reach[0, 0] < 80.0
    vt = qkv_ref[:, 256:384].astype(jnp.float32).T
    sub = lax.broadcasted_iota(jnp.int32, vt.shape, 0)
    vt_ref[0, 0:128] = jnp.where(sub < 64, vt, 0.0).astype(jnp.bfloat16)
    vt_ref[1, 0:128] = jnp.where(sub < 64, 0.0, vt).astype(jnp.bfloat16)
    sub = lax.broadcasted_iota(jnp.int32, (16, vt.shape[1]), 0)
    vt_ref[0, 128:144] = jnp.where(sub < 8, 1.0, 0.0).astype(jnp.bfloat16)
    vt_ref[1, 128:144] = jnp.where(sub < 8, 0.0, 1.0).astype(jnp.bfloat16)
    sub = lax.broadcasted_iota(jnp.int32, (CHUNK, TILE), 0)

    def query_block(block, carry):
        here = chunk_row(block, seq_index, half_blocks)
        queries = split_pair(qkv_ref[pl.ds(here, TILE), 0:128])
        at = pl.multiple_of(block * TILE, TILE)
        row_end = end_ref[0:1, pl.ds(at, TILE)]
        count = (nk_ref[block] + per - 1) // per
        full = full_ref[block] // CHUNK
        lane0 = pl.multiple_of((block * TILE) % table_size, TILE)

        def logits(j, masked):
            keys = qkv_ref[pl.ds(chunk_row(j * per, seq_index, half_blocks), CHUNK), 128:256]
            trow = pl.multiple_of((j * CHUNK) % table_size, CHUNK)
            out = []
            for h in range(2):
                x = dot(keys, queries[h], NT) * scale + tab_ref[h, pl.ds(trow, CHUNK), pl.ds(lane0, TILE)]
                if masked:
                    x = jnp.where(sub < row_end - j * CHUNK, x, MASKED)
                out.append(x)
            return out

        def accumulate(j, probs):
            there = chunk_row(j * per, seq_index, half_blocks)
            values = jnp.concatenate([vt_ref[h, :, pl.ds(there, CHUNK)] for h in range(2)], axis=1)
            acc_ref[...] += dot(values, jnp.concatenate([p.astype(jnp.bfloat16) for p in probs], axis=0))

        def finish(peak):
            acc = acc_ref[...]
            sums = [acc[128:129], acc[136:137]]
            out = jnp.concatenate([acc[0:64] / sums[0], acc[64:128] / sums[1]], axis=0).T
            o32_ref[pl.ds(here, TILE), :] = out
            att_ref[pl.ds(here, TILE), :] = out.astype(jnp.bfloat16)
            for h in range(2):
                lse_ref[0, h : h + 1, pl.ds(at, TILE)] = peak[h] + jnp.log2(sums[h])

        acc_ref[...] = jnp.zeros_like(acc_ref)

        @pl.when(small)
        def _():
            def step(masked, j, carry):
                accumulate(j, [jnp.exp2(x) for x in logits(j, masked)])
                return carry

            lax.fori_loop(0, full, functools.partial(step, False), 0)
            lax.fori_loop(full, count, functools.partial(step, True), 0)
            finish([0.0, 0.0])

        @pl.when(jnp.logical_not(small))
        def _():
            def score(j, peaks):
                out = []
                for h, x in enumerate(logits(j, True)):
                    st_ref[h, pl.ds(pl.multiple_of(j * CHUNK, CHUNK), CHUNK), :] = x
                    out.append(jnp.maximum(peaks[h], jnp.max(x.reshape(CHUNK // 8, 8, TILE), axis=0)))
                return tuple(out)

            start = jnp.full((8, TILE), MASKED, jnp.float32)
            peaks = lax.fori_loop(0, count, score, (start, start))
            peak = [jnp.max(p, axis=0, keepdims=True) for p in peaks]

            def mix(j, carry):
                at_chunk = pl.ds(pl.multiple_of(j * CHUNK, CHUNK), CHUNK)
                accumulate(j, [jnp.exp2(st_ref[h, at_chunk, :] - peak[h]) for h in range(2)])
                return carry

            lax.fori_loop(0, count, mix, 0)
            finish(peak)

        return carry

    lax.fori_loop(0, nk_ref.shape[0], query_block, 0)


def attend(qkv, tables, row_end, scalars, score_scale):
    rows = qkv.shape[0]
    pairs = qkv.shape[1] // 384
    tsize = tables.shape[1]
    spec = pltpu.PrefetchScalarGridSpec(
        num_scalar_prefetch=len(scalars),
        grid=(pairs,),
        in_specs=[
            pl.BlockSpec((rows, 384), lambda p, *_: (0, p)),
            pl.BlockSpec((2, tsize, tsize), lambda p, *_: (p, 0, 0)),
            pl.BlockSpec((1, rows), lambda p, *_: (0, 0)),
        ],
        out_specs=[
            pl.BlockSpec((rows, 128), lambda p, *_: (0, p)),
            pl.BlockSpec((rows, 128), lambda p, *_: (0, p)),
            pl.BlockSpec((1, 8, rows), lambda p, *_: (p, 0, 0)),
        ],
        scratch_shapes=[
            pltpu.VMEM((2, 144, rows), jnp.bfloat16),
            pltpu.VMEM((2, rows, TILE), jnp.float32),
            pltpu.VMEM((144, TILE), jnp.float32),
        ],
    )
    return pl.pallas_call(
        functools.partial(attend_kernel, rows // TILE // 2, score_scale * LOG2E),
        grid_spec=spec,
        out_shape=[
            jax.ShapeDtypeStruct((rows, pairs * 128), jnp.bfloat16),
            jax.ShapeDtypeStruct((rows, pairs * 128), jnp.float32),
            jax.ShapeDtypeStruct((pairs, 8, rows), jnp.float32),
        ],
        compiler_params=pltpu.CompilerParams(dimension_semantics=("arbitrary",), vmem_limit_bytes=40 << 20),
        cost_estimate=pl.CostEstimate(flops=8 * rows * rows * 128, transcendentals=2 * rows * rows, bytes_accessed=8 << 20),
        name="attend",
    )(*scalars, qkv, tables, row_end)


def attend_back_kernel(half_blocks, scale, score_scale, s_ref, nk_ref, full_ref, qkv_ref, grad_ref, o32_ref, tab_ref, end_ref, lse_ref,
                       turned_ref, back_ref, turn_ref, dqkv_ref, table_ref, weight_ref, bias_ref, gtab_ref, kt_ref, dk_ref, dv_ref, dq_ref):
    seq_index = s_ref[0]
    table_size = tab_ref.shape[1]
    per = BACK // TILE
    kt = qkv_ref[:, 128:256].astype(jnp.float32).T
    sub = lax.broadcasted_iota(jnp.int32, kt.shape, 0)
    kt_ref[0] = jnp.where(sub < 64, kt, 0.0).astype(jnp.bfloat16)
    kt_ref[1] = jnp.where(sub < 64, 0.0, kt).astype(jnp.bfloat16)
    dk_ref[...] = jnp.zeros_like(dk_ref)
    dv_ref[...] = jnp.zeros_like(dv_ref)
    gtab_ref[...] = jnp.zeros_like(gtab_ref)
    sub = lax.broadcasted_iota(jnp.int32, (BACK, TILE), 0)

    def query_block(block, carry):
        here = chunk_row(block, seq_index, half_blocks)
        queries = split_pair(qkv_ref[pl.ds(here, TILE), 0:128])
        grad_rows = grad_ref[pl.ds(here, TILE), :]
        grads = split_pair(grad_rows)
        at = pl.multiple_of(block * TILE, TILE)
        row_end = end_ref[0:1, pl.ds(at, TILE)]
        inner = (grad_rows.astype(jnp.float32) * o32_ref[pl.ds(here, TILE), :]).T
        delta = [jnp.sum(inner[0:64], axis=0, keepdims=True), jnp.sum(inner[64:128], axis=0, keepdims=True)]
        lse = [lse_ref[0, h : h + 1, pl.ds(at, TILE)] for h in range(2)]
        q_stack = jnp.concatenate(queries, axis=0)
        g_stack = jnp.concatenate(grads, axis=0)
        lane0 = pl.multiple_of((block * TILE) % table_size, TILE)
        count = (nk_ref[block] + per - 1) // per
        full = full_ref[block] // BACK
        dq_ref[...] = jnp.zeros_like(dq_ref)

        def step(masked, j, carry):
            rows_at = pl.ds(chunk_row(j * per, seq_index, half_blocks), BACK)
            keys = qkv_ref[rows_at, 128:256]
            values = qkv_ref[rows_at, 256:384]
            trow = pl.ds(pl.multiple_of((j * BACK) % table_size, BACK), BACK)
            probs, scores = [], []
            for h in range(2):
                x = dot(keys, queries[h], NT) * scale + tab_ref[h, trow, pl.ds(lane0, TILE)] - lse[h]
                if masked:
                    x = jnp.where(sub < row_end - j * BACK, x, MASKED)
                p = jnp.exp2(x)
                d = p * (dot(values, grads[h], NT) - delta[h])
                gtab_ref[h, trow, pl.ds(lane0, TILE)] += d
                probs.append(p.astype(jnp.bfloat16))
                scores.append(d.astype(jnp.bfloat16))
            dv_ref[rows_at, :] += dot(jnp.concatenate(probs, axis=1), g_stack)
            dk_ref[rows_at, :] += dot(jnp.concatenate(scores, axis=1), q_stack)
            kt = jnp.concatenate([kt_ref[h, :, rows_at] for h in range(2)], axis=1)
            dq_ref[...] += dot(kt, jnp.concatenate(scores, axis=0))
            return carry

        lax.fori_loop(0, full, functools.partial(step, False), 0)
        lax.fori_loop(full, count, functools.partial(step, True), 0)
        dqkv_ref[pl.ds(here, TILE), 0:128] = (dq_ref[...] * score_scale).T.astype(jnp.bfloat16)
        return carry

    lax.fori_loop(0, nk_ref.shape[0], query_block, 0)
    dqkv_ref[:, 128:256] = (dk_ref[...] * score_scale).astype(jnp.bfloat16)
    dqkv_ref[:, 256:384] = dv_ref[...].astype(jnp.bfloat16)
    bias_ref[...] = jnp.broadcast_to(
        jnp.sum(dqkv_ref[...].astype(jnp.float32), axis=0, keepdims=True), bias_ref.shape
    )
    for h in range(2):
        rows = dot(back_ref[...], gtab_ref[h].astype(jnp.bfloat16), NT).astype(jnp.bfloat16)
        table_ref[h] = dot(rows, turn_ref[...]).astype(jnp.bfloat16)

    def weights(i, carry):
        at = pl.ds(pl.multiple_of(i * 128, 128), 128)
        weight_ref[at, :] = dot(turned_ref[:, at], dqkv_ref[...], TN).astype(jnp.bfloat16)
        return carry

    lax.fori_loop(0, weight_ref.shape[0] // 128, weights, 0)


def attend_back(pair, qkv, grads, o32, tables, row_end, lse, turned, back, turn, scalars, score_scale):
    rows = qkv.shape[0]
    tsize = tables.shape[1]
    width = turned.shape[1]
    spec = pltpu.PrefetchScalarGridSpec(
        num_scalar_prefetch=len(scalars),
        grid=(1,),
        in_specs=[
            pl.BlockSpec((rows, 384), lambda p, *_: (0, pair)),
            pl.BlockSpec((rows, 128), lambda p, *_: (0, 0)),
            pl.BlockSpec((rows, 128), lambda p, *_: (0, pair)),
            pl.BlockSpec((2, tsize, tsize), lambda p, *_: (pair, 0, 0)),
            pl.BlockSpec((1, rows), lambda p, *_: (0, 0)),
            pl.BlockSpec((1, 8, rows), lambda p, *_: (pair, 0, 0)),
            pl.BlockSpec((rows, width), lambda p, *_: (0, 0)),
            pl.BlockSpec((tsize, tsize), lambda p, *_: (0, 0)),
            pl.BlockSpec((tsize, tsize), lambda p, *_: (0, 0)),
        ],
        out_specs=[
            pl.BlockSpec((rows, 384), lambda p, *_: (0, 0)),
            pl.BlockSpec((2, tsize, tsize), lambda p, *_: (0, 0, 0)),
            pl.BlockSpec((width, 384), lambda p, *_: (0, 0)),
            pl.BlockSpec((8, 384), lambda p, *_: (0, 0)),
        ],
        scratch_shapes=[
            pltpu.VMEM((2, tsize, tsize), jnp.float32),
            pltpu.VMEM((2, 128, rows), jnp.bfloat16),
            pltpu.VMEM((rows, 128), jnp.float32),
            pltpu.VMEM((rows, 128), jnp.float32),
            pltpu.VMEM((128, TILE), jnp.float32),
        ],
    )
    return pl.pallas_call(
        functools.partial(attend_back_kernel, rows // TILE // 2, score_scale * LOG2E, score_scale),
        grid_spec=spec,
        out_shape=[
            jax.ShapeDtypeStruct((rows, 384), jnp.bfloat16),
            jax.ShapeDtypeStruct((2, tsize, tsize), jnp.bfloat16),
            jax.ShapeDtypeStruct((width, 384), jnp.bfloat16),
            jax.ShapeDtypeStruct((8, 384), jnp.float32),
        ],
        compiler_params=pltpu.CompilerParams(dimension_semantics=("arbitrary",), vmem_limit_bytes=56 << 20),
        cost_estimate=pl.CostEstimate(flops=20 * rows * rows * 128, transcendentals=2 * rows * rows, bytes_accessed=12 << 20),
        name="attend_back",
    )(*scalars, qkv, grads, o32, tables, row_end, lse, turned, back, turn)

GELU_A = math.sqrt(2.0 / math.pi)
GELU_B = 0.044715


def row_stats(values):
    center = values - jnp.mean(values, axis=-1, keepdims=True)
    rstdev = lax.rsqrt(jnp.mean(center * center, axis=-1, keepdims=True) + EPSILON)
    return center * rstdev, rstdev


def row_back(gradient, normed, rstdev, gain):
    scaled = gradient * gain
    return rstdev * (
        scaled
        - jnp.mean(scaled, axis=-1, keepdims=True)
        - normed * jnp.mean(scaled * normed, axis=-1, keepdims=True)
    )


def layer_kernel(s_ref, *refs):
    f32, bf16 = jnp.float32, jnp.bfloat16
    (own_ref, their_ref, x_ref, up_ref, wide_ref, vec_ref, bias_ref,
     out_ref, gsum_ref, gatt_ref, att_ref, first_ref, active_ref, ginner_ref, gouter_ref, gproj_ref,
     vsum_ref, bsum_ref, slope_ref, acc_ref, n1_ref, f1_ref) = refs
    width = x_ref.shape[1]
    inner = active_ref.shape[1]
    step = width
    vec = lambda i: vec_ref[i : i + 1, :]
    total = lambda value: jnp.sum(value, axis=0, keepdims=True)

    def outer_rows(c):
        return wide_ref[:, pl.ds(pl.multiple_of(width + inner + c * step, 128), width)]

    @pl.when(pl.program_id(0) == 0)
    def _():
        vsum_ref[...] = jnp.zeros_like(vsum_ref)
        bsum_ref[...] = jnp.zeros_like(bsum_ref)

    first_seq = s_ref[0] == 0
    mine, others = own_ref[...], their_ref[...]

    @pl.when(first_seq)
    def _():
        att_ref[:, : width // 2] = mine
        att_ref[:, width // 2 :] = others

    @pl.when(jnp.logical_not(first_seq))
    def _():
        att_ref[:, : width // 2] = others
        att_ref[:, width // 2 :] = mine

    summed = x_ref[...].astype(f32) + (dot(att_ref[...], wide_ref[:, :width]) + vec(0))
    normed, rstdev1 = row_stats(summed)
    n1_ref[...] = normed
    first = normed * vec(1) + vec(2)
    f1_ref[...] = first
    first_ref[...] = first.astype(bf16)
    acc_ref[...] = jnp.zeros_like(acc_ref)

    def up(c, carry):
        at = pl.ds(pl.multiple_of(c * step, 128), step)
        w_at = pl.ds(pl.multiple_of(width + c * step, 128), step)
        u = dot(first_ref[...], wide_ref[:, w_at]) + bias_ref[0:1, at]
        square = u * u
        t = jnp.tanh(GELU_A * (u + GELU_B * (square * u)))
        half = 0.5 * (1.0 + t)
        slope_ref[:, at] = half + 0.5 * u * (1.0 - t * t) * (GELU_A * (1.0 + 3.0 * GELU_B * square))
        active = (u * half).astype(bf16)
        active_ref[:, at] = active
        acc_ref[...] += dot(active, outer_rows(c))
        return carry

    lax.fori_loop(0, inner // step, up, 0)
    normed, rstdev = row_stats(f1_ref[...] + (acc_ref[...] + vec(3)))
    out_ref[...] = (normed * vec(4) + vec(5)).astype(bf16)
    gradient = up_ref[...].astype(f32)
    vsum_ref[4:5, :] += total(gradient * normed)
    vsum_ref[5:6, :] += total(gradient)
    grad_sum = row_back(gradient, normed, rstdev, vec(4))
    grad_low = grad_sum.astype(bf16)
    gouter_ref[...] = grad_low
    vsum_ref[3:4, :] += total(grad_low.astype(f32))
    acc_ref[...] = grad_sum

    def down(c, carry):
        at = pl.ds(pl.multiple_of(c * step, 128), step)
        w_at = pl.ds(pl.multiple_of(width + c * step, 128), step)
        g = (dot(gouter_ref[...], outer_rows(c), NT) * slope_ref[:, at]).astype(bf16)
        ginner_ref[:, at] = g
        bsum_ref[0:1, at] += total(g.astype(f32))
        acc_ref[...] += dot(g, wide_ref[:, w_at], NT)
        return carry

    lax.fori_loop(0, inner // step, down, 0)
    grad_first = acc_ref[...]
    normed = n1_ref[...]
    vsum_ref[1:2, :] += total(grad_first * normed)
    vsum_ref[2:3, :] += total(grad_first)
    grad_summed = row_back(grad_first, normed, rstdev1, vec(1))
    gsum_ref[...] = grad_summed
    grad_low = grad_summed.astype(bf16)
    gproj_ref[...] = grad_low
    vsum_ref[0:1, :] += total(grad_low.astype(f32))
    gatt_ref[...] = dot(grad_low, wide_ref[:, :width], NT).astype(bf16)


def layer(seq_index, own, their, x, upstream, wide, vectors, bias):
    rows, width = x.shape
    inner = bias.shape[1]
    block = 256
    by_rows = lambda size: pl.BlockSpec((block, size), lambda i, *_: (i, 0))
    whole = lambda shape: pl.BlockSpec(shape, lambda i, *_: (0,) * len(shape), pipeline_mode=pl.Buffered(1))
    once = lambda shape: pl.BlockSpec(shape, lambda i, *_: (0, 0))
    spec = pltpu.PrefetchScalarGridSpec(
        num_scalar_prefetch=1,
        grid=(rows // block,),
        in_specs=[by_rows(width // 2)] * 2
        + [by_rows(width), by_rows(width), whole(wide.shape), whole(vectors.shape), whole(bias.shape)],
        out_specs=[by_rows(width)] * 5
        + [by_rows(inner)] * 2
        + [by_rows(width)] * 2
        + [once((8, width)), once((8, inner))],
        scratch_shapes=[pltpu.VMEM((block, inner), jnp.float32)] + [pltpu.VMEM((block, width), jnp.float32)] * 3,
    )
    shape = lambda size, dtype: jax.ShapeDtypeStruct((rows, size), dtype)
    low = jnp.bfloat16
    return pl.pallas_call(
        layer_kernel,
        grid_spec=spec,
        out_shape=[shape(width, low), shape(width, jnp.float32), shape(width, low), shape(width, low), shape(width, low)]
        + [shape(inner, low)] * 2
        + [shape(width, low)] * 2
        + [jax.ShapeDtypeStruct((8, width), jnp.float32), jax.ShapeDtypeStruct((8, inner), jnp.float32)],
        compiler_params=pltpu.CompilerParams(dimension_semantics=("arbitrary",), vmem_limit_bytes=56 << 20),
        cost_estimate=pl.CostEstimate(
            flops=8 * rows * width * (width // 2 + inner), transcendentals=rows * inner, bytes_accessed=36 << 20
        ),
        name="layer",
    )(seq_index, own, their, x, upstream, wide, vectors, bias)


def weights_kernel(att_ref, first_ref, active_ref, gproj_ref, gouter_ref, ginner_ref, wide_ref):
    bf16 = jnp.bfloat16
    c = pl.program_id(1)
    width = gproj_ref.shape[1]
    inner = width * pl.num_programs(1)

    @pl.when(c == 0)
    def _():
        wide_ref[:, :width] = dot(att_ref[...], gproj_ref[...], TN).astype(bf16)

    at = pl.ds(pl.multiple_of(width * (c + 1), 128), width)
    wide_ref[:, at] = dot(first_ref[...], ginner_ref[...], TN).astype(bf16)
    at = pl.ds(pl.multiple_of(inner + width * (c + 1), 128), width)
    wide_ref[:, at] = dot(active_ref[...], gouter_ref[...], TN).astype(bf16)


def layer_weights(attended, first, active, gproj, gouter, ginner):
    rows, width = gproj.shape
    inner = ginner.shape[1]
    half = width // 2
    steps = inner // width
    spec = pltpu.PrefetchScalarGridSpec(
        num_scalar_prefetch=0,
        grid=(2, steps),
        in_specs=[
            pl.BlockSpec((rows, half), lambda i, c: (0, i)),
            pl.BlockSpec((rows, half), lambda i, c: (0, i)),
            pl.BlockSpec((rows, half), lambda i, c: (0, 2 * c + i)),
            pl.BlockSpec((rows, width), lambda i, c: (0, 0)),
            pl.BlockSpec((rows, width), lambda i, c: (0, 0)),
            pl.BlockSpec((rows, width), lambda i, c: (0, c)),
        ],
        out_specs=pl.BlockSpec((half, width + 2 * inner), lambda i, c: (i, 0)),
    )
    return pl.pallas_call(
        weights_kernel,
        grid_spec=spec,
        out_shape=jax.ShapeDtypeStruct((width, width + 2 * inner), jnp.bfloat16),
        compiler_params=pltpu.CompilerParams(dimension_semantics=("arbitrary", "arbitrary"), vmem_limit_bytes=56 << 20),
        cost_estimate=pl.CostEstimate(
            flops=4 * rows * width * (width // 2 + inner), transcendentals=0, bytes_accessed=32 << 20
        ),
        name="layer_weights",
    )(attended, first, active, gproj, gouter, ginner)


def matmul(left_side, right_side):
    return jnp.dot(left_side, right_side, preferred_element_type=jnp.float32)


def contract_rows(left_side, right_side):
    return jnp.einsum("rd,re->de", left_side, right_side, preferred_element_type=jnp.float32)


def times_transpose(left_side, right_side):
    return jnp.einsum("re,de->rd", left_side, right_side, preferred_element_type=jnp.float32)


def norm_forward(values, norm_gain, norm_shift):
    center = values - jnp.mean(values, axis=-1, keepdims=True)
    rstdev = lax.rsqrt(jnp.mean(center * center, axis=-1, keepdims=True) + EPSILON)
    normed = center * rstdev
    return (normed * norm_gain + norm_shift, normed, rstdev)


def norm_backward(gradient, normed, rstdev, norm_gain):
    scaled = gradient * norm_gain
    back = rstdev * (
        scaled
        - jnp.mean(scaled, axis=-1, keepdims=True)
        - normed * jnp.mean(scaled * normed, axis=-1, keepdims=True)
    )
    return (back, jnp.sum(gradient * normed, axis=0), jnp.sum(gradient, axis=0))


def swap_seq(value):
    return lax.ppermute(value, "seq", [(0, 1), (1, 0)])


def flip(value, axis, bit):
    return lax.ppermute(value, axis, [(i, i ^ bit) for i in range(lax.axis_size(axis))])


def row_steps():
    bits = [1 << i for i in range(1, lax.axis_size("row").bit_length() - 1)]
    return [("row", bit) for bit in bits], [("row", 1)]


def scatter_order():
    far, near = row_steps()
    return [("core", 1)] + near + far


def coordinates(owner):
    row_size = lax.axis_size("row")
    return {"seq": owner // (2 * row_size), "row": (owner // 2) % row_size, "core": owner % 2}


def places_of(order, count):
    owner = coordinates(jnp.arange(count, dtype=jnp.int32))
    place = jnp.zeros((count,), jnp.int32)
    for step, (axis, bit) in enumerate(order):
        place = place + ((((owner[axis] ^ lax.axis_index(axis)) // bit) & 1) << step)
    return place


def scatter_step(parts, axis, bit):
    half = parts.shape[0] // 2
    arrived = flip(parts[half:], axis, bit)
    return (parts[:half].astype(jnp.float32) + arrived.astype(jnp.float32)).astype(jnp.bfloat16)


def sum_small(value, axes):
    for axis in axes:
        bit = 1
        while bit < lax.axis_size(axis):
            value = value + flip(value, axis, bit)
            bit *= 2
    return value


def body(
    incoming_activations,
    upstream_derivative,
    grid_coordinates,
    word_segment_ids,
    asking_matrix,
    asking_shift,
    lookup_matrix,
    content_matrix,
    content_shift,
    mixing_result_matrix,
    mixing_result_shift,
    post_mixing_scaling,
    post_mixing_offset,
    expand_matrix,
    expand_shift,
    contract_matrix,
    contract_shift,
    post_perceptron_scaling,
    post_perceptron_offset,
    pair_gate_scores,
    gate_random_jitter,
    softening_scale,
):
    f32, bf16 = jnp.float32, jnp.bfloat16
    heads = softening_scale.shape[0]
    width = incoming_activations.shape[2]
    rows = incoming_activations.shape[1]
    inner = expand_matrix.shape[1]
    tsize = pair_gate_scores.shape[2]
    score_scale = 1.0 / math.sqrt(width // heads)
    half_width, half_heads = width // 2, heads // 2
    pairs = half_heads // 2
    seq_index = lax.axis_index("seq")
    dp_size = 2 * lax.axis_size("row")
    dp_index = 2 * lax.axis_index("row") + lax.axis_index("core")
    owner = seq_index * dp_size + dp_index
    first_seq = seq_index == 0
    inputs = incoming_activations[0]
    share = asking_matrix.shape[0]
    inner_share = expand_shift.shape[0]
    mask_rows = tsize // (2 * dp_size)
    lanes = tsize // 128
    everyone = ("seq", "row", "core")

    packed = jnp.stack(
        [part.reshape(share, 2, pairs, 128) for part in (asking_matrix, lookup_matrix, content_matrix)], axis=3
    )
    packed = packed.transpose(1, 2, 3, 0, 4).reshape(2, 3 * pairs * share, 128)
    small = jnp.concatenate(
        [
            asking_shift,
            content_shift,
            mixing_result_shift,
            post_mixing_scaling,
            post_mixing_offset,
            contract_shift,
            post_perceptron_scaling,
            post_perceptron_offset,
            expand_shift,
        ]
    )
    lines = jnp.pad(small, (0, 1024 - small.shape[0])).reshape(1, 8, 128)
    smoothed_gate = jax.nn.sigmoid(
        (pair_gate_scores + gate_random_jitter) / softening_scale[:, None, None]
    )
    mask_low = smoothed_gate.astype(bf16).reshape(2, half_heads, mask_rows, lanes, 128)
    mask_low = mask_low.transpose(0, 1, 3, 2, 4).reshape(2, -1, 128)
    packed = jnp.concatenate([packed, jnp.concatenate([lines, lines], axis=0), mask_low], axis=1)
    kept = lax.dynamic_index_in_dim(packed, seq_index, 0, keepdims=False)
    sent = lax.dynamic_index_in_dim(packed, 1 - seq_index, 0, keepdims=False)
    packed = jnp.concatenate([kept, swap_seq(sent)], axis=0)
    other_inputs = swap_seq(inputs)
    hidden_blocks = inner_share // share
    hidden = expand_matrix.reshape(share, 2 * dp_size, hidden_blocks, share)
    contract_blocks = contract_matrix.reshape(hidden_blocks, share, width)
    wide_share = jnp.concatenate(
        [mixing_result_matrix, hidden.transpose(0, 2, 1, 3).reshape(share, inner)]
        + [contract_blocks[k] for k in range(hidden_blocks)],
        axis=1,
    )
    packed, wide_share = lax.optimization_barrier((packed, wide_share))
    gathered = lax.all_gather(packed, ("row", "core"), axis=0, tiled=True)
    wide_matrix = lax.all_gather(wide_share, everyone, axis=0, tiled=True)
    both_inputs = jnp.concatenate([inputs, other_inputs], axis=0)
    start = grid_coordinates[0, 0]
    turned = (jnp.arange(tsize, dtype=jnp.int32) + start) % tsize
    turn = (turned[:, None] == jnp.arange(tsize, dtype=jnp.int32)[None, :]).astype(bf16)
    row = jnp.arange(mask_rows, dtype=jnp.int32)
    table_order = scatter_order()
    table_places = places_of(table_order[::-1], dp_size)
    own_seq = (jnp.arange(2, dtype=jnp.int32) ^ seq_index)[:, None, None]
    input_spots = ((table_places[None, :] * 2 + own_seq[:, :, 0]) * share)[:, :, None] + jnp.arange(share)
    turned_inputs = matmul(
        both_inputs,
        (input_spots.reshape(-1)[:, None] == jnp.arange(width, dtype=jnp.int32)[None, :]).astype(bf16),
    ).astype(bf16)
    table_spots = ((table_places[None, :] * 2 + own_seq[:, :, 0]) * mask_rows)[:, :, None] + row
    table_spots = table_spots.reshape(-1)
    spot_turn = jnp.sum(jnp.where(turn > 0, table_spots[None, :], 0), axis=1)
    turn_back = (jnp.arange(tsize, dtype=jnp.int32)[:, None] == spot_turn[None, :]).astype(bf16)

    gathered, turned_inputs = lax.optimization_barrier((gathered, turned_inputs))
    gathered = gathered.reshape(dp_size, 2, -1, 128)
    weight_lines = 3 * pairs * share

    def seq_ordered(value):
        mine, others = value[:, 0], value[:, 1]
        return jnp.stack([jnp.where(first_seq, mine, others), jnp.where(first_seq, others, mine)])

    heads_matrix = seq_ordered(gathered[:, :, :weight_lines]).reshape(2, dp_size, 3 * pairs, share, 128)
    heads_matrix = heads_matrix.transpose(0, 1, 3, 2, 4).reshape(width, 3 * half_width)
    vectors = seq_ordered(gathered[:, :, weight_lines : weight_lines + 8]).reshape(2 * dp_size, 1024)
    own_mask = gathered[:, :, weight_lines + 8 :].reshape(dp_size, 2, half_heads, lanes, mask_rows, 128)
    own_mask = own_mask.transpose(2, 0, 1, 4, 3, 5).reshape(half_heads, tsize, tsize)

    def vector(index, size=share):
        return vectors[:, index * share : index * share + size].reshape(-1).astype(f32)

    segments = word_segment_ids[0]
    values_range = jnp.arange(8, dtype=jnp.int32)[:, None]
    segment_ends = jnp.sum((segments[None, :] <= values_range).astype(jnp.int32), axis=1)
    row_end = jnp.sum(jnp.where(segments[None, :] == values_range, segment_ends[:, None], 0), axis=0)
    counts = (row_end.reshape(-1, TILE)[:, -1] + (TILE - 1)) // TILE
    full = row_end.reshape(-1, TILE)[:, 0]
    mask_places = (
        (jnp.arange(2, dtype=jnp.int32) ^ seq_index)[None, :, None] * (tsize // 2)
        + jnp.arange(dp_size, dtype=jnp.int32)[:, None, None] * mask_rows
        + row
    ).reshape(-1)
    turn_rows = (turned[:, None] == mask_places[None, :]).astype(bf16)
    tables = jnp.einsum("hab,cb->hca", own_mask, turn, preferred_element_type=f32).astype(bf16)
    tables = jnp.einsum("hca,da->hcd", tables, turn_rows, preferred_element_type=f32) * (4.0 * LOG2E)

    own_columns = lambda index: lax.dynamic_slice_in_dim(
        vector(index), seq_index * half_width, half_width
    ).reshape(pairs, 128)
    query_shift, value_shift = own_columns(0), own_columns(1)
    heads_shift = jnp.stack([query_shift, jnp.zeros_like(query_shift), value_shift], axis=1)
    heads_rows = (matmul(both_inputs, heads_matrix) + heads_shift.reshape(-1)).astype(bf16)
    seq_scalar = seq_index[None].astype(jnp.int32)
    scalars = (seq_scalar, counts, full)
    row_end = row_end[None]
    own_attended, wide_attended, logsum = attend(heads_rows, tables, row_end, scalars, score_scale)
    their_attended = swap_seq(own_attended[rows:])

    inner_shift = vector(8, inner_share).reshape(2 * dp_size, hidden_blocks, share).transpose(1, 0, 2)
    layer_vectors = jnp.stack([vector(i) for i in (2, 3, 4, 5, 6, 7)] + [jnp.zeros((width,), f32)] * 2)
    (layer_out, grad_summed, grad_attended, attended, first_low, active_low, grad_inner_low, grad_outer_low,
     grad_proj_low, vector_sums, inner_sums) = layer(
        seq_scalar,
        own_attended,
        their_attended,
        inputs,
        upstream_derivative[0],
        wide_matrix,
        layer_vectors,
        inner_shift.reshape(1, inner),
    )
    grads_all = []
    for p in range(pairs):
        low, high = grad_attended[:, p * 128 : (p + 1) * 128], grad_attended[:, (pairs + p) * 128 : (pairs + p + 1) * 128]
        arrived = swap_seq(jnp.where(first_seq, high, low))
        grads_all.append(jnp.concatenate([jnp.where(first_seq, low, high), arrived], axis=0))
    wide_grad = layer_weights(
        attended, first_low, active_low, grad_proj_low, grad_outer_low, grad_inner_low
    )
    wide_grad, grads_all = lax.optimization_barrier((wide_grad, grads_all))
    wide_sum = lax.psum_scatter(wide_grad, everyone, scatter_dimension=0, tiled=True).astype(f32)

    grad_heads, head_bias, chains = [], [], []
    for p in range(pairs):
        grad_pair, table_part, weight_part, bias_part = attend_back(
            p, heads_rows, grads_all[p], wide_attended, tables, row_end, logsum,
            turned_inputs, turn_back, turn, scalars, score_scale,
        )
        grad_heads.append(grad_pair)
        head_bias.append(bias_part[0])
        table_part = table_part.reshape(2, 2 * dp_size, mask_rows, lanes, 128)
        table_part = table_part.transpose(1, 0, 3, 2, 4).reshape(dp_size, 2, -1, 128)
        weight_part = weight_part.reshape(2 * dp_size, share, 3, 128).transpose(0, 2, 1, 3)
        weight_part = weight_part.reshape(dp_size, 2, -1, 128)
        chains.append((jnp.concatenate([table_part, weight_part], axis=2), list(table_order)))
        if p + 1 < pairs:
            moved = []
            for parts, steps in chains:
                if steps:
                    parts = scatter_step(parts, *steps[0])
                moved.append((parts, steps[1:]))
            chains = moved
            held = lax.optimization_barrier((grads_all[p + 1], [c[0] for c in chains]))
            grads_all[p + 1] = held[0]
            chains = [(parts, steps) for parts, (unused, steps) in zip(held[1], chains)]

    grad_heads = jnp.concatenate(grad_heads, axis=1)
    their_part = swap_seq(times_transpose(grad_heads[rows:], heads_matrix).astype(bf16))
    input_grad = grad_summed + times_transpose(grad_heads[:rows], heads_matrix) + their_part.astype(f32)
    own_sums, their_sums = [], []
    for parts, steps in chains:
        for step in steps:
            parts = scatter_step(parts, *step)
        own_sums.append(parts[0, 0])
        their_sums.append(swap_seq(parts[0, 1]))

    own_sums, their_sums = jnp.stack(own_sums), jnp.stack(their_sums)
    both_sums = jnp.stack(
        [jnp.where(first_seq, own_sums, their_sums), jnp.where(first_seq, their_sums, own_sums)]
    ).astype(f32)
    table_lines = 2 * mask_rows * lanes
    table_grad = both_sums[:, :, :table_lines].reshape(2, pairs, 2, lanes, mask_rows, 128)
    table_grad = table_grad.transpose(0, 1, 2, 4, 3, 5).reshape(heads, mask_rows, tsize)
    mask_logits_gradient = (
        4.0 * table_grad * smoothed_gate * (1.0 - smoothed_gate) / softening_scale[:, None, None]
    )
    heads_grad = both_sums[:, :, table_lines:].reshape(2, pairs, 3, share, 128)
    heads_grad = heads_grad.transpose(2, 3, 0, 1, 4).reshape(3, share, width)

    layer_sums = sum_small(
        jnp.concatenate([vector_sums[:6].reshape(-1), inner_sums[0]]), ("core", "row", "seq")
    )
    head_bias = sum_small(
        jnp.stack(head_bias).reshape(pairs, 3, 128)[:, ::2].transpose(1, 0, 2).reshape(-1), ("core", "row")
    )

    def piece(index, size=share):
        return lax.dynamic_slice_in_dim(layer_sums, index * width + owner * size, size)

    def bias_piece(index):
        return lax.dynamic_slice_in_dim(head_bias, index * half_width + dp_index * share, share)

    inner_sum = wide_sum[:, width : width + inner].reshape(share, hidden_blocks, 2 * dp_size, share)
    inner_sum = inner_sum.transpose(0, 2, 1, 3).reshape(share, inner)
    outer_sum = jnp.concatenate(
        [wide_sum[:, width + inner + k * width : width + inner + (k + 1) * width] for k in range(hidden_blocks)], axis=0
    )
    inner_piece = lax.dynamic_slice_in_dim(
        layer_sums[6 * width :].reshape(hidden_blocks, 2 * dp_size, share), owner, 1, 1
    ).reshape(inner_share)
    return (
        layer_out[None],
        input_grad[None],
        heads_grad[0],
        bias_piece(0),
        heads_grad[1],
        heads_grad[2],
        bias_piece(1),
        wide_sum[:, :width],
        piece(0),
        piece(1),
        piece(2),
        inner_sum,
        inner_piece,
        outer_sum,
        piece(3),
        piece(4),
        piece(5),
        mask_logits_gradient,
    )


def solution(mesh):
    split = jax.sharding.Mesh(
        mesh.devices.reshape(2, -1, 2), ("seq", "row", "core")
    )
    return jax.shard_map(
        body,
        mesh=split,
        in_specs=(
            P(("row", "core"), "seq", None),
            P(("row", "core"), "seq", None),
            P(("row", "core"), None),
            P(("row", "core"), None),
            P(("seq", "row", "core"), None),
            P(("seq", "row", "core")),
            P(("seq", "row", "core"), None),
            P(("seq", "row", "core"), None),
            P(("seq", "row", "core")),
            P(("seq", "row", "core"), None),
            P(("seq", "row", "core")),
            P(("seq", "row", "core")),
            P(("seq", "row", "core")),
            P(("seq", "row", "core"), None),
            P(("seq", "row", "core")),
            P(("seq", "row", "core"), None),
            P(("seq", "row", "core")),
            P(("seq", "row", "core")),
            P(("seq", "row", "core")),
            P(None, ("seq", "row", "core"), None),
            P(None, ("seq", "row", "core"), None),
            P(),
        ),
        out_specs=(
            P(("row", "core"), "seq", None),
            P(("row", "core"), "seq", None),
            P(("seq", "row", "core"), None),
            P(("seq", "row", "core")),
            P(("seq", "row", "core"), None),
            P(("seq", "row", "core"), None),
            P(("seq", "row", "core")),
            P(("seq", "row", "core"), None),
            P(("seq", "row", "core")),
            P(("seq", "row", "core")),
            P(("seq", "row", "core")),
            P(("seq", "row", "core"), None),
            P(("seq", "row", "core")),
            P(("seq", "row", "core"), None),
            P(("seq", "row", "core")),
            P(("seq", "row", "core")),
            P(("seq", "row", "core")),
            P(None, ("seq", "row", "core"), None),
        ),
        check_vma=False,
    )
```

```python
import functools
import math

import jax
import jax.numpy as jnp
from jax import lax
from jax.experimental import pallas as pl
from jax.experimental.pallas import tpu as pltpu
from jax.sharding import PartitionSpec as P

EPSILON = 1e-06
LOG2E = math.log2(math.e)
MASKED = -1e30
TILE = 256
NT = (((1,), (1,)), ((), ()))
NN = (((1,), (0,)), ((), ()))
TN = (((0,), (0,)), ((), ()))


def dot(a, b, dims=NN):
    return lax.dot_general(a, b, dims, preferred_element_type=jnp.float32)


def local_row(block, seq_index, half_blocks):
    return ((block // half_blocks) ^ seq_index) * (half_blocks * TILE) + (block % half_blocks) * TILE


def split_pair(rows):
    lane = lax.broadcasted_iota(jnp.int32, rows.shape, 1)
    zero = jnp.zeros_like(rows)
    return jnp.where(lane < 64, rows, zero), jnp.where(lane < 64, zero, rows)


CHUNK = 256
UNROLL = 8
BACK = 256
BACK_UNROLL = 4
LINES = 32


def chunk_row(block, seq_index, half_blocks):
    return pl.multiple_of(local_row(block, seq_index, half_blocks), TILE)


def attend_kernel(half_blocks, scale, s_ref, nk_ref, items_ref, qkv_ref, tab_ref, end_ref, att_ref, o32_ref, lse_ref, vt_ref, st_ref, acc_ref, even_ref, odd_ref):
    seq_index = s_ref[0]
    table_size = tab_ref.shape[1]
    per = CHUNK // TILE
    rows = qkv_ref.shape[0]
    pick = split_pair(jnp.ones((128, 128), jnp.bfloat16))
    reach = jnp.zeros((1, 1), jnp.float32)
    for half in pick:
        longest = []
        for at in (0, 128):
            part = qkv_ref[:, at : at + 128].astype(jnp.float32)
            squares = dot((part * part).astype(jnp.bfloat16), half, NT)
            longest.append(jnp.max(squares, keepdims=True))
        reach = jnp.maximum(reach, jnp.sqrt(longest[0]) * jnp.sqrt(longest[1]) * scale)
    small = reach[0, 0] < 80.0
    vt = qkv_ref[:, 256:384].astype(jnp.float32).T
    sub = lax.broadcasted_iota(jnp.int32, vt.shape, 0)
    vt_ref[0, 0:128] = jnp.where(sub < 64, vt, 0.0).astype(jnp.bfloat16)
    vt_ref[1, 0:128] = jnp.where(sub < 64, 0.0, vt).astype(jnp.bfloat16)
    sub = lax.broadcasted_iota(jnp.int32, (16, vt.shape[1]), 0)
    vt_ref[0, 128:144] = jnp.where(sub < 8, 1.0, 0.0).astype(jnp.bfloat16)
    vt_ref[1, 128:144] = jnp.where(sub < 8, 0.0, 1.0).astype(jnp.bfloat16)
    sub = lax.broadcasted_iota(jnp.int32, (CHUNK, TILE), 0)

    def products(block, j):
        queries = split_pair(qkv_ref[pl.ds(chunk_row(block, seq_index, half_blocks), TILE), 0:128])
        keys = qkv_ref[pl.ds(chunk_row((j * per) % (2 * half_blocks), seq_index, half_blocks), CHUNK), 128:256]
        return [dot(keys, queries[h], NT) for h in range(2)]

    def logits(block, j, raw):
        row_end = end_ref[0:1, pl.ds(pl.multiple_of(block * TILE, TILE), TILE)]
        lane0 = pl.multiple_of((block * TILE) % table_size, TILE)
        trow = pl.multiple_of((j * CHUNK) % table_size, CHUNK)
        allowed = sub < row_end - j * CHUNK
        return [
            jnp.where(allowed, raw[h] * scale + tab_ref[h, pl.ds(trow, CHUNK), pl.ds(lane0, TILE)], MASKED)
            for h in range(2)
        ]

    def accumulate(block, j, probs):
        there = chunk_row((j * per) % (2 * half_blocks), seq_index, half_blocks)
        values = jnp.concatenate([vt_ref[h, :, pl.ds(there, CHUNK)] for h in range(2)], axis=1)
        acc_ref[block] += dot(values, jnp.concatenate([p.astype(jnp.bfloat16) for p in probs], axis=0))

    def finish(block, peak):
        here = chunk_row(block, seq_index, half_blocks)
        at = pl.multiple_of(block * TILE, TILE)
        acc = acc_ref[block]
        sums = [acc[128:129], acc[136:137]]
        out = jnp.concatenate([acc[0:64] / sums[0], acc[64:128] / sums[1]], axis=0).T
        o32_ref[pl.ds(here, TILE), :] = out
        att_ref[pl.ds(here, TILE), :] = out.astype(jnp.bfloat16)
        for h in range(2):
            lse_ref[0, h : h + 1, pl.ds(at, TILE)] = peak[h] + jnp.log2(sums[h])

    acc_ref[...] = jnp.zeros_like(acc_ref)

    @pl.when(small)
    def _():
        last = nk_ref.shape[0] - 1
        buffers = (even_ref, odd_ref)

        def prepare(t, to_ref):
            for h, raw in enumerate(products(jnp.minimum(items_ref[0, t], last), items_ref[1, t])):
                to_ref[h] = raw

        def use(t, from_ref):
            block, j = jnp.minimum(items_ref[0, t], last), items_ref[1, t]
            accumulate(block, j, [jnp.exp2(x) for x in logits(block, j, [from_ref[h] for h in range(2)])])

        prepare(0, even_ref)

        def step(i, carry):
            for u in range(0, UNROLL, 2):
                t = UNROLL * i + u
                prepare(t + 1, odd_ref)
                use(t, even_ref)
                prepare(t + 2, even_ref)
                use(t + 1, odd_ref)
            return carry

        lax.fori_loop(0, (items_ref[2, 0] + UNROLL - 1) // UNROLL, step, 0)

        def close(block, carry):
            finish(block, [0.0, 0.0])
            return carry

        lax.fori_loop(0, last + 1, close, 0)

    @pl.when(jnp.logical_not(small))
    def _():
        def query_block(block, carry):
            count = (nk_ref[block] + per - 1) // per

            def score(j, peaks):
                out = []
                for h, x in enumerate(logits(block, j, products(block, j))):
                    st_ref[h, pl.ds(pl.multiple_of(j * CHUNK, CHUNK), CHUNK), :] = x
                    out.append(jnp.maximum(peaks[h], jnp.max(x.reshape(CHUNK // 8, 8, TILE), axis=0)))
                return tuple(out)

            start = jnp.full((8, TILE), MASKED, jnp.float32)
            peaks = lax.fori_loop(0, count, score, (start, start))
            peak = [jnp.max(p, axis=0, keepdims=True) for p in peaks]

            def mix(j, carry):
                at_chunk = pl.ds(pl.multiple_of(j * CHUNK, CHUNK), CHUNK)
                accumulate(block, j, [jnp.exp2(st_ref[h, at_chunk, :] - peak[h]) for h in range(2)])
                return carry

            lax.fori_loop(0, count, mix, 0)
            finish(block, peak)
            return carry

        lax.fori_loop(0, nk_ref.shape[0], query_block, 0)


def work_items(counts, per):
    chunks = (counts + (per - 1)) // per
    ends = jnp.sum(jnp.where(jnp.arange(len(counts))[:, None] >= jnp.arange(len(counts))[None, :], chunks[None, :], 0), axis=1)
    step = jnp.arange(len(counts) * len(counts) // per + 16, dtype=jnp.int32)
    block = jnp.sum((step[:, None] >= ends[None, :]).astype(jnp.int32), axis=1)
    first = jnp.sum(jnp.where(jnp.arange(len(counts))[None, :] < block[:, None], chunks[None, :], 0), axis=1)
    inside = block < len(counts)
    chunk = jnp.where(inside, step - first, len(counts) // per)
    return jnp.stack([jnp.where(inside, block, len(counts)), chunk, jnp.full_like(step, ends[-1])]).astype(jnp.int32)


def attend(qkv, tables, row_end, scalars, score_scale):
    rows = qkv.shape[0]
    pairs = qkv.shape[1] // 384
    tsize = tables.shape[1]
    spec = pltpu.PrefetchScalarGridSpec(
        num_scalar_prefetch=len(scalars),
        grid=(pairs,),
        in_specs=[
            pl.BlockSpec((rows, 384), lambda p, *_: (0, p)),
            pl.BlockSpec((2, tsize, tsize), lambda p, *_: (p, 0, 0)),
            pl.BlockSpec((1, rows), lambda p, *_: (0, 0)),
        ],
        out_specs=[
            pl.BlockSpec((rows, 128), lambda p, *_: (0, p)),
            pl.BlockSpec((rows, 128), lambda p, *_: (0, p)),
            pl.BlockSpec((1, 8, rows), lambda p, *_: (p, 0, 0)),
        ],
        scratch_shapes=[
            pltpu.VMEM((2, 144, rows), jnp.bfloat16),
            pltpu.VMEM((2, rows, TILE), jnp.float32),
            pltpu.VMEM((rows // TILE, 144, TILE), jnp.float32),
            pltpu.VMEM((2, CHUNK, TILE), jnp.float32),
            pltpu.VMEM((2, CHUNK, TILE), jnp.float32),
        ],
    )
    return pl.pallas_call(
        functools.partial(attend_kernel, rows // TILE // 2, score_scale * LOG2E),
        grid_spec=spec,
        out_shape=[
            jax.ShapeDtypeStruct((rows, pairs * 128), jnp.bfloat16),
            jax.ShapeDtypeStruct((rows, pairs * 128), jnp.float32),
            jax.ShapeDtypeStruct((pairs, 8, rows), jnp.float32),
        ],
        compiler_params=pltpu.CompilerParams(dimension_semantics=("arbitrary",), vmem_limit_bytes=40 << 20),
        cost_estimate=pl.CostEstimate(flops=40 * rows * rows * 128, transcendentals=2 * rows * rows, bytes_accessed=8 << 20),
        name="attend",
    )(*scalars, qkv, tables, row_end)


def attend_back_kernel(half_blocks, scale, score_scale, s_ref, items_ref, qkv_ref, grad_ref, o32_ref, tab_ref, end_ref, lse_ref,
                       turned_ref, back_ref, turn_ref, dqkv_ref, parts_ref, gtab_ref, kt_ref, dk_ref, dv_ref,
                       dq_ref, delta_ref, even_ref, odd_ref):
    seq_index = s_ref[0]
    table_size = tab_ref.shape[1]
    per = BACK // TILE
    blocks = 2 * half_blocks
    kt = qkv_ref[:, 128:256].astype(jnp.float32).T
    sub = lax.broadcasted_iota(jnp.int32, kt.shape, 0)
    kt_ref[0] = jnp.where(sub < 64, kt, 0.0).astype(jnp.bfloat16)
    kt_ref[1] = jnp.where(sub < 64, 0.0, kt).astype(jnp.bfloat16)
    dk_ref[...] = jnp.zeros_like(dk_ref)
    dv_ref[...] = jnp.zeros_like(dv_ref)
    dq_ref[...] = jnp.zeros_like(dq_ref)
    gtab_ref[...] = jnp.zeros_like(gtab_ref)
    inner = (grad_ref[...].astype(jnp.float32) * o32_ref[...]).T
    delta_ref[0:1, :] = jnp.sum(inner[0:64], axis=0, keepdims=True)
    delta_ref[1:2, :] = jnp.sum(inner[64:128], axis=0, keepdims=True)
    sub = lax.broadcasted_iota(jnp.int32, (BACK, TILE), 0)

    def item(t):
        block, j = jnp.minimum(items_ref[0, t], blocks - 1), items_ref[1, t]
        here = pl.ds(chunk_row(block, seq_index, half_blocks), TILE)
        there = pl.ds(chunk_row((j * per) % blocks, seq_index, half_blocks), BACK)
        return block, j, here, there

    def prepare(t, to_ref):
        block, j, here, there = item(t)
        queries, grads = split_pair(qkv_ref[here, 0:128]), split_pair(grad_ref[here, :])
        keys, values = qkv_ref[there, 128:256], qkv_ref[there, 256:384]
        for h in range(2):
            to_ref[h] = dot(keys, queries[h], NT)
            to_ref[2 + h] = dot(values, grads[h], NT)

    def use(t, from_ref):
        block, j, here, there = item(t)
        at = pl.ds(pl.multiple_of(block * TILE, TILE), TILE)
        lane0 = pl.ds(pl.multiple_of((block * TILE) % table_size, TILE), TILE)
        trow = pl.ds(pl.multiple_of((j * BACK) % table_size, BACK), BACK)
        allowed = sub < end_ref[0:1, at] - j * BACK
        probs, scores = [], []
        for h in range(2):
            x = from_ref[h] * scale + tab_ref[h, trow, lane0] - lse_ref[0, h : h + 1, at]
            p = jnp.exp2(jnp.where(allowed, x, MASKED))
            d = p * (from_ref[2 + h] - delta_ref[h : h + 1, here])
            gtab_ref[h, trow, lane0] += d
            probs.append(p.astype(jnp.bfloat16))
            scores.append(d.astype(jnp.bfloat16))
        queries, grads = split_pair(qkv_ref[here, 0:128]), split_pair(grad_ref[here, :])
        dv_ref[there, :] += dot(jnp.concatenate(probs, axis=1), jnp.concatenate(grads, axis=0))
        dk_ref[there, :] += dot(jnp.concatenate(scores, axis=1), jnp.concatenate(queries, axis=0))
        kt = jnp.concatenate([kt_ref[h, :, there] for h in range(2)], axis=1)
        dq_ref[block] += dot(kt, jnp.concatenate(scores, axis=0))

    prepare(0, even_ref)

    def step(i, carry):
        for u in range(0, BACK_UNROLL, 2):
            t = BACK_UNROLL * i + u
            prepare(t + 1, odd_ref)
            use(t, even_ref)
            prepare(t + 2, even_ref)
            use(t + 1, odd_ref)
        return carry

    lax.fori_loop(0, (items_ref[2, 0] + BACK_UNROLL - 1) // BACK_UNROLL, step, 0)

    def close(block, carry):
        here = pl.ds(chunk_row(block, seq_index, half_blocks), TILE)
        dqkv_ref[here, 0:128] = (dq_ref[block] * score_scale).T.astype(jnp.bfloat16)
        return carry

    lax.fori_loop(0, blocks, close, 0)
    dqkv_ref[:, 128:256] = (dk_ref[...] * score_scale).astype(jnp.bfloat16)
    dqkv_ref[:, 256:384] = dv_ref[...].astype(jnp.bfloat16)
    owners, lines = 2 * parts_ref.shape[0], parts_ref.shape[3]
    mask_rows = table_size // owners
    share = turned_ref.shape[1] // owners
    table_lines = lines - 3 * LINES
    for h in range(2):
        table = dot(back_ref[...], gtab_ref[h].astype(jnp.bfloat16), NT).astype(jnp.bfloat16)
        table = dot(table, turn_ref[...])
        for i in range(table_size // 128):
            at = (h * (table_size // 128) + i) * mask_rows
            part = table[:, i * 128 : (i + 1) * 128].reshape(owners // 2, 2, mask_rows, 128)
            parts_ref[:, 0, :, at : at + mask_rows, :] = part.astype(jnp.bfloat16)
    bias = jnp.sum(dqkv_ref[...].astype(jnp.float32), axis=0, keepdims=True)
    step = 384 // share
    for i in range(owners // step):
        part = dot(turned_ref[:, i * 384 : (i + 1) * 384], dqkv_ref[...], TN)
        for c in range(3):
            lanes = slice(c * 128, (c + 1) * 128)
            sums = jnp.broadcast_to(bias[:, lanes], (step * (LINES - share), 128))
            block = jnp.concatenate(
                [part[:, lanes].reshape(step, share, 128), sums.reshape(step, LINES - share, 128)], axis=1
            )
            at = table_lines + c * LINES
            block = block.reshape(step // 2, 2, LINES, 128)
            parts_ref[i * step // 2 : (i + 1) * step // 2, 0, :, at : at + LINES, :] = block.astype(jnp.bfloat16)


def attend_back(first, pairs, owners, qkv, grads, o32, tables, row_end, lse, turned, back, turn, scalars, score_scale):
    rows = qkv.shape[0]
    tsize = tables.shape[1]
    width = turned.shape[1]
    lines = 2 * (tsize // owners) * (tsize // 128) + 3 * LINES
    spec = pltpu.PrefetchScalarGridSpec(
        num_scalar_prefetch=len(scalars),
        grid=(pairs,),
        in_specs=[
            pl.BlockSpec((rows, 384), lambda p, *_: (0, first + p)),
            pl.BlockSpec((rows, 128), lambda p, *_: (0, first + p)),
            pl.BlockSpec((rows, 128), lambda p, *_: (0, first + p)),
            pl.BlockSpec((2, tsize, tsize), lambda p, *_: (first + p, 0, 0)),
            pl.BlockSpec((1, rows), lambda p, *_: (0, 0)),
            pl.BlockSpec((1, 8, rows), lambda p, *_: (first + p, 0, 0)),
            pl.BlockSpec((rows, width), lambda p, *_: (0, 0), pipeline_mode=pl.Buffered(1)),
            pl.BlockSpec((tsize, tsize), lambda p, *_: (0, 0), pipeline_mode=pl.Buffered(1)),
            pl.BlockSpec((tsize, tsize), lambda p, *_: (0, 0), pipeline_mode=pl.Buffered(1)),
        ],
        out_specs=[
            pl.BlockSpec((rows, 384), lambda p, *_: (0, p)),
            pl.BlockSpec((owners // 2, 1, 2, lines, 128), lambda p, *_: (0, p, 0, 0, 0)),
        ],
        scratch_shapes=[
            pltpu.VMEM((2, tsize, tsize), jnp.float32),
            pltpu.VMEM((2, 128, rows), jnp.bfloat16),
            pltpu.VMEM((rows, 128), jnp.float32),
            pltpu.VMEM((rows, 128), jnp.float32),
            pltpu.VMEM((rows // TILE, 128, TILE), jnp.float32),
            pltpu.VMEM((8, rows), jnp.float32),
            pltpu.VMEM((4, BACK, TILE), jnp.float32),
            pltpu.VMEM((4, BACK, TILE), jnp.float32),
        ],
    )
    return pl.pallas_call(
        functools.partial(attend_back_kernel, rows // TILE // 2, score_scale * LOG2E, score_scale),
        grid_spec=spec,
        out_shape=[
            jax.ShapeDtypeStruct((rows, pairs * 384), jnp.bfloat16),
            jax.ShapeDtypeStruct((owners // 2, pairs, 2, lines, 128), jnp.bfloat16),
        ],
        compiler_params=pltpu.CompilerParams(dimension_semantics=("arbitrary",), vmem_limit_bytes=56 << 20),
        cost_estimate=pl.CostEstimate(
            flops=pairs * rows * rows, transcendentals=rows * rows // 64, bytes_accessed=1 << 20
        ),
        name="attend_back",
    )(*scalars, qkv, grads, o32, tables, row_end, lse, turned, back, turn)


GELU_A = math.sqrt(2.0 / math.pi)
GELU_B = 0.044715


def row_stats(values):
    center = values - jnp.mean(values, axis=-1, keepdims=True)
    rstdev = lax.rsqrt(jnp.mean(center * center, axis=-1, keepdims=True) + EPSILON)
    return center * rstdev, rstdev


def row_back(gradient, normed, rstdev, gain):
    scaled = gradient * gain
    return rstdev * (
        scaled
        - jnp.mean(scaled, axis=-1, keepdims=True)
        - normed * jnp.mean(scaled * normed, axis=-1, keepdims=True)
    )


def layer_kernel(s_ref, *refs):
    f32, bf16 = jnp.float32, jnp.bfloat16
    (own_ref, their_ref, x_ref, up_ref, wide_ref,
     out_ref, gsum_ref, gatt_ref, att_ref, first_ref, active_ref, ginner_ref, gouter_ref, gproj_ref,
     vsum_ref, slope_ref, acc_ref, n1_ref, f1_ref, vec_ref) = refs
    width = x_ref.shape[1]
    inner = active_ref.shape[1]
    step = width
    vec = lambda i: vec_ref[i : i + 1, :]
    total = lambda value: jnp.sum(value, axis=0, keepdims=True)

    def outer_rows(c):
        return wide_ref[:, pl.ds(pl.multiple_of(width + inner + c * step, 128), width)]

    @pl.when(pl.program_id(0) == 0)
    def _():
        vsum_ref[...] = jnp.zeros_like(vsum_ref)
        vec_ref[...] = wide_ref[:, width + 2 * inner :].astype(f32).T

    first_seq = s_ref[0] == 0
    mine, others = own_ref[...], their_ref[...]

    @pl.when(first_seq)
    def _():
        att_ref[:, : width // 2] = mine
        att_ref[:, width // 2 :] = others

    @pl.when(jnp.logical_not(first_seq))
    def _():
        att_ref[:, : width // 2] = others
        att_ref[:, width // 2 :] = mine

    summed = x_ref[...].astype(f32) + (dot(att_ref[...], wide_ref[:, :width]) + vec(0))
    normed, rstdev1 = row_stats(summed)
    n1_ref[...] = normed
    first = normed * vec(1) + vec(2)
    f1_ref[...] = first
    first_ref[...] = first.astype(bf16)
    acc_ref[...] = jnp.zeros_like(acc_ref)

    def up(c, carry):
        at = pl.ds(pl.multiple_of(c * step, 128), step)
        w_at = pl.ds(pl.multiple_of(width + c * step, 128), step)
        u = dot(first_ref[...], wide_ref[:, w_at]) + vec_ref[pl.ds(6 + c, 1), :]
        square = u * u
        t = jnp.tanh(GELU_A * (u + GELU_B * (square * u)))
        half = 0.5 * (1.0 + t)
        slope_ref[:, at] = half + 0.5 * u * (1.0 - t * t) * (GELU_A * (1.0 + 3.0 * GELU_B * square))
        active = (u * half).astype(bf16)
        active_ref[:, at] = active
        acc_ref[...] += dot(active, outer_rows(c))
        return carry

    lax.fori_loop(0, inner // step, up, 0)
    normed, rstdev = row_stats(f1_ref[...] + (acc_ref[...] + vec(3)))
    out_ref[...] = (normed * vec(4) + vec(5)).astype(bf16)
    gradient = up_ref[...].astype(f32)
    vsum_ref[4:5, :] += total(gradient * normed)
    vsum_ref[5:6, :] += total(gradient)
    grad_sum = row_back(gradient, normed, rstdev, vec(4))
    grad_low = grad_sum.astype(bf16)
    gouter_ref[...] = grad_low
    vsum_ref[3:4, :] += total(grad_low.astype(f32))
    acc_ref[...] = grad_sum

    def down(c, carry):
        at = pl.ds(pl.multiple_of(c * step, 128), step)
        w_at = pl.ds(pl.multiple_of(width + c * step, 128), step)
        g = (dot(gouter_ref[...], outer_rows(c), NT) * slope_ref[:, at]).astype(bf16)
        ginner_ref[:, at] = g
        vsum_ref[pl.ds(6 + c, 1), :] += total(g.astype(f32))
        acc_ref[...] += dot(g, wide_ref[:, w_at], NT)
        return carry

    lax.fori_loop(0, inner // step, down, 0)
    grad_first = acc_ref[...]
    normed = n1_ref[...]
    vsum_ref[1:2, :] += total(grad_first * normed)
    vsum_ref[2:3, :] += total(grad_first)
    grad_summed = row_back(grad_first, normed, rstdev1, vec(1))
    gsum_ref[...] = grad_summed
    grad_low = grad_summed.astype(bf16)
    gproj_ref[...] = grad_low
    vsum_ref[0:1, :] += total(grad_low.astype(f32))
    gatt_ref[...] = dot(grad_low, wide_ref[:, :width], NT).astype(bf16)


def layer(seq_index, own, their, x, upstream, wide):
    rows, width = x.shape
    inner = (wide.shape[1] - width - 128) // 2
    block = 256
    by_rows = lambda size: pl.BlockSpec((block, size), lambda i, *_: (i, 0))
    whole = lambda shape: pl.BlockSpec(shape, lambda i, *_: (0,) * len(shape), pipeline_mode=pl.Buffered(1))
    once = lambda shape: pl.BlockSpec(shape, lambda i, *_: (0, 0))
    spec = pltpu.PrefetchScalarGridSpec(
        num_scalar_prefetch=1,
        grid=(rows // block,),
        in_specs=[by_rows(width // 2)] * 2
        + [by_rows(width), by_rows(width), whole(wide.shape)],
        out_specs=[by_rows(width)] * 5
        + [by_rows(inner)] * 2
        + [by_rows(width)] * 2
        + [once((16, width))],
        scratch_shapes=[pltpu.VMEM((block, inner), jnp.float32)] + [pltpu.VMEM((block, width), jnp.float32)] * 3
        + [pltpu.VMEM((128, width), jnp.float32)],
    )
    shape = lambda size, dtype: jax.ShapeDtypeStruct((rows, size), dtype)
    low = jnp.bfloat16
    return pl.pallas_call(
        layer_kernel,
        grid_spec=spec,
        out_shape=[shape(width, low), shape(width, jnp.float32), shape(width, low), shape(width, low), shape(width, low)]
        + [shape(inner, low)] * 2
        + [shape(width, low)] * 2
        + [jax.ShapeDtypeStruct((16, width), jnp.float32)],
        compiler_params=pltpu.CompilerParams(dimension_semantics=("arbitrary",), vmem_limit_bytes=56 << 20),
        cost_estimate=pl.CostEstimate(
            flops=8 * rows * width * (width // 2 + inner), transcendentals=rows * inner, bytes_accessed=36 << 20
        ),
        name="layer",
    )(seq_index, own, their, x, upstream, wide)


def weights_kernel(s_ref, place_ref, vsum_ref, att_ref, first_ref, active_ref, gproj_ref, gouter_ref, ginner_ref,
                   wide_ref, mine_ref, their_ref):
    bf16 = jnp.bfloat16
    i, c = pl.program_id(0), pl.program_id(1)
    width = gproj_ref.shape[1]
    inner = width * pl.num_programs(1)
    owners, share = mine_ref.shape[0], mine_ref.shape[3]

    @pl.when(c == 0)
    def _():
        wide_ref[:, :width] = dot(att_ref[...], gproj_ref[...], TN).astype(bf16)
        sums = vsum_ref[...]
        sums = jnp.concatenate([sums, jnp.zeros((128 - sums.shape[0], sums.shape[1]), jnp.float32)], axis=0)
        wide_ref[:, width + inner :] = sums.T.astype(bf16)

    at = pl.ds(pl.multiple_of(width * (c + 1), 128), width)
    wide_ref[:, at] = dot(first_ref[...], ginner_ref[...], TN).astype(bf16)
    part = dot(active_ref[...], gouter_ref[...], TN)

    def place(out_ref):
        for k in range(owners):
            rows = part[k * share : (k + 1) * share].astype(bf16)
            for i in range(width // 128):
                out_ref[place_ref[k], i, c] = rows[:, i * 128 : (i + 1) * 128]

    @pl.when(i == s_ref[0])
    def _():
        place(mine_ref)

    @pl.when(i != s_ref[0])
    def _():
        place(their_ref)


def layer_weights(seq_index, places, sums, attended, first, active, gproj, gouter, ginner):
    rows, width = gproj.shape
    inner = ginner.shape[1]
    half = width // 2
    steps = inner // width
    owners = places.shape[0]
    blocks = (owners, width // 128, steps, half // owners, 128)
    spec = pltpu.PrefetchScalarGridSpec(
        num_scalar_prefetch=2,
        grid=(2, steps),
        in_specs=[
            pl.BlockSpec((sums.shape[0], half), lambda i, c, *_: (0, i)),
            pl.BlockSpec((rows, half), lambda i, c, *_: (0, i)),
            pl.BlockSpec((rows, half), lambda i, c, *_: (0, i)),
            pl.BlockSpec((rows, half), lambda i, c, *_: (0, 2 * c + i)),
            pl.BlockSpec((rows, width), lambda i, c, *_: (0, 0)),
            pl.BlockSpec((rows, width), lambda i, c, *_: (0, 0)),
            pl.BlockSpec((rows, width), lambda i, c, *_: (0, c)),
        ],
        out_specs=[
            pl.BlockSpec((half, width + inner + 128), lambda i, c, *_: (0, i)),
            pl.BlockSpec(blocks, lambda i, c, *_: (0, 0, 0, 0, 0)),
            pl.BlockSpec(blocks, lambda i, c, *_: (0, 0, 0, 0, 0)),
        ],
    )
    return pl.pallas_call(
        weights_kernel,
        grid_spec=spec,
        out_shape=[
            jax.ShapeDtypeStruct((half, 2 * (width + inner + 128)), jnp.bfloat16),
            jax.ShapeDtypeStruct(blocks, jnp.bfloat16),
            jax.ShapeDtypeStruct(blocks, jnp.bfloat16),
        ],
        compiler_params=pltpu.CompilerParams(dimension_semantics=("arbitrary", "arbitrary"), vmem_limit_bytes=56 << 20),
        cost_estimate=pl.CostEstimate(
            flops=4 * rows * width * (width // 2 + inner), transcendentals=0, bytes_accessed=32 << 20
        ),
        name="layer_weights",
    )(seq_index, places, sums, attended, first, active, gproj, gouter, ginner)


def matmul(left_side, right_side):
    return jnp.dot(left_side, right_side, preferred_element_type=jnp.float32)


def contract_rows(left_side, right_side):
    return jnp.einsum("rd,re->de", left_side, right_side, preferred_element_type=jnp.float32)


def times_transpose(left_side, right_side):
    return jnp.einsum("re,de->rd", left_side, right_side, preferred_element_type=jnp.float32)


def norm_forward(values, norm_gain, norm_shift):
    center = values - jnp.mean(values, axis=-1, keepdims=True)
    rstdev = lax.rsqrt(jnp.mean(center * center, axis=-1, keepdims=True) + EPSILON)
    normed = center * rstdev
    return (normed * norm_gain + norm_shift, normed, rstdev)


def norm_backward(gradient, normed, rstdev, norm_gain):
    scaled = gradient * norm_gain
    back = rstdev * (
        scaled
        - jnp.mean(scaled, axis=-1, keepdims=True)
        - normed * jnp.mean(scaled * normed, axis=-1, keepdims=True)
    )
    return (back, jnp.sum(gradient * normed, axis=0), jnp.sum(gradient, axis=0))


def swap_seq(value):
    return lax.ppermute(value, "seq", [(0, 1), (1, 0)])


def flip(value, axis, bit):
    return lax.ppermute(value, axis, [(i, i ^ bit) for i in range(lax.axis_size(axis))])


def row_steps():
    bits = [1 << i for i in range(1, lax.axis_size("row").bit_length() - 1)]
    return [("row", bit) for bit in bits], [("row", 1)]


def scatter_order():
    far, near = row_steps()
    return [("core", 1)] + near + far


def coordinates(owner):
    row_size = lax.axis_size("row")
    return {"seq": owner // (2 * row_size), "row": (owner // 2) % row_size, "core": owner % 2}


def places_of(order, count):
    owner = coordinates(jnp.arange(count, dtype=jnp.int32))
    place = jnp.zeros((count,), jnp.int32)
    for step, (axis, bit) in enumerate(order):
        place = place + ((((owner[axis] ^ lax.axis_index(axis)) // bit) & 1) << step)
    return place


def scatter_start(parts, axis, bit):
    half = parts[0].shape[0] // 2
    kept = [part[:half] for part in parts]
    sent = [part[half:] for part in parts]
    joined = lambda values: values[0] if len(values) == 1 else jnp.concatenate(values, axis=1)
    return joined(kept), flip(joined(sent), axis, bit)


def scatter_end(kept, arrived):
    return (kept.astype(jnp.float32) + arrived.astype(jnp.float32)).astype(jnp.bfloat16)


def body(
    incoming_activations,
    upstream_derivative,
    grid_coordinates,
    word_segment_ids,
    asking_matrix,
    asking_shift,
    lookup_matrix,
    content_matrix,
    content_shift,
    mixing_result_matrix,
    mixing_result_shift,
    post_mixing_scaling,
    post_mixing_offset,
    expand_matrix,
    expand_shift,
    contract_matrix,
    contract_shift,
    post_perceptron_scaling,
    post_perceptron_offset,
    pair_gate_scores,
    gate_random_jitter,
    softening_scale,
):
    f32, bf16 = jnp.float32, jnp.bfloat16
    heads = softening_scale.shape[0]
    width = incoming_activations.shape[2]
    rows = incoming_activations.shape[1]
    inner = expand_matrix.shape[1]
    tsize = pair_gate_scores.shape[2]
    score_scale = 1.0 / math.sqrt(width // heads)
    half_width, half_heads = width // 2, heads // 2
    pairs = half_heads // 2
    seq_index = lax.axis_index("seq")
    dp_size = 2 * lax.axis_size("row")
    dp_index = 2 * lax.axis_index("row") + lax.axis_index("core")
    owner = seq_index * dp_size + dp_index
    first_seq = seq_index == 0
    inputs = incoming_activations[0]
    share = asking_matrix.shape[0]
    inner_share = expand_shift.shape[0]
    mask_rows = tsize // (2 * dp_size)
    lanes = tsize // 128

    def seq_ordered(mine, others):
        return jnp.stack([jnp.where(first_seq, mine, others), jnp.where(first_seq, others, mine)])


    packed = jnp.stack(
        [part.reshape(share, 2, pairs, 128) for part in (asking_matrix, lookup_matrix, content_matrix)], axis=3
    )
    packed = packed.transpose(1, 2, 3, 0, 4).reshape(2, 3 * pairs * share, 128)
    lines = jnp.stack([asking_shift, content_shift])
    lines = jnp.pad(lines, ((0, 6), (0, 128 - share)))[None]
    smoothed_gate = jax.nn.sigmoid(
        (pair_gate_scores + gate_random_jitter) / softening_scale[:, None, None]
    )
    mask_low = smoothed_gate.astype(bf16).reshape(2, half_heads, mask_rows, lanes, 128)
    mask_low = mask_low.transpose(0, 1, 3, 2, 4).reshape(2, -1, 128)
    packed = jnp.concatenate([packed, jnp.concatenate([lines, lines], axis=0), mask_low], axis=1)
    kept = lax.dynamic_index_in_dim(packed, seq_index, 0, keepdims=False)
    sent = lax.dynamic_index_in_dim(packed, 1 - seq_index, 0, keepdims=False)
    packed = seq_ordered(kept, swap_seq(sent))
    other_inputs = swap_seq(inputs)
    hidden_blocks = inner_share // share
    hidden = expand_matrix.reshape(share, 2 * dp_size, hidden_blocks, share)
    contract_blocks = contract_matrix.reshape(hidden_blocks, share, width)
    columns = jnp.stack(
        [
            mixing_result_shift,
            post_mixing_scaling,
            post_mixing_offset,
            contract_shift,
            post_perceptron_scaling,
            post_perceptron_offset,
        ]
        + [expand_shift[k * share : (k + 1) * share] for k in range(hidden_blocks)],
        axis=1,
    )
    wide_share = jnp.concatenate(
        [mixing_result_matrix, hidden.transpose(0, 2, 1, 3).reshape(share, inner)]
        + [contract_blocks[k] for k in range(hidden_blocks)]
        + [jnp.pad(columns, ((0, 0), (0, 128 - columns.shape[1])))],
        axis=1,
    )
    wide_share = seq_ordered(wide_share, swap_seq(wide_share))
    wide_share, unused = lax.optimization_barrier((wide_share, packed))
    gathered = lax.all_gather(packed, ("row", "core"), axis=1, tiled=True)
    wide_matrix = lax.all_gather(wide_share, ("row", "core"), axis=1, tiled=True).reshape(width, -1)
    both_inputs = jnp.concatenate([inputs, other_inputs], axis=0)
    start = grid_coordinates[0, 0]
    turned = (jnp.arange(tsize, dtype=jnp.int32) + start) % tsize
    turn = (turned[:, None] == jnp.arange(tsize, dtype=jnp.int32)[None, :]).astype(bf16)
    row = jnp.arange(mask_rows, dtype=jnp.int32)
    table_order = scatter_order()
    table_places = places_of(table_order[::-1], dp_size)
    own_seq = (jnp.arange(2, dtype=jnp.int32) ^ seq_index)[:, None, None]
    input_spots = ((table_places[None, :] * 2 + own_seq[:, :, 0]) * share)[:, :, None] + jnp.arange(share)
    turned_inputs = matmul(
        both_inputs,
        (input_spots.reshape(-1)[:, None] == jnp.arange(width, dtype=jnp.int32)[None, :]).astype(bf16),
    ).astype(bf16)
    table_spots = ((table_places[None, :] * 2 + own_seq[:, :, 0]) * mask_rows)[:, :, None] + row
    table_spots = table_spots.reshape(-1)
    spot_turn = jnp.sum(jnp.where(turn > 0, table_spots[None, :], 0), axis=1)
    turn_back = (jnp.arange(tsize, dtype=jnp.int32)[:, None] == spot_turn[None, :]).astype(bf16)

    gathered, turned_inputs = lax.optimization_barrier((gathered, turned_inputs))
    gathered = gathered.reshape(2, dp_size, -1, 128)
    weight_lines = 3 * pairs * share
    heads_matrix = gathered[:, :, :weight_lines].reshape(2, dp_size, 3 * pairs, share, 128)
    heads_matrix = heads_matrix.transpose(0, 1, 3, 2, 4).reshape(width, 3 * half_width)
    shifts = lax.dynamic_index_in_dim(gathered, seq_index, 0, keepdims=False)
    shifts = shifts[:, weight_lines : weight_lines + 2, :share].astype(f32).transpose(1, 0, 2).reshape(2, pairs, 128)
    own_mask = gathered[:, :, weight_lines + 8 :].reshape(2 * dp_size, half_heads, lanes, mask_rows, 128)
    own_mask = own_mask.transpose(1, 0, 3, 2, 4).reshape(half_heads, tsize, tsize)

    segments = word_segment_ids[0]
    values_range = jnp.arange(8, dtype=jnp.int32)[:, None]
    segment_ends = jnp.sum((segments[None, :] <= values_range).astype(jnp.int32), axis=1)
    row_end = jnp.sum(jnp.where(segments[None, :] == values_range, segment_ends[:, None], 0), axis=0)
    counts = (row_end.reshape(-1, TILE)[:, -1] + (TILE - 1)) // TILE
    tables = jnp.einsum("hab,cb->hca", own_mask, turn, preferred_element_type=f32).astype(bf16)
    tables = jnp.einsum("hca,da->hcd", tables, turn, preferred_element_type=f32) * (4.0 * LOG2E)

    heads_shift = jnp.stack([shifts[0], jnp.zeros_like(shifts[0]), shifts[1]], axis=1)
    heads_rows = (matmul(both_inputs, heads_matrix) + heads_shift.reshape(-1)).astype(bf16)
    seq_scalar = seq_index[None].astype(jnp.int32)
    items = work_items(counts, CHUNK // TILE)
    scalars = (seq_scalar, counts, items)
    back_scalars = (seq_scalar, work_items(counts, BACK // TILE))
    row_end = row_end[None]
    own_attended, wide_attended, logsum = attend(heads_rows, tables, row_end, scalars, score_scale)
    their_attended = swap_seq(own_attended[rows:])

    their_columns = swap_seq(heads_matrix[:, (pairs - 1) * 384 :])

    (layer_out, grad_summed, grad_attended, attended, first_low, active_low, grad_inner_low, grad_outer_low,
     grad_proj_low, vector_sums) = layer(
        seq_scalar,
        own_attended,
        their_attended,
        inputs,
        upstream_derivative[0],
        wide_matrix,
    )
    low, high = grad_attended[:, :half_width], grad_attended[:, half_width:]
    arrived = swap_seq(jnp.where(first_seq, high, low))
    grads_all = jnp.concatenate([jnp.where(first_seq, low, high), arrived], axis=0)
    table_places_here = places_of(table_order[::-1], dp_size)
    wide_grad, outer_mine, outer_theirs = layer_weights(
        seq_scalar, table_places_here, vector_sums, attended, first_low, active_low,
        grad_proj_low, grad_outer_low, grad_inner_low,
    )
    wide_grad, grads_all, outer_mine, outer_theirs = lax.optimization_barrier(
        (wide_grad, grads_all, outer_mine, outer_theirs)
    )
    wide_half = lax.psum_scatter(wide_grad, ("row", "core"), scatter_dimension=0, tiled=True)
    wide_half = wide_half.reshape(share, 2, -1)
    outer_arrived = swap_seq(outer_theirs)

    split = pairs - 1
    back = lambda first, count, grads: attend_back(
        first, count, 2 * dp_size, heads_rows, grads, wide_attended, tables, row_end, logsum,
        turned_inputs, turn_back, turn, back_scalars, score_scale,
    )
    heads_columns = lambda first, last: heads_matrix[:, first * 384 : last * 384]
    early_heads, early_parts = back(0, split, grads_all)
    flat = lambda parts: parts.reshape(dp_size, -1, 128)
    early_heads, early_parts, outer_arrived = lax.optimization_barrier((early_heads, early_parts, outer_arrived))
    outer_parts = scatter_end(outer_mine, outer_arrived)
    parts = scatter_end(*scatter_start([flat(early_parts), flat(outer_parts)], *table_order[0]))
    early_sent = times_transpose(early_heads[rows:], heads_columns(0, split)).astype(bf16)
    grads_all, parts, early_sent = lax.optimization_barrier((grads_all, parts, early_sent))
    early_theirs = swap_seq(early_sent)
    parts, parts_flip = scatter_start([parts], *table_order[1])
    late_heads, late_parts = back(split, 1, grads_all)
    late_heads, late_parts, parts_flip, early_theirs, wide_half = lax.optimization_barrier(
        (late_heads, late_parts, parts_flip, early_theirs, wide_half)
    )
    late_theirs = swap_seq(late_heads[rows:])
    late_parts = flat(late_parts)
    parts = scatter_end(parts, parts_flip)
    for step in table_order:
        late_parts = scatter_end(*scatter_start([late_parts], *step))
    for step in table_order[2:]:
        parts = scatter_end(*scatter_start([parts], *step))
    lines = late_parts.shape[1] // 2
    outer_parts = parts[0, 2 * split * lines :]
    all_parts = jnp.concatenate(
        [parts[0, : 2 * split * lines].reshape(split, 2, lines, 128), late_parts[0].reshape(1, 2, lines, 128)], axis=0
    )
    own_sums, their_sums = all_parts[:, 0], swap_seq(all_parts[:, 1])
    input_grad = (
        grad_summed
        + times_transpose(early_heads[:rows], heads_columns(0, split))
        + times_transpose(late_heads[:rows], heads_columns(split, pairs))
        + early_theirs.astype(f32)
        + times_transpose(late_theirs, their_columns)
    )

    both_sums = jnp.stack(
        [jnp.where(first_seq, own_sums, their_sums), jnp.where(first_seq, their_sums, own_sums)]
    ).astype(f32)
    table_lines = 2 * mask_rows * lanes
    table_grad = both_sums[:, :, :table_lines].reshape(2, pairs, 2, lanes, mask_rows, 128)
    table_grad = table_grad.transpose(0, 1, 2, 4, 3, 5).reshape(heads, mask_rows, tsize)
    mask_logits_gradient = (
        4.0 * table_grad * smoothed_gate * (1.0 - smoothed_gate) / softening_scale[:, None, None]
    )
    heads_lines = both_sums[:, :, table_lines:].reshape(2, pairs, 3, LINES, 128)
    heads_grad = heads_lines[:, :, :, :share].transpose(2, 3, 0, 1, 4).reshape(3, share, width)
    head_bias = own_sums[:, table_lines:].reshape(pairs, 3, LINES, 128)[:, :, share].astype(f32)

    own_half = lax.dynamic_index_in_dim(wide_half, seq_index, 1, keepdims=False)
    their_half = lax.dynamic_index_in_dim(wide_half, 1 - seq_index, 1, keepdims=False)
    wide_sum = own_half.astype(f32) + swap_seq(their_half).astype(f32)

    vector_columns = wide_sum[:, width + inner :]
    piece = lambda index: vector_columns[:, index]

    def bias_piece(index):
        return lax.dynamic_slice_in_dim(head_bias[:, index].reshape(half_width), dp_index * share, share)

    inner_sum = wide_sum[:, width : width + inner].reshape(share, hidden_blocks, 2 * dp_size, share)
    inner_sum = inner_sum.transpose(0, 2, 1, 3).reshape(share, inner)
    outer_sum = outer_parts.reshape(width // 128, inner_share, 128).transpose(1, 0, 2).reshape(inner_share, width)
    outer_sum = outer_sum.astype(f32)
    inner_piece = vector_columns[:, 6 : 6 + hidden_blocks].T.reshape(inner_share)
    return (
        layer_out[None],
        input_grad[None],
        heads_grad[0],
        bias_piece(0),
        heads_grad[1],
        heads_grad[2],
        bias_piece(2),
        wide_sum[:, :width],
        piece(0),
        piece(1),
        piece(2),
        inner_sum,
        inner_piece,
        outer_sum,
        piece(3),
        piece(4),
        piece(5),
        mask_logits_gradient,
    )


def solution(mesh):
    split = jax.sharding.Mesh(
        mesh.devices.reshape(2, -1, 2), ("seq", "row", "core")
    )
    return jax.shard_map(
        body,
        mesh=split,
        in_specs=(
            P(("row", "core"), "seq", None),
            P(("row", "core"), "seq", None),
            P(("row", "core"), None),
            P(("row", "core"), None),
            P(("seq", "row", "core"), None),
            P(("seq", "row", "core")),
            P(("seq", "row", "core"), None),
            P(("seq", "row", "core"), None),
            P(("seq", "row", "core")),
            P(("seq", "row", "core"), None),
            P(("seq", "row", "core")),
            P(("seq", "row", "core")),
            P(("seq", "row", "core")),
            P(("seq", "row", "core"), None),
            P(("seq", "row", "core")),
            P(("seq", "row", "core"), None),
            P(("seq", "row", "core")),
            P(("seq", "row", "core")),
            P(("seq", "row", "core")),
            P(None, ("seq", "row", "core"), None),
            P(None, ("seq", "row", "core"), None),
            P(),
        ),
        out_specs=(
            P(("row", "core"), "seq", None),
            P(("row", "core"), "seq", None),
            P(("seq", "row", "core"), None),
            P(("seq", "row", "core")),
            P(("seq", "row", "core"), None),
            P(("seq", "row", "core"), None),
            P(("seq", "row", "core")),
            P(("seq", "row", "core"), None),
            P(("seq", "row", "core")),
            P(("seq", "row", "core")),
            P(("seq", "row", "core")),
            P(("seq", "row", "core"), None),
            P(("seq", "row", "core")),
            P(("seq", "row", "core"), None),
            P(("seq", "row", "core")),
            P(("seq", "row", "core")),
            P(("seq", "row", "core")),
            P(None, ("seq", "row", "core"), None),
        ),
        check_vma=False,
    )
```

```python
import functools
import math

import jax
import jax.numpy as jnp
from jax import lax
from jax.experimental import pallas as pl
from jax.experimental.pallas import tpu as pltpu
from jax.sharding import PartitionSpec as P

EPSILON = 1e-06
LOG2E = math.log2(math.e)
MASKED = -1e30
TILE = 256
NT = (((1,), (1,)), ((), ()))
NN = (((1,), (0,)), ((), ()))
TN = (((0,), (0,)), ((), ()))


def dot(a, b, dims=NN):
    return lax.dot_general(a, b, dims, preferred_element_type=jnp.float32)


def local_row(block, seq_index, half_blocks):
    return ((block // half_blocks) ^ seq_index) * (half_blocks * TILE) + (block % half_blocks) * TILE


def split_pair(rows):
    lane = lax.broadcasted_iota(jnp.int32, rows.shape, 1)
    zero = jnp.zeros_like(rows)
    return jnp.where(lane < 64, rows, zero), jnp.where(lane < 64, zero, rows)


CHUNK = 256
UNROLL = 8
BACK = 256
BACK_UNROLL = 4
LINES = 32


def chunk_row(block, seq_index, half_blocks):
    return pl.multiple_of(local_row(block, seq_index, half_blocks), TILE)


def attend_kernel(half_blocks, scale, s_ref, nk_ref, items_ref, qkv_ref, tab_ref, end_ref, att_ref, o32_ref, lse_ref, vt_ref, st_ref, acc_ref, even_ref, odd_ref):
    seq_index = s_ref[0]
    table_size = tab_ref.shape[1]
    per = CHUNK // TILE
    rows = qkv_ref.shape[0]
    pick = split_pair(jnp.ones((128, 128), jnp.bfloat16))
    reach = jnp.zeros((1, 1), jnp.float32)
    for half in pick:
        longest = []
        for at in (0, 128):
            part = qkv_ref[:, at : at + 128].astype(jnp.float32)
            squares = dot((part * part).astype(jnp.bfloat16), half, NT)
            longest.append(jnp.max(squares, keepdims=True))
        reach = jnp.maximum(reach, jnp.sqrt(longest[0]) * jnp.sqrt(longest[1]) * scale)
    small = reach[0, 0] < 80.0
    vt = qkv_ref[:, 256:384].astype(jnp.float32).T
    sub = lax.broadcasted_iota(jnp.int32, vt.shape, 0)
    vt_ref[0, 0:128] = jnp.where(sub < 64, vt, 0.0).astype(jnp.bfloat16)
    vt_ref[1, 0:128] = jnp.where(sub < 64, 0.0, vt).astype(jnp.bfloat16)
    sub = lax.broadcasted_iota(jnp.int32, (16, vt.shape[1]), 0)
    vt_ref[0, 128:144] = jnp.where(sub < 8, 1.0, 0.0).astype(jnp.bfloat16)
    vt_ref[1, 128:144] = jnp.where(sub < 8, 0.0, 1.0).astype(jnp.bfloat16)
    sub = lax.broadcasted_iota(jnp.int32, (CHUNK, TILE), 0)

    def products(block, j):
        queries = split_pair(qkv_ref[pl.ds(chunk_row(block, seq_index, half_blocks), TILE), 0:128])
        keys = qkv_ref[pl.ds(chunk_row((j * per) % (2 * half_blocks), seq_index, half_blocks), CHUNK), 128:256]
        return [dot(keys, queries[h], NT) for h in range(2)]

    def logits(block, j, raw):
        row_end = end_ref[0:1, pl.ds(pl.multiple_of(block * TILE, TILE), TILE)]
        lane0 = pl.multiple_of((block * TILE) % table_size, TILE)
        trow = pl.multiple_of((j * CHUNK) % table_size, CHUNK)
        allowed = sub < row_end - j * CHUNK
        return [
            jnp.where(allowed, raw[h] * scale + tab_ref[h, pl.ds(trow, CHUNK), pl.ds(lane0, TILE)], MASKED)
            for h in range(2)
        ]

    def accumulate(block, j, probs):
        there = chunk_row((j * per) % (2 * half_blocks), seq_index, half_blocks)
        values = jnp.concatenate([vt_ref[h, :, pl.ds(there, CHUNK)] for h in range(2)], axis=1)
        acc_ref[block] += dot(values, jnp.concatenate([p.astype(jnp.bfloat16) for p in probs], axis=0))

    def finish(block, peak):
        here = chunk_row(block, seq_index, half_blocks)
        at = pl.multiple_of(block * TILE, TILE)
        acc = acc_ref[block]
        sums = [acc[128:129], acc[136:137]]
        out = jnp.concatenate([acc[0:64] / sums[0], acc[64:128] / sums[1]], axis=0).T
        o32_ref[pl.ds(here, TILE), :] = out
        att_ref[pl.ds(here, TILE), :] = out.astype(jnp.bfloat16)
        for h in range(2):
            lse_ref[0, h : h + 1, pl.ds(at, TILE)] = peak[h] + jnp.log2(sums[h])

    acc_ref[...] = jnp.zeros_like(acc_ref)

    @pl.when(small)
    def _():
        last = nk_ref.shape[0] - 1
        buffers = (even_ref, odd_ref)

        def prepare(t, to_ref):
            for h, raw in enumerate(products(jnp.minimum(items_ref[0, t], last), items_ref[1, t])):
                to_ref[h] = raw

        def use(t, from_ref):
            block, j = jnp.minimum(items_ref[0, t], last), items_ref[1, t]
            accumulate(block, j, [jnp.exp2(x) for x in logits(block, j, [from_ref[h] for h in range(2)])])

        prepare(0, even_ref)

        def step(i, carry):
            for u in range(0, UNROLL, 2):
                t = UNROLL * i + u
                prepare(t + 1, odd_ref)
                use(t, even_ref)
                prepare(t + 2, even_ref)
                use(t + 1, odd_ref)
            return carry

        lax.fori_loop(0, (items_ref[2, 0] + UNROLL - 1) // UNROLL, step, 0)

        def close(block, carry):
            finish(block, [0.0, 0.0])
            return carry

        lax.fori_loop(0, last + 1, close, 0)

    @pl.when(jnp.logical_not(small))
    def _():
        def query_block(block, carry):
            count = (nk_ref[block] + per - 1) // per

            def score(j, peaks):
                out = []
                for h, x in enumerate(logits(block, j, products(block, j))):
                    st_ref[h, pl.ds(pl.multiple_of(j * CHUNK, CHUNK), CHUNK), :] = x
                    out.append(jnp.maximum(peaks[h], jnp.max(x.reshape(CHUNK // 8, 8, TILE), axis=0)))
                return tuple(out)

            start = jnp.full((8, TILE), MASKED, jnp.float32)
            peaks = lax.fori_loop(0, count, score, (start, start))
            peak = [jnp.max(p, axis=0, keepdims=True) for p in peaks]

            def mix(j, carry):
                at_chunk = pl.ds(pl.multiple_of(j * CHUNK, CHUNK), CHUNK)
                accumulate(block, j, [jnp.exp2(st_ref[h, at_chunk, :] - peak[h]) for h in range(2)])
                return carry

            lax.fori_loop(0, count, mix, 0)
            finish(block, peak)
            return carry

        lax.fori_loop(0, nk_ref.shape[0], query_block, 0)


def work_items(counts, per):
    chunks = (counts + (per - 1)) // per
    ends = jnp.sum(jnp.where(jnp.arange(len(counts))[:, None] >= jnp.arange(len(counts))[None, :], chunks[None, :], 0), axis=1)
    step = jnp.arange(len(counts) * len(counts) // per + 16, dtype=jnp.int32)
    block = jnp.sum((step[:, None] >= ends[None, :]).astype(jnp.int32), axis=1)
    first = jnp.sum(jnp.where(jnp.arange(len(counts))[None, :] < block[:, None], chunks[None, :], 0), axis=1)
    inside = block < len(counts)
    chunk = jnp.where(inside, step - first, len(counts) // per)
    return jnp.stack([jnp.where(inside, block, len(counts)), chunk, jnp.full_like(step, ends[-1])]).astype(jnp.int32)


def attend(qkv, tables, row_end, scalars, score_scale):
    rows = qkv.shape[0]
    pairs = qkv.shape[1] // 384
    tsize = tables.shape[1]
    spec = pltpu.PrefetchScalarGridSpec(
        num_scalar_prefetch=len(scalars),
        grid=(pairs,),
        in_specs=[
            pl.BlockSpec((rows, 384), lambda p, *_: (0, p)),
            pl.BlockSpec((2, tsize, tsize), lambda p, *_: (p, 0, 0)),
            pl.BlockSpec((1, rows), lambda p, *_: (0, 0)),
        ],
        out_specs=[
            pl.BlockSpec((rows, 128), lambda p, *_: (0, p)),
            pl.BlockSpec((rows, 128), lambda p, *_: (0, p)),
            pl.BlockSpec((1, 8, rows), lambda p, *_: (p, 0, 0)),
        ],
        scratch_shapes=[
            pltpu.VMEM((2, 144, rows), jnp.bfloat16),
            pltpu.VMEM((2, rows, TILE), jnp.float32),
            pltpu.VMEM((rows // TILE, 144, TILE), jnp.float32),
            pltpu.VMEM((2, CHUNK, TILE), jnp.float32),
            pltpu.VMEM((2, CHUNK, TILE), jnp.float32),
        ],
    )
    return pl.pallas_call(
        functools.partial(attend_kernel, rows // TILE // 2, score_scale * LOG2E),
        grid_spec=spec,
        out_shape=[
            jax.ShapeDtypeStruct((rows, pairs * 128), jnp.bfloat16),
            jax.ShapeDtypeStruct((rows, pairs * 128), jnp.float32),
            jax.ShapeDtypeStruct((pairs, 8, rows), jnp.float32),
        ],
        compiler_params=pltpu.CompilerParams(dimension_semantics=("arbitrary",), vmem_limit_bytes=40 << 20),
        cost_estimate=pl.CostEstimate(flops=40 * rows * rows * 128, transcendentals=2 * rows * rows, bytes_accessed=8 << 20),
        name="attend",
    )(*scalars, qkv, tables, row_end)


def attend_back_kernel(half_blocks, scale, score_scale, s_ref, items_ref, qkv_ref, grad_ref, o32_ref, tab_ref, end_ref, lse_ref,
                       turned_ref, back_ref, turn_ref, dqkv_ref, parts_ref, gtab_ref, kt_ref, dk_ref, dv_ref,
                       dq_ref, delta_ref, even_ref, odd_ref):
    seq_index = s_ref[0]
    table_size = tab_ref.shape[1]
    per = BACK // TILE
    blocks = 2 * half_blocks
    kt = qkv_ref[:, 128:256].astype(jnp.float32).T
    sub = lax.broadcasted_iota(jnp.int32, kt.shape, 0)
    kt_ref[0] = jnp.where(sub < 64, kt, 0.0).astype(jnp.bfloat16)
    kt_ref[1] = jnp.where(sub < 64, 0.0, kt).astype(jnp.bfloat16)
    dk_ref[...] = jnp.zeros_like(dk_ref)
    dv_ref[...] = jnp.zeros_like(dv_ref)
    dq_ref[...] = jnp.zeros_like(dq_ref)
    gtab_ref[...] = jnp.zeros_like(gtab_ref)
    inner = (grad_ref[...].astype(jnp.float32) * o32_ref[...]).T
    delta_ref[0:1, :] = jnp.sum(inner[0:64], axis=0, keepdims=True)
    delta_ref[1:2, :] = jnp.sum(inner[64:128], axis=0, keepdims=True)
    sub = lax.broadcasted_iota(jnp.int32, (BACK, TILE), 0)

    def item(t):
        block, j = jnp.minimum(items_ref[0, t], blocks - 1), items_ref[1, t]
        here = pl.ds(chunk_row(block, seq_index, half_blocks), TILE)
        there = pl.ds(chunk_row((j * per) % blocks, seq_index, half_blocks), BACK)
        return block, j, here, there

    def prepare(t, to_ref):
        block, j, here, there = item(t)
        queries, grads = split_pair(qkv_ref[here, 0:128]), split_pair(grad_ref[here, :])
        keys, values = qkv_ref[there, 128:256], qkv_ref[there, 256:384]
        for h in range(2):
            to_ref[h] = dot(keys, queries[h], NT)
            to_ref[2 + h] = dot(values, grads[h], NT)

    def use(t, from_ref):
        block, j, here, there = item(t)
        at = pl.ds(pl.multiple_of(block * TILE, TILE), TILE)
        lane0 = pl.ds(pl.multiple_of((block * TILE) % table_size, TILE), TILE)
        trow = pl.ds(pl.multiple_of((j * BACK) % table_size, BACK), BACK)
        allowed = sub < end_ref[0:1, at] - j * BACK
        probs, scores = [], []
        for h in range(2):
            x = from_ref[h] * scale + tab_ref[h, trow, lane0] - lse_ref[0, h : h + 1, at]
            p = jnp.exp2(jnp.where(allowed, x, MASKED))
            d = p * (from_ref[2 + h] - delta_ref[h : h + 1, here])
            gtab_ref[h, trow, lane0] += d
            probs.append(p.astype(jnp.bfloat16))
            scores.append(d.astype(jnp.bfloat16))
        queries, grads = split_pair(qkv_ref[here, 0:128]), split_pair(grad_ref[here, :])
        dv_ref[there, :] += dot(jnp.concatenate(probs, axis=1), jnp.concatenate(grads, axis=0))
        dk_ref[there, :] += dot(jnp.concatenate(scores, axis=1), jnp.concatenate(queries, axis=0))
        kt = jnp.concatenate([kt_ref[h, :, there] for h in range(2)], axis=1)
        dq_ref[block] += dot(kt, jnp.concatenate(scores, axis=0))

    prepare(0, even_ref)

    def step(i, carry):
        for u in range(0, BACK_UNROLL, 2):
            t = BACK_UNROLL * i + u
            prepare(t + 1, odd_ref)
            use(t, even_ref)
            prepare(t + 2, even_ref)
            use(t + 1, odd_ref)
        return carry

    lax.fori_loop(0, (items_ref[2, 0] + BACK_UNROLL - 1) // BACK_UNROLL, step, 0)

    def close(block, carry):
        here = pl.ds(chunk_row(block, seq_index, half_blocks), TILE)
        dqkv_ref[here, 0:128] = (dq_ref[block] * score_scale).T.astype(jnp.bfloat16)
        return carry

    lax.fori_loop(0, blocks, close, 0)
    dqkv_ref[:, 128:256] = (dk_ref[...] * score_scale).astype(jnp.bfloat16)
    dqkv_ref[:, 256:384] = dv_ref[...].astype(jnp.bfloat16)
    owners, lines = 2 * parts_ref.shape[0], parts_ref.shape[3]
    mask_rows = table_size // owners
    share = turned_ref.shape[1] // owners
    table_lines = lines - 3 * LINES
    for h in range(2):
        table = dot(back_ref[...], gtab_ref[h].astype(jnp.bfloat16), NT).astype(jnp.bfloat16)
        table = dot(table, turn_ref[...])
        for i in range(table_size // 128):
            at = (h * (table_size // 128) + i) * mask_rows
            part = table[:, i * 128 : (i + 1) * 128].reshape(owners // 2, 2, mask_rows, 128)
            parts_ref[:, 0, :, at : at + mask_rows, :] = part.astype(jnp.bfloat16)
    bias = jnp.sum(dqkv_ref[...].astype(jnp.float32), axis=0, keepdims=True)
    step = 384 // share
    for i in range(owners // step):
        part = dot(turned_ref[:, i * 384 : (i + 1) * 384], dqkv_ref[...], TN)
        for c in range(3):
            lanes = slice(c * 128, (c + 1) * 128)
            sums = jnp.broadcast_to(bias[:, lanes], (step * (LINES - share), 128))
            block = jnp.concatenate(
                [part[:, lanes].reshape(step, share, 128), sums.reshape(step, LINES - share, 128)], axis=1
            )
            at = table_lines + c * LINES
            block = block.reshape(step // 2, 2, LINES, 128)
            parts_ref[i * step // 2 : (i + 1) * step // 2, 0, :, at : at + LINES, :] = block.astype(jnp.bfloat16)


def attend_back(first, pairs, owners, qkv, grads, o32, tables, row_end, lse, turned, back, turn, scalars, score_scale):
    rows = qkv.shape[0]
    tsize = tables.shape[1]
    width = turned.shape[1]
    lines = 2 * (tsize // owners) * (tsize // 128) + 3 * LINES
    spec = pltpu.PrefetchScalarGridSpec(
        num_scalar_prefetch=len(scalars),
        grid=(pairs,),
        in_specs=[
            pl.BlockSpec((rows, 384), lambda p, *_: (0, first + p)),
            pl.BlockSpec((rows, 128), lambda p, *_: (0, first + p)),
            pl.BlockSpec((rows, 128), lambda p, *_: (0, first + p)),
            pl.BlockSpec((2, tsize, tsize), lambda p, *_: (first + p, 0, 0)),
            pl.BlockSpec((1, rows), lambda p, *_: (0, 0)),
            pl.BlockSpec((1, 8, rows), lambda p, *_: (first + p, 0, 0)),
            pl.BlockSpec((rows, width), lambda p, *_: (0, 0), pipeline_mode=pl.Buffered(1)),
            pl.BlockSpec((tsize, tsize), lambda p, *_: (0, 0), pipeline_mode=pl.Buffered(1)),
            pl.BlockSpec((tsize, tsize), lambda p, *_: (0, 0), pipeline_mode=pl.Buffered(1)),
        ],
        out_specs=[
            pl.BlockSpec((rows, 384), lambda p, *_: (0, p)),
            pl.BlockSpec((owners // 2, 1, 2, lines, 128), lambda p, *_: (0, p, 0, 0, 0)),
        ],
        scratch_shapes=[
            pltpu.VMEM((2, tsize, tsize), jnp.float32),
            pltpu.VMEM((2, 128, rows), jnp.bfloat16),
            pltpu.VMEM((rows, 128), jnp.float32),
            pltpu.VMEM((rows, 128), jnp.float32),
            pltpu.VMEM((rows // TILE, 128, TILE), jnp.float32),
            pltpu.VMEM((8, rows), jnp.float32),
            pltpu.VMEM((4, BACK, TILE), jnp.float32),
            pltpu.VMEM((4, BACK, TILE), jnp.float32),
        ],
    )
    return pl.pallas_call(
        functools.partial(attend_back_kernel, rows // TILE // 2, score_scale * LOG2E, score_scale),
        grid_spec=spec,
        out_shape=[
            jax.ShapeDtypeStruct((rows, pairs * 384), jnp.bfloat16),
            jax.ShapeDtypeStruct((owners // 2, pairs, 2, lines, 128), jnp.bfloat16),
        ],
        compiler_params=pltpu.CompilerParams(dimension_semantics=("arbitrary",), vmem_limit_bytes=56 << 20),
        cost_estimate=pl.CostEstimate(
            flops=pairs * rows * rows, transcendentals=rows * rows // 64, bytes_accessed=1 << 20
        ),
        name="attend_back",
    )(*scalars, qkv, grads, o32, tables, row_end, lse, turned, back, turn)


GELU_A = math.sqrt(2.0 / math.pi)
GELU_B = 0.044715


def row_stats(values):
    center = values - jnp.mean(values, axis=-1, keepdims=True)
    rstdev = lax.rsqrt(jnp.mean(center * center, axis=-1, keepdims=True) + EPSILON)
    return center * rstdev, rstdev


def row_back(gradient, normed, rstdev, gain):
    scaled = gradient * gain
    return rstdev * (
        scaled
        - jnp.mean(scaled, axis=-1, keepdims=True)
        - normed * jnp.mean(scaled * normed, axis=-1, keepdims=True)
    )


def layer_kernel(s_ref, *refs):
    f32, bf16 = jnp.float32, jnp.bfloat16
    (own_ref, their_ref, x_ref, up_ref, wide_ref,
     out_ref, gsum_ref, gatt_ref, att_ref, first_ref, active_ref, ginner_ref, gouter_ref, gproj_ref,
     vsum_ref, slope_ref, acc_ref, n1_ref, f1_ref, vec_ref) = refs
    width = x_ref.shape[1]
    inner = active_ref.shape[1]
    step = width
    vec = lambda i: vec_ref[i : i + 1, :]
    total = lambda value: jnp.sum(value, axis=0, keepdims=True)

    def outer_rows(c):
        return wide_ref[:, pl.ds(pl.multiple_of(width + inner + c * step, 128), width)]

    @pl.when(pl.program_id(0) == 0)
    def _():
        vsum_ref[...] = jnp.zeros_like(vsum_ref)
        vec_ref[...] = wide_ref[:, width + 2 * inner :].astype(f32).T

    first_seq = s_ref[0] == 0
    mine, others = own_ref[...], their_ref[...]

    @pl.when(first_seq)
    def _():
        att_ref[:, : width // 2] = mine
        att_ref[:, width // 2 :] = others

    @pl.when(jnp.logical_not(first_seq))
    def _():
        att_ref[:, : width // 2] = others
        att_ref[:, width // 2 :] = mine

    summed = x_ref[...].astype(f32) + (dot(att_ref[...], wide_ref[:, :width]) + vec(0))
    normed, rstdev1 = row_stats(summed)
    n1_ref[...] = normed
    first = normed * vec(1) + vec(2)
    f1_ref[...] = first
    first_ref[...] = first.astype(bf16)
    acc_ref[...] = jnp.zeros_like(acc_ref)

    def up(c, carry):
        at = pl.ds(pl.multiple_of(c * step, 128), step)
        w_at = pl.ds(pl.multiple_of(width + c * step, 128), step)
        u = dot(first_ref[...], wide_ref[:, w_at]) + vec_ref[pl.ds(6 + c, 1), :]
        square = u * u
        t = jnp.tanh(GELU_A * (u + GELU_B * (square * u)))
        half = 0.5 * (1.0 + t)
        slope_ref[:, at] = half + 0.5 * u * (1.0 - t * t) * (GELU_A * (1.0 + 3.0 * GELU_B * square))
        active = (u * half).astype(bf16)
        active_ref[:, at] = active
        acc_ref[...] += dot(active, outer_rows(c))
        return carry

    lax.fori_loop(0, inner // step, up, 0)
    normed, rstdev = row_stats(f1_ref[...] + (acc_ref[...] + vec(3)))
    out_ref[...] = (normed * vec(4) + vec(5)).astype(bf16)
    gradient = up_ref[...].astype(f32)
    vsum_ref[4:5, :] += total(gradient * normed)
    vsum_ref[5:6, :] += total(gradient)
    grad_sum = row_back(gradient, normed, rstdev, vec(4))
    grad_low = grad_sum.astype(bf16)
    gouter_ref[...] = grad_low
    vsum_ref[3:4, :] += total(grad_low.astype(f32))
    acc_ref[...] = grad_sum

    def down(c, carry):
        at = pl.ds(pl.multiple_of(c * step, 128), step)
        w_at = pl.ds(pl.multiple_of(width + c * step, 128), step)
        g = (dot(gouter_ref[...], outer_rows(c), NT) * slope_ref[:, at]).astype(bf16)
        ginner_ref[:, at] = g
        vsum_ref[pl.ds(6 + c, 1), :] += total(g.astype(f32))
        acc_ref[...] += dot(g, wide_ref[:, w_at], NT)
        return carry

    lax.fori_loop(0, inner // step, down, 0)
    grad_first = acc_ref[...]
    normed = n1_ref[...]
    vsum_ref[1:2, :] += total(grad_first * normed)
    vsum_ref[2:3, :] += total(grad_first)
    grad_summed = row_back(grad_first, normed, rstdev1, vec(1))
    gsum_ref[...] = grad_summed
    grad_low = grad_summed.astype(bf16)
    gproj_ref[...] = grad_low
    vsum_ref[0:1, :] += total(grad_low.astype(f32))
    gatt_ref[...] = dot(grad_low, wide_ref[:, :width], NT).astype(bf16)


def layer(seq_index, own, their, x, upstream, wide):
    rows, width = x.shape
    inner = (wide.shape[1] - width - 128) // 2
    block = 512
    by_rows = lambda size: pl.BlockSpec((block, size), lambda i, *_: (i, 0))
    whole = lambda shape: pl.BlockSpec(shape, lambda i, *_: (0,) * len(shape), pipeline_mode=pl.Buffered(1))
    once = lambda shape: pl.BlockSpec(shape, lambda i, *_: (0, 0))
    spec = pltpu.PrefetchScalarGridSpec(
        num_scalar_prefetch=1,
        grid=(rows // block,),
        in_specs=[by_rows(width // 2)] * 2
        + [by_rows(width), by_rows(width), whole(wide.shape)],
        out_specs=[by_rows(width)] * 5
        + [by_rows(inner)] * 2
        + [by_rows(width)] * 2
        + [once((16, width))],
        scratch_shapes=[pltpu.VMEM((block, inner), jnp.float32)] + [pltpu.VMEM((block, width), jnp.float32)] * 3
        + [pltpu.VMEM((128, width), jnp.float32)],
    )
    shape = lambda size, dtype: jax.ShapeDtypeStruct((rows, size), dtype)
    low = jnp.bfloat16
    return pl.pallas_call(
        layer_kernel,
        grid_spec=spec,
        out_shape=[shape(width, low), shape(width, jnp.float32), shape(width, low), shape(width, low), shape(width, low)]
        + [shape(inner, low)] * 2
        + [shape(width, low)] * 2
        + [jax.ShapeDtypeStruct((16, width), jnp.float32)],
        compiler_params=pltpu.CompilerParams(dimension_semantics=("arbitrary",), vmem_limit_bytes=56 << 20),
        cost_estimate=pl.CostEstimate(
            flops=8 * rows * width * (width // 2 + inner), transcendentals=rows * inner, bytes_accessed=36 << 20
        ),
        name="layer",
    )(seq_index, own, their, x, upstream, wide)


def weights_kernel(s_ref, place_ref, vsum_ref, att_ref, first_ref, active_ref, gproj_ref, gouter_ref, ginner_ref,
                   wide_ref, mine_ref, their_ref):
    bf16 = jnp.bfloat16
    i, c = pl.program_id(0), pl.program_id(1)
    width = gproj_ref.shape[1]
    inner = width * pl.num_programs(1)
    owners, share = mine_ref.shape[0], mine_ref.shape[3]

    @pl.when(c == 0)
    def _():
        wide_ref[:, :width] = dot(att_ref[...], gproj_ref[...], TN).astype(bf16)
        sums = vsum_ref[...]
        sums = jnp.concatenate([sums, jnp.zeros((128 - sums.shape[0], sums.shape[1]), jnp.float32)], axis=0)
        wide_ref[:, width + inner :] = sums.T.astype(bf16)

    at = pl.ds(pl.multiple_of(width * (c + 1), 128), width)
    wide_ref[:, at] = dot(first_ref[...], ginner_ref[...], TN).astype(bf16)
    part = dot(active_ref[...], gouter_ref[...], TN)

    def place(out_ref):
        for k in range(owners):
            rows = part[k * share : (k + 1) * share].astype(bf16)
            for i in range(width // 128):
                out_ref[place_ref[k], i, c] = rows[:, i * 128 : (i + 1) * 128]

    @pl.when(i == s_ref[0])
    def _():
        place(mine_ref)

    @pl.when(i != s_ref[0])
    def _():
        place(their_ref)


def layer_weights(seq_index, places, sums, attended, first, active, gproj, gouter, ginner):
    rows, width = gproj.shape
    inner = ginner.shape[1]
    half = width // 2
    steps = inner // width
    owners = places.shape[0]
    blocks = (owners, width // 128, steps, half // owners, 128)
    spec = pltpu.PrefetchScalarGridSpec(
        num_scalar_prefetch=2,
        grid=(2, steps),
        in_specs=[
            pl.BlockSpec((sums.shape[0], half), lambda i, c, *_: (0, i)),
            pl.BlockSpec((rows, half), lambda i, c, *_: (0, i)),
            pl.BlockSpec((rows, half), lambda i, c, *_: (0, i)),
            pl.BlockSpec((rows, half), lambda i, c, *_: (0, 2 * c + i)),
            pl.BlockSpec((rows, width), lambda i, c, *_: (0, 0)),
            pl.BlockSpec((rows, width), lambda i, c, *_: (0, 0)),
            pl.BlockSpec((rows, width), lambda i, c, *_: (0, c)),
        ],
        out_specs=[
            pl.BlockSpec((half, width + inner + 128), lambda i, c, *_: (0, i)),
            pl.BlockSpec(blocks, lambda i, c, *_: (0, 0, 0, 0, 0)),
            pl.BlockSpec(blocks, lambda i, c, *_: (0, 0, 0, 0, 0)),
        ],
    )
    return pl.pallas_call(
        weights_kernel,
        grid_spec=spec,
        out_shape=[
            jax.ShapeDtypeStruct((half, 2 * (width + inner + 128)), jnp.bfloat16),
            jax.ShapeDtypeStruct(blocks, jnp.bfloat16),
            jax.ShapeDtypeStruct(blocks, jnp.bfloat16),
        ],
        compiler_params=pltpu.CompilerParams(dimension_semantics=("arbitrary", "arbitrary"), vmem_limit_bytes=56 << 20),
        cost_estimate=pl.CostEstimate(
            flops=4 * rows * width * (width // 2 + inner), transcendentals=0, bytes_accessed=32 << 20
        ),
        name="layer_weights",
    )(seq_index, places, sums, attended, first, active, gproj, gouter, ginner)


def matmul(left_side, right_side):
    return jnp.dot(left_side, right_side, preferred_element_type=jnp.float32)


def contract_rows(left_side, right_side):
    return jnp.einsum("rd,re->de", left_side, right_side, preferred_element_type=jnp.float32)


def times_transpose(left_side, right_side):
    return jnp.einsum("re,de->rd", left_side, right_side, preferred_element_type=jnp.float32)


def norm_forward(values, norm_gain, norm_shift):
    center = values - jnp.mean(values, axis=-1, keepdims=True)
    rstdev = lax.rsqrt(jnp.mean(center * center, axis=-1, keepdims=True) + EPSILON)
    normed = center * rstdev
    return (normed * norm_gain + norm_shift, normed, rstdev)


def norm_backward(gradient, normed, rstdev, norm_gain):
    scaled = gradient * norm_gain
    back = rstdev * (
        scaled
        - jnp.mean(scaled, axis=-1, keepdims=True)
        - normed * jnp.mean(scaled * normed, axis=-1, keepdims=True)
    )
    return (back, jnp.sum(gradient * normed, axis=0), jnp.sum(gradient, axis=0))


def swap_seq(value):
    return lax.ppermute(value, "seq", [(0, 1), (1, 0)])


def flip(value, axis, bit):
    return lax.ppermute(value, axis, [(i, i ^ bit) for i in range(lax.axis_size(axis))])


def row_steps():
    bits = [1 << i for i in range(1, lax.axis_size("row").bit_length() - 1)]
    return [("row", bit) for bit in bits], [("row", 1)]


def scatter_order():
    far, near = row_steps()
    return [("core", 1)] + near + far


def coordinates(owner):
    row_size = lax.axis_size("row")
    return {"seq": owner // (2 * row_size), "row": (owner // 2) % row_size, "core": owner % 2}


def places_of(order, count):
    owner = coordinates(jnp.arange(count, dtype=jnp.int32))
    place = jnp.zeros((count,), jnp.int32)
    for step, (axis, bit) in enumerate(order):
        place = place + ((((owner[axis] ^ lax.axis_index(axis)) // bit) & 1) << step)
    return place


def scatter_start(parts, axis, bit):
    half = parts[0].shape[0] // 2
    kept = [part[:half] for part in parts]
    sent = [part[half:] for part in parts]
    joined = lambda values: values[0] if len(values) == 1 else jnp.concatenate(values, axis=1)
    return joined(kept), flip(joined(sent), axis, bit)


def scatter_end(kept, arrived):
    return (kept.astype(jnp.float32) + arrived.astype(jnp.float32)).astype(jnp.bfloat16)


def body(
    incoming_activations,
    upstream_derivative,
    grid_coordinates,
    word_segment_ids,
    asking_matrix,
    asking_shift,
    lookup_matrix,
    content_matrix,
    content_shift,
    mixing_result_matrix,
    mixing_result_shift,
    post_mixing_scaling,
    post_mixing_offset,
    expand_matrix,
    expand_shift,
    contract_matrix,
    contract_shift,
    post_perceptron_scaling,
    post_perceptron_offset,
    pair_gate_scores,
    gate_random_jitter,
    softening_scale,
):
    f32, bf16 = jnp.float32, jnp.bfloat16
    heads = softening_scale.shape[0]
    width = incoming_activations.shape[2]
    rows = incoming_activations.shape[1]
    inner = expand_matrix.shape[1]
    tsize = pair_gate_scores.shape[2]
    score_scale = 1.0 / math.sqrt(width // heads)
    half_width, half_heads = width // 2, heads // 2
    pairs = half_heads // 2
    seq_index = lax.axis_index("seq")
    dp_size = 2 * lax.axis_size("row")
    dp_index = 2 * lax.axis_index("row") + lax.axis_index("core")
    owner = seq_index * dp_size + dp_index
    first_seq = seq_index == 0
    inputs = incoming_activations[0]
    share = asking_matrix.shape[0]
    inner_share = expand_shift.shape[0]
    mask_rows = tsize // (2 * dp_size)
    lanes = tsize // 128

    def seq_ordered(mine, others):
        return jnp.stack([jnp.where(first_seq, mine, others), jnp.where(first_seq, others, mine)])


    packed = jnp.stack(
        [part.reshape(share, 2, pairs, 128) for part in (asking_matrix, lookup_matrix, content_matrix)], axis=3
    )
    packed = packed.transpose(1, 2, 3, 0, 4).reshape(2, 3 * pairs * share, 128)
    lines = jnp.stack([asking_shift, content_shift])
    lines = jnp.pad(lines, ((0, 6), (0, 128 - share)))[None]
    smoothed_gate = jax.nn.sigmoid(
        (pair_gate_scores + gate_random_jitter) / softening_scale[:, None, None]
    )
    mask_low = smoothed_gate.astype(bf16).reshape(2, half_heads, mask_rows, lanes, 128)
    mask_low = mask_low.transpose(0, 1, 3, 2, 4).reshape(2, -1, 128)
    packed = jnp.concatenate([packed, jnp.concatenate([lines, lines], axis=0), mask_low], axis=1)
    kept = lax.dynamic_index_in_dim(packed, seq_index, 0, keepdims=False)
    sent = lax.dynamic_index_in_dim(packed, 1 - seq_index, 0, keepdims=False)
    packed = seq_ordered(kept, swap_seq(sent))
    other_inputs = swap_seq(inputs)
    hidden_blocks = inner_share // share
    hidden = expand_matrix.reshape(share, 2 * dp_size, hidden_blocks, share)
    contract_blocks = contract_matrix.reshape(hidden_blocks, share, width)
    columns = jnp.stack(
        [
            mixing_result_shift,
            post_mixing_scaling,
            post_mixing_offset,
            contract_shift,
            post_perceptron_scaling,
            post_perceptron_offset,
        ]
        + [expand_shift[k * share : (k + 1) * share] for k in range(hidden_blocks)],
        axis=1,
    )
    wide_share = jnp.concatenate(
        [mixing_result_matrix, hidden.transpose(0, 2, 1, 3).reshape(share, inner)]
        + [contract_blocks[k] for k in range(hidden_blocks)]
        + [jnp.pad(columns, ((0, 0), (0, 128 - columns.shape[1])))],
        axis=1,
    )
    wide_share = seq_ordered(wide_share, swap_seq(wide_share))
    wide_share, unused = lax.optimization_barrier((wide_share, packed))
    gathered = lax.all_gather(packed, ("row", "core"), axis=1, tiled=True)
    wide_matrix = lax.all_gather(wide_share, ("row", "core"), axis=1, tiled=True).reshape(width, -1)
    both_inputs = jnp.concatenate([inputs, other_inputs], axis=0)
    start = grid_coordinates[0, 0]
    turned = (jnp.arange(tsize, dtype=jnp.int32) + start) % tsize
    turn = (turned[:, None] == jnp.arange(tsize, dtype=jnp.int32)[None, :]).astype(bf16)
    row = jnp.arange(mask_rows, dtype=jnp.int32)
    table_order = scatter_order()
    table_places = places_of(table_order[::-1], dp_size)
    own_seq = (jnp.arange(2, dtype=jnp.int32) ^ seq_index)[:, None, None]
    input_spots = ((table_places[None, :] * 2 + own_seq[:, :, 0]) * share)[:, :, None] + jnp.arange(share)
    turned_inputs = matmul(
        both_inputs,
        (input_spots.reshape(-1)[:, None] == jnp.arange(width, dtype=jnp.int32)[None, :]).astype(bf16),
    ).astype(bf16)
    table_spots = ((table_places[None, :] * 2 + own_seq[:, :, 0]) * mask_rows)[:, :, None] + row
    table_spots = table_spots.reshape(-1)
    spot_turn = jnp.sum(jnp.where(turn > 0, table_spots[None, :], 0), axis=1)
    turn_back = (jnp.arange(tsize, dtype=jnp.int32)[:, None] == spot_turn[None, :]).astype(bf16)

    gathered, turned_inputs = lax.optimization_barrier((gathered, turned_inputs))
    gathered = gathered.reshape(2, dp_size, -1, 128)
    weight_lines = 3 * pairs * share
    heads_matrix = gathered[:, :, :weight_lines].reshape(2, dp_size, 3 * pairs, share, 128)
    heads_matrix = heads_matrix.transpose(0, 1, 3, 2, 4).reshape(width, 3 * half_width)
    shifts = lax.dynamic_index_in_dim(gathered, seq_index, 0, keepdims=False)
    shifts = shifts[:, weight_lines : weight_lines + 2, :share].astype(f32).transpose(1, 0, 2).reshape(2, pairs, 128)
    own_mask = gathered[:, :, weight_lines + 8 :].reshape(2 * dp_size, half_heads, lanes, mask_rows, 128)
    own_mask = own_mask.transpose(1, 0, 3, 2, 4).reshape(half_heads, tsize, tsize)

    segments = word_segment_ids[0]
    values_range = jnp.arange(8, dtype=jnp.int32)[:, None]
    segment_ends = jnp.sum((segments[None, :] <= values_range).astype(jnp.int32), axis=1)
    row_end = jnp.sum(jnp.where(segments[None, :] == values_range, segment_ends[:, None], 0), axis=0)
    counts = (row_end.reshape(-1, TILE)[:, -1] + (TILE - 1)) // TILE
    tables = jnp.einsum("hab,cb->hca", own_mask, turn, preferred_element_type=f32).astype(bf16)
    tables = jnp.einsum("hca,da->hcd", tables, turn, preferred_element_type=f32) * (4.0 * LOG2E)

    heads_shift = jnp.stack([shifts[0], jnp.zeros_like(shifts[0]), shifts[1]], axis=1)
    heads_rows = (matmul(both_inputs, heads_matrix) + heads_shift.reshape(-1)).astype(bf16)
    seq_scalar = seq_index[None].astype(jnp.int32)
    items = work_items(counts, CHUNK // TILE)
    scalars = (seq_scalar, counts, items)
    back_scalars = (seq_scalar, work_items(counts, BACK // TILE))
    row_end = row_end[None]
    own_attended, wide_attended, logsum = attend(heads_rows, tables, row_end, scalars, score_scale)
    their_attended = swap_seq(own_attended[rows:])

    their_columns = swap_seq(heads_matrix[:, (pairs - 1) * 384 :])

    (layer_out, grad_summed, grad_attended, attended, first_low, active_low, grad_inner_low, grad_outer_low,
     grad_proj_low, vector_sums) = layer(
        seq_scalar,
        own_attended,
        their_attended,
        inputs,
        upstream_derivative[0],
        wide_matrix,
    )
    grad_attended, their_columns = lax.optimization_barrier((grad_attended, their_columns))
    low, high = grad_attended[:, :half_width], grad_attended[:, half_width:]
    arrived = swap_seq(jnp.where(first_seq, high, low))
    grads_all = jnp.concatenate([jnp.where(first_seq, low, high), arrived], axis=0)
    table_places_here = places_of(table_order[::-1], dp_size)
    wide_grad, outer_mine, outer_theirs = layer_weights(
        seq_scalar, table_places_here, vector_sums, attended, first_low, active_low,
        grad_proj_low, grad_outer_low, grad_inner_low,
    )
    wide_grad, grads_all, outer_mine, outer_theirs = lax.optimization_barrier(
        (wide_grad, grads_all, outer_mine, outer_theirs)
    )
    wide_half = lax.psum_scatter(wide_grad, ("row", "core"), scatter_dimension=0, tiled=True)
    wide_half = wide_half.reshape(share, 2, -1)
    outer_arrived = swap_seq(outer_theirs)

    split = pairs - 1
    back = lambda first, count, grads: attend_back(
        first, count, 2 * dp_size, heads_rows, grads, wide_attended, tables, row_end, logsum,
        turned_inputs, turn_back, turn, back_scalars, score_scale,
    )
    heads_columns = lambda first, last: heads_matrix[:, first * 384 : last * 384]
    early_heads, early_parts = back(0, split, grads_all)
    flat = lambda parts: parts.reshape(dp_size, -1, 128)
    early_heads, early_parts, outer_arrived = lax.optimization_barrier((early_heads, early_parts, outer_arrived))
    outer_parts = scatter_end(outer_mine, outer_arrived)
    parts = scatter_end(*scatter_start([flat(early_parts), flat(outer_parts)], *table_order[0]))
    early_sent = times_transpose(early_heads[rows:], heads_columns(0, split)).astype(bf16)
    grads_all, parts, early_sent = lax.optimization_barrier((grads_all, parts, early_sent))
    early_theirs = swap_seq(early_sent)
    parts, parts_flip = scatter_start([parts], *table_order[1])
    late_heads, late_parts = back(split, 1, grads_all)
    late_heads, late_parts, parts_flip, early_theirs, wide_half, early_heads = lax.optimization_barrier(
        (late_heads, late_parts, parts_flip, early_theirs, wide_half, early_heads)
    )
    late_theirs = swap_seq(late_heads[rows:])
    late_parts = flat(late_parts)
    parts = scatter_end(parts, parts_flip)
    own_half = lax.dynamic_index_in_dim(wide_half, seq_index, 1, keepdims=False)
    their_half = lax.dynamic_index_in_dim(wide_half, 1 - seq_index, 1, keepdims=False)
    wide_sum = own_half.astype(f32) + swap_seq(their_half).astype(f32)
    late_parts = scatter_end(*scatter_start([late_parts], *table_order[0]))
    late_parts, wide_sum, early_heads = lax.optimization_barrier((late_parts, wide_sum, early_heads))
    for step in table_order[1:]:
        late_parts = scatter_end(*scatter_start([late_parts], *step))
    for step in table_order[2:]:
        parts = scatter_end(*scatter_start([parts], *step))
    lines = late_parts.shape[1] // 2
    outer_parts = parts[0, 2 * split * lines :]
    all_parts = jnp.concatenate(
        [parts[0, : 2 * split * lines].reshape(split, 2, lines, 128), late_parts[0].reshape(1, 2, lines, 128)], axis=0
    )
    own_sums, their_sums = all_parts[:, 0], swap_seq(all_parts[:, 1])
    input_grad = (
        grad_summed
        + times_transpose(early_heads[:rows], heads_columns(0, split))
        + times_transpose(late_heads[:rows], heads_columns(split, pairs))
        + early_theirs.astype(f32)
        + times_transpose(late_theirs, their_columns)
    )

    both_sums = jnp.stack(
        [jnp.where(first_seq, own_sums, their_sums), jnp.where(first_seq, their_sums, own_sums)]
    ).astype(f32)
    table_lines = 2 * mask_rows * lanes
    table_grad = both_sums[:, :, :table_lines].reshape(2, pairs, 2, lanes, mask_rows, 128)
    table_grad = table_grad.transpose(0, 1, 2, 4, 3, 5).reshape(heads, mask_rows, tsize)
    mask_logits_gradient = (
        4.0 * table_grad * smoothed_gate * (1.0 - smoothed_gate) / softening_scale[:, None, None]
    )
    heads_lines = both_sums[:, :, table_lines:].reshape(2, pairs, 3, LINES, 128)
    heads_grad = heads_lines[:, :, :, :share].transpose(2, 3, 0, 1, 4).reshape(3, share, width)
    head_bias = own_sums[:, table_lines:].reshape(pairs, 3, LINES, 128)[:, :, share].astype(f32)

    vector_columns = wide_sum[:, width + inner :]
    piece = lambda index: vector_columns[:, index]

    def bias_piece(index):
        return lax.dynamic_slice_in_dim(head_bias[:, index].reshape(half_width), dp_index * share, share)

    inner_sum = wide_sum[:, width : width + inner].reshape(share, hidden_blocks, 2 * dp_size, share)
    inner_sum = inner_sum.transpose(0, 2, 1, 3).reshape(share, inner)
    outer_sum = outer_parts.reshape(width // 128, inner_share, 128).transpose(1, 0, 2).reshape(inner_share, width)
    outer_sum = outer_sum.astype(f32)
    inner_piece = vector_columns[:, 6 : 6 + hidden_blocks].T.reshape(inner_share)
    return (
        layer_out[None],
        input_grad[None],
        heads_grad[0],
        bias_piece(0),
        heads_grad[1],
        heads_grad[2],
        bias_piece(2),
        wide_sum[:, :width],
        piece(0),
        piece(1),
        piece(2),
        inner_sum,
        inner_piece,
        outer_sum,
        piece(3),
        piece(4),
        piece(5),
        mask_logits_gradient,
    )


def solution(mesh):
    split = jax.sharding.Mesh(
        mesh.devices.reshape(2, -1, 2), ("seq", "row", "core")
    )
    return jax.shard_map(
        body,
        mesh=split,
        in_specs=(
            P(("row", "core"), "seq", None),
            P(("row", "core"), "seq", None),
            P(("row", "core"), None),
            P(("row", "core"), None),
            P(("seq", "row", "core"), None),
            P(("seq", "row", "core")),
            P(("seq", "row", "core"), None),
            P(("seq", "row", "core"), None),
            P(("seq", "row", "core")),
            P(("seq", "row", "core"), None),
            P(("seq", "row", "core")),
            P(("seq", "row", "core")),
            P(("seq", "row", "core")),
            P(("seq", "row", "core"), None),
            P(("seq", "row", "core")),
            P(("seq", "row", "core"), None),
            P(("seq", "row", "core")),
            P(("seq", "row", "core")),
            P(("seq", "row", "core")),
            P(None, ("seq", "row", "core"), None),
            P(None, ("seq", "row", "core"), None),
            P(),
        ),
        out_specs=(
            P(("row", "core"), "seq", None),
            P(("row", "core"), "seq", None),
            P(("seq", "row", "core"), None),
            P(("seq", "row", "core")),
            P(("seq", "row", "core"), None),
            P(("seq", "row", "core"), None),
            P(("seq", "row", "core")),
            P(("seq", "row", "core"), None),
            P(("seq", "row", "core")),
            P(("seq", "row", "core")),
            P(("seq", "row", "core")),
            P(("seq", "row", "core"), None),
            P(("seq", "row", "core")),
            P(("seq", "row", "core"), None),
            P(("seq", "row", "core")),
            P(("seq", "row", "core")),
            P(("seq", "row", "core")),
            P(None, ("seq", "row", "core"), None),
        ),
        check_vma=False,
    )
```

```python
import functools
import math

import jax
import jax.numpy as jnp
from jax import lax
from jax.experimental import pallas as pl
from jax.experimental.pallas import tpu as pltpu
from jax.sharding import PartitionSpec as P

EPSILON = 1e-06
LOG2E = math.log2(math.e)
MASKED = -1e30
TILE = 256
NT = (((1,), (1,)), ((), ()))
NN = (((1,), (0,)), ((), ()))
TN = (((0,), (0,)), ((), ()))


def dot(a, b, dims=NN):
    return lax.dot_general(a, b, dims, preferred_element_type=jnp.float32)


def local_row(block, seq_index, half_blocks):
    return ((block // half_blocks) ^ seq_index) * (half_blocks * TILE) + (block % half_blocks) * TILE


def split_pair(rows):
    lane = lax.broadcasted_iota(jnp.int32, rows.shape, 1)
    zero = jnp.zeros_like(rows)
    return jnp.where(lane < 64, rows, zero), jnp.where(lane < 64, zero, rows)


CHUNK = 256
UNROLL = 4
BACK = 256
BACK_UNROLL = 4
LINES = 32


def chunk_row(block, seq_index, half_blocks):
    return pl.multiple_of(local_row(block, seq_index, half_blocks), TILE)


def attend_kernel(half_blocks, scale, s_ref, nk_ref, items_ref, qkv_ref, tab_ref, end_ref, att_ref, o32_ref, lse_ref, vt_ref, st_ref, acc_ref, even_ref, odd_ref):
    seq_index = s_ref[0]
    table_size = tab_ref.shape[1]
    per = CHUNK // TILE
    rows = qkv_ref.shape[0]
    pick = split_pair(jnp.ones((128, 128), jnp.bfloat16))
    reach = jnp.zeros((1, 1), jnp.float32)
    for half in pick:
        longest = []
        for at in (0, 128):
            part = qkv_ref[:, at : at + 128].astype(jnp.float32)
            squares = dot((part * part).astype(jnp.bfloat16), half, NT)
            longest.append(jnp.max(squares, keepdims=True))
        reach = jnp.maximum(reach, jnp.sqrt(longest[0]) * jnp.sqrt(longest[1]) * scale)
    small = reach[0, 0] < 80.0
    vt = qkv_ref[:, 256:384].astype(jnp.float32).T
    sub = lax.broadcasted_iota(jnp.int32, vt.shape, 0)
    vt_ref[0, 0:128] = jnp.where(sub < 64, vt, 0.0).astype(jnp.bfloat16)
    vt_ref[1, 0:128] = jnp.where(sub < 64, 0.0, vt).astype(jnp.bfloat16)
    sub = lax.broadcasted_iota(jnp.int32, (16, vt.shape[1]), 0)
    vt_ref[0, 128:144] = jnp.where(sub < 8, 1.0, 0.0).astype(jnp.bfloat16)
    vt_ref[1, 128:144] = jnp.where(sub < 8, 0.0, 1.0).astype(jnp.bfloat16)
    sub = lax.broadcasted_iota(jnp.int32, (CHUNK, TILE), 0)

    def products(block, j):
        queries = split_pair(qkv_ref[pl.ds(chunk_row(block, seq_index, half_blocks), TILE), 0:128])
        keys = qkv_ref[pl.ds(chunk_row((j * per) % (2 * half_blocks), seq_index, half_blocks), CHUNK), 128:256]
        return [dot(keys, queries[h], NT) for h in range(2)]

    def logits(block, j, raw, masked=True):
        row_end = end_ref[0:1, pl.ds(pl.multiple_of(block * TILE, TILE), TILE)]
        lane0 = pl.multiple_of((block * TILE) % table_size, TILE)
        trow = pl.multiple_of((j * CHUNK) % table_size, CHUNK)
        allowed = sub < row_end - j * CHUNK
        out = [raw[h] * scale + tab_ref[h, pl.ds(trow, CHUNK), pl.ds(lane0, TILE)] for h in range(2)]
        return [jnp.where(allowed, x, MASKED) for x in out] if masked else out

    def accumulate(block, j, probs):
        there = chunk_row((j * per) % (2 * half_blocks), seq_index, half_blocks)
        values = jnp.concatenate([vt_ref[h, :, pl.ds(there, CHUNK)] for h in range(2)], axis=1)
        acc_ref[block] += dot(values, jnp.concatenate([p.astype(jnp.bfloat16) for p in probs], axis=0))

    def finish(block, peak):
        here = chunk_row(block, seq_index, half_blocks)
        at = pl.multiple_of(block * TILE, TILE)
        acc = acc_ref[block]
        sums = [acc[128:129], acc[136:137]]
        out = jnp.concatenate([acc[0:64] / sums[0], acc[64:128] / sums[1]], axis=0).T
        o32_ref[pl.ds(here, TILE), :] = out
        att_ref[pl.ds(here, TILE), :] = out.astype(jnp.bfloat16)
        for h in range(2):
            lse_ref[0, h : h + 1, pl.ds(at, TILE)] = peak[h] + jnp.log2(sums[h])

    acc_ref[...] = jnp.zeros_like(acc_ref)

    @pl.when(small)
    def _():
        last = nk_ref.shape[0] - 1
        buffers = (even_ref, odd_ref)

        def prepare(t, to_ref):
            for h, raw in enumerate(products(jnp.minimum(items_ref[0, t], last), items_ref[1, t])):
                to_ref[h] = raw

        def use(t, from_ref, masked):
            block, j = jnp.minimum(items_ref[0, t], last), items_ref[1, t]
            accumulate(block, j, [jnp.exp2(x) for x in logits(block, j, [from_ref[h] for h in range(2)], masked)])

        prepare(0, even_ref)

        def step(masked, i, carry):
            for u in range(0, UNROLL, 2):
                t = UNROLL * i + u
                prepare(t + 1, odd_ref)
                use(t, even_ref, masked)
                prepare(t + 2, even_ref)
                use(t + 1, odd_ref, masked)
            return carry

        plain = items_ref[2, 1] // UNROLL
        lax.fori_loop(0, plain, functools.partial(step, False), 0)
        lax.fori_loop(plain, (items_ref[2, 0] + UNROLL - 1) // UNROLL, functools.partial(step, True), 0)

        def close(block, carry):
            finish(block, [0.0, 0.0])
            return carry

        lax.fori_loop(0, last + 1, close, 0)

    @pl.when(jnp.logical_not(small))
    def _():
        def query_block(block, carry):
            count = (nk_ref[block] + per - 1) // per

            def score(j, peaks):
                out = []
                for h, x in enumerate(logits(block, j, products(block, j))):
                    st_ref[h, pl.ds(pl.multiple_of(j * CHUNK, CHUNK), CHUNK), :] = x
                    out.append(jnp.maximum(peaks[h], jnp.max(x.reshape(CHUNK // 8, 8, TILE), axis=0)))
                return tuple(out)

            start = jnp.full((8, TILE), MASKED, jnp.float32)
            peaks = lax.fori_loop(0, count, score, (start, start))
            peak = [jnp.max(p, axis=0, keepdims=True) for p in peaks]

            def mix(j, carry):
                at_chunk = pl.ds(pl.multiple_of(j * CHUNK, CHUNK), CHUNK)
                accumulate(block, j, [jnp.exp2(st_ref[h, at_chunk, :] - peak[h]) for h in range(2)])
                return carry

            lax.fori_loop(0, count, mix, 0)
            finish(block, peak)
            return carry

        lax.fori_loop(0, nk_ref.shape[0], query_block, 0)


def work_items(counts, full):
    blocks = counts.shape[0]
    full = jnp.minimum(full, counts)
    parts = jnp.concatenate([full, counts - full])
    order = jnp.arange(2 * blocks, dtype=jnp.int32)
    ends = jnp.sum(jnp.where(order[:, None] >= order[None, :], parts[None, :], 0), axis=1)
    step = jnp.arange(blocks * blocks + 32, dtype=jnp.int32)
    part = jnp.sum((step[:, None] >= ends[None, :]).astype(jnp.int32), axis=1)
    first = jnp.sum(jnp.where(order[None, :] < part[:, None], parts[None, :], 0), axis=1)
    block = part % blocks
    before = jnp.sum(jnp.where(order[None, :blocks] == block[:, None], full[None, :], 0), axis=1)
    chunk = step - first + jnp.where(part >= blocks, before, 0)
    inside = part < 2 * blocks
    numbers = jnp.where(step == 0, ends[-1], ends[blocks - 1])
    rows = [jnp.where(inside, block, blocks), jnp.where(inside, chunk, blocks), numbers]
    return jnp.stack(rows).astype(jnp.int32)


def attend(qkv, tables, row_end, scalars, score_scale):
    rows = qkv.shape[0]
    pairs = qkv.shape[1] // 384
    tsize = tables.shape[1]
    spec = pltpu.PrefetchScalarGridSpec(
        num_scalar_prefetch=len(scalars),
        grid=(pairs,),
        in_specs=[
            pl.BlockSpec((rows, 384), lambda p, *_: (0, p)),
            pl.BlockSpec((2, tsize, tsize), lambda p, *_: (p, 0, 0)),
            pl.BlockSpec((1, rows), lambda p, *_: (0, 0)),
        ],
        out_specs=[
            pl.BlockSpec((rows, 128), lambda p, *_: (0, p)),
            pl.BlockSpec((rows, 128), lambda p, *_: (0, p)),
            pl.BlockSpec((1, 8, rows), lambda p, *_: (p, 0, 0)),
        ],
        scratch_shapes=[
            pltpu.VMEM((2, 144, rows), jnp.bfloat16),
            pltpu.VMEM((2, rows, TILE), jnp.float32),
            pltpu.VMEM((rows // TILE, 144, TILE), jnp.float32),
            pltpu.VMEM((2, CHUNK, TILE), jnp.float32),
            pltpu.VMEM((2, CHUNK, TILE), jnp.float32),
        ],
    )
    return pl.pallas_call(
        functools.partial(attend_kernel, rows // TILE // 2, score_scale * LOG2E),
        grid_spec=spec,
        out_shape=[
            jax.ShapeDtypeStruct((rows, pairs * 128), jnp.bfloat16),
            jax.ShapeDtypeStruct((rows, pairs * 128), jnp.float32),
            jax.ShapeDtypeStruct((pairs, 8, rows), jnp.float32),
        ],
        compiler_params=pltpu.CompilerParams(dimension_semantics=("arbitrary",), vmem_limit_bytes=40 << 20),
        cost_estimate=pl.CostEstimate(flops=40 * rows * rows * 128, transcendentals=2 * rows * rows, bytes_accessed=8 << 20),
        name="attend",
    )(*scalars, qkv, tables, row_end)


def attend_back_kernel(half_blocks, scale, score_scale, s_ref, items_ref, qkv_ref, grad_ref, o32_ref, tab_ref, end_ref, lse_ref,
                       turned_ref, back_ref, turn_ref, dqkv_ref, parts_ref, gtab_ref, kt_ref, dk_ref, dv_ref,
                       dq_ref, delta_ref, even_ref, odd_ref):
    seq_index = s_ref[0]
    table_size = tab_ref.shape[1]
    per = BACK // TILE
    blocks = 2 * half_blocks
    kt = qkv_ref[:, 128:256].astype(jnp.float32).T
    sub = lax.broadcasted_iota(jnp.int32, kt.shape, 0)
    kt_ref[0] = jnp.where(sub < 64, kt, 0.0).astype(jnp.bfloat16)
    kt_ref[1] = jnp.where(sub < 64, 0.0, kt).astype(jnp.bfloat16)
    dk_ref[...] = jnp.zeros_like(dk_ref)
    dv_ref[...] = jnp.zeros_like(dv_ref)
    dq_ref[...] = jnp.zeros_like(dq_ref)
    gtab_ref[...] = jnp.zeros_like(gtab_ref)
    inner = (grad_ref[...].astype(jnp.float32) * o32_ref[...]).T
    delta_ref[0:1, :] = jnp.sum(inner[0:64], axis=0, keepdims=True)
    delta_ref[1:2, :] = jnp.sum(inner[64:128], axis=0, keepdims=True)
    sub = lax.broadcasted_iota(jnp.int32, (BACK, TILE), 0)

    def item(t):
        block, j = jnp.minimum(items_ref[0, t], blocks - 1), items_ref[1, t]
        here = pl.ds(chunk_row(block, seq_index, half_blocks), TILE)
        there = pl.ds(chunk_row((j * per) % blocks, seq_index, half_blocks), BACK)
        return block, j, here, there

    def prepare(t, to_ref):
        block, j, here, there = item(t)
        queries, grads = split_pair(qkv_ref[here, 0:128]), split_pair(grad_ref[here, :])
        keys, values = qkv_ref[there, 128:256], qkv_ref[there, 256:384]
        for h in range(2):
            to_ref[h] = dot(keys, queries[h], NT)
            to_ref[2 + h] = dot(values, grads[h], NT)

    def use(t, from_ref, masked):
        block, j, here, there = item(t)
        at = pl.ds(pl.multiple_of(block * TILE, TILE), TILE)
        lane0 = pl.ds(pl.multiple_of((block * TILE) % table_size, TILE), TILE)
        trow = pl.ds(pl.multiple_of((j * BACK) % table_size, BACK), BACK)
        allowed = sub < end_ref[0:1, at] - j * BACK
        probs, scores = [], []
        for h in range(2):
            x = from_ref[h] * scale + tab_ref[h, trow, lane0] - lse_ref[0, h : h + 1, at]
            p = jnp.exp2(jnp.where(allowed, x, MASKED) if masked else x)
            d = p * (from_ref[2 + h] - delta_ref[h : h + 1, here])
            gtab_ref[h, trow, lane0] += d
            probs.append(p.astype(jnp.bfloat16))
            scores.append(d.astype(jnp.bfloat16))
        queries, grads = split_pair(qkv_ref[here, 0:128]), split_pair(grad_ref[here, :])
        dv_ref[there, :] += dot(jnp.concatenate(probs, axis=1), jnp.concatenate(grads, axis=0))
        dk_ref[there, :] += dot(jnp.concatenate(scores, axis=1), jnp.concatenate(queries, axis=0))
        kt = jnp.concatenate([kt_ref[h, :, there] for h in range(2)], axis=1)
        dq_ref[block] += dot(kt, jnp.concatenate(scores, axis=0))

    prepare(0, even_ref)

    def step(masked, i, carry):
        for u in range(0, BACK_UNROLL, 2):
            t = BACK_UNROLL * i + u
            prepare(t + 1, odd_ref)
            use(t, even_ref, masked)
            prepare(t + 2, even_ref)
            use(t + 1, odd_ref, masked)
        return carry

    plain = items_ref[2, 1] // BACK_UNROLL
    lax.fori_loop(0, plain, functools.partial(step, False), 0)
    lax.fori_loop(plain, (items_ref[2, 0] + BACK_UNROLL - 1) // BACK_UNROLL, functools.partial(step, True), 0)

    def close(block, carry):
        here = pl.ds(chunk_row(block, seq_index, half_blocks), TILE)
        dqkv_ref[here, 0:128] = (dq_ref[block] * score_scale).T.astype(jnp.bfloat16)
        return carry

    lax.fori_loop(0, blocks, close, 0)
    dqkv_ref[:, 128:256] = (dk_ref[...] * score_scale).astype(jnp.bfloat16)
    dqkv_ref[:, 256:384] = dv_ref[...].astype(jnp.bfloat16)
    owners, lines = 2 * parts_ref.shape[0], parts_ref.shape[3]
    mask_rows = table_size // owners
    share = turned_ref.shape[1] // owners
    table_lines = lines - 3 * LINES
    for h in range(2):
        table = dot(back_ref[...], gtab_ref[h].astype(jnp.bfloat16), NT).astype(jnp.bfloat16)
        table = dot(table, turn_ref[...])
        for i in range(table_size // 128):
            at = (h * (table_size // 128) + i) * mask_rows
            part = table[:, i * 128 : (i + 1) * 128].reshape(owners // 2, 2, mask_rows, 128)
            parts_ref[:, 0, :, at : at + mask_rows, :] = part.astype(jnp.bfloat16)
    bias = jnp.sum(dqkv_ref[...].astype(jnp.float32), axis=0, keepdims=True)
    step = 384 // share
    for i in range(owners // step):
        part = dot(turned_ref[:, i * 384 : (i + 1) * 384], dqkv_ref[...], TN)
        for c in range(3):
            lanes = slice(c * 128, (c + 1) * 128)
            sums = jnp.broadcast_to(bias[:, lanes], (step * (LINES - share), 128))
            block = jnp.concatenate(
                [part[:, lanes].reshape(step, share, 128), sums.reshape(step, LINES - share, 128)], axis=1
            )
            at = table_lines + c * LINES
            block = block.reshape(step // 2, 2, LINES, 128)
            parts_ref[i * step // 2 : (i + 1) * step // 2, 0, :, at : at + LINES, :] = block.astype(jnp.bfloat16)


def attend_back(first, pairs, owners, qkv, grads, o32, tables, row_end, lse, turned, back, turn, scalars, score_scale):
    rows = qkv.shape[0]
    tsize = tables.shape[1]
    width = turned.shape[1]
    lines = 2 * (tsize // owners) * (tsize // 128) + 3 * LINES
    spec = pltpu.PrefetchScalarGridSpec(
        num_scalar_prefetch=len(scalars),
        grid=(pairs,),
        in_specs=[
            pl.BlockSpec((rows, 384), lambda p, *_: (0, first + p)),
            pl.BlockSpec((rows, 128), lambda p, *_: (0, first + p)),
            pl.BlockSpec((rows, 128), lambda p, *_: (0, first + p)),
            pl.BlockSpec((2, tsize, tsize), lambda p, *_: (first + p, 0, 0)),
            pl.BlockSpec((1, rows), lambda p, *_: (0, 0)),
            pl.BlockSpec((1, 8, rows), lambda p, *_: (first + p, 0, 0)),
            pl.BlockSpec((rows, width), lambda p, *_: (0, 0), pipeline_mode=pl.Buffered(1)),
            pl.BlockSpec((tsize, tsize), lambda p, *_: (0, 0), pipeline_mode=pl.Buffered(1)),
            pl.BlockSpec((tsize, tsize), lambda p, *_: (0, 0), pipeline_mode=pl.Buffered(1)),
        ],
        out_specs=[
            pl.BlockSpec((rows, 384), lambda p, *_: (0, p)),
            pl.BlockSpec((owners // 2, 1, 2, lines, 128), lambda p, *_: (0, p, 0, 0, 0)),
        ],
        scratch_shapes=[
            pltpu.VMEM((2, tsize, tsize), jnp.float32),
            pltpu.VMEM((2, 128, rows), jnp.bfloat16),
            pltpu.VMEM((rows, 128), jnp.float32),
            pltpu.VMEM((rows, 128), jnp.float32),
            pltpu.VMEM((rows // TILE, 128, TILE), jnp.float32),
            pltpu.VMEM((8, rows), jnp.float32),
            pltpu.VMEM((4, BACK, TILE), jnp.float32),
            pltpu.VMEM((4, BACK, TILE), jnp.float32),
        ],
    )
    return pl.pallas_call(
        functools.partial(attend_back_kernel, rows // TILE // 2, score_scale * LOG2E, score_scale),
        grid_spec=spec,
        out_shape=[
            jax.ShapeDtypeStruct((rows, pairs * 384), jnp.bfloat16),
            jax.ShapeDtypeStruct((owners // 2, pairs, 2, lines, 128), jnp.bfloat16),
        ],
        compiler_params=pltpu.CompilerParams(dimension_semantics=("arbitrary",), vmem_limit_bytes=56 << 20),
        cost_estimate=pl.CostEstimate(
            flops=pairs * rows * rows, transcendentals=rows * rows // 64, bytes_accessed=1 << 20
        ),
        name="attend_back",
    )(*scalars, qkv, grads, o32, tables, row_end, lse, turned, back, turn)


GELU_A = math.sqrt(2.0 / math.pi)
GELU_B = 0.044715


def row_stats(values):
    center = values - jnp.mean(values, axis=-1, keepdims=True)
    rstdev = lax.rsqrt(jnp.mean(center * center, axis=-1, keepdims=True) + EPSILON)
    return center * rstdev, rstdev


def row_back(gradient, normed, rstdev, gain):
    scaled = gradient * gain
    return rstdev * (
        scaled
        - jnp.mean(scaled, axis=-1, keepdims=True)
        - normed * jnp.mean(scaled * normed, axis=-1, keepdims=True)
    )


def layer_kernel(s_ref, *refs):
    f32, bf16 = jnp.float32, jnp.bfloat16
    (own_ref, their_ref, x_ref, up_ref, wide_ref,
     out_ref, gsum_ref, gatt_ref, att_ref, first_ref, active_ref, ginner_ref, gouter_ref, gproj_ref,
     vsum_ref, slope_ref, acc_ref, n1_ref, f1_ref, vec_ref) = refs
    width = x_ref.shape[1]
    inner = active_ref.shape[1]
    step = width
    vec = lambda i: vec_ref[i : i + 1, :]
    total = lambda value: jnp.sum(value, axis=0, keepdims=True)

    def outer_rows(c):
        return wide_ref[:, pl.ds(pl.multiple_of(width + inner + c * step, 128), width)]

    @pl.when(pl.program_id(0) == 0)
    def _():
        vsum_ref[...] = jnp.zeros_like(vsum_ref)
        vec_ref[...] = wide_ref[:, width + 2 * inner :].astype(f32).T

    first_seq = s_ref[0] == 0
    mine, others = own_ref[...], their_ref[...]

    @pl.when(first_seq)
    def _():
        att_ref[:, : width // 2] = mine
        att_ref[:, width // 2 :] = others

    @pl.when(jnp.logical_not(first_seq))
    def _():
        att_ref[:, : width // 2] = others
        att_ref[:, width // 2 :] = mine

    summed = x_ref[...].astype(f32) + (dot(att_ref[...], wide_ref[:, :width]) + vec(0))
    normed, rstdev1 = row_stats(summed)
    n1_ref[...] = normed
    first = normed * vec(1) + vec(2)
    f1_ref[...] = first
    first_ref[...] = first.astype(bf16)
    acc_ref[...] = jnp.zeros_like(acc_ref)

    def up(c, carry):
        at = pl.ds(pl.multiple_of(c * step, 128), step)
        w_at = pl.ds(pl.multiple_of(width + c * step, 128), step)
        u = dot(first_ref[...], wide_ref[:, w_at]) + vec_ref[pl.ds(6 + c, 1), :]
        square = u * u
        t = jnp.tanh(GELU_A * (u + GELU_B * (square * u)))
        half = 0.5 * (1.0 + t)
        slope_ref[:, at] = half + 0.5 * u * (1.0 - t * t) * (GELU_A * (1.0 + 3.0 * GELU_B * square))
        active = (u * half).astype(bf16)
        active_ref[:, at] = active
        acc_ref[...] += dot(active, outer_rows(c))
        return carry

    lax.fori_loop(0, inner // step, up, 0)
    normed, rstdev = row_stats(f1_ref[...] + (acc_ref[...] + vec(3)))
    out_ref[...] = (normed * vec(4) + vec(5)).astype(bf16)
    gradient = up_ref[...].astype(f32)
    vsum_ref[4:5, :] += total(gradient * normed)
    vsum_ref[5:6, :] += total(gradient)
    grad_sum = row_back(gradient, normed, rstdev, vec(4))
    grad_low = grad_sum.astype(bf16)
    gouter_ref[...] = grad_low
    vsum_ref[3:4, :] += total(grad_low.astype(f32))
    acc_ref[...] = grad_sum

    def down(c, carry):
        at = pl.ds(pl.multiple_of(c * step, 128), step)
        w_at = pl.ds(pl.multiple_of(width + c * step, 128), step)
        g = (dot(gouter_ref[...], outer_rows(c), NT) * slope_ref[:, at]).astype(bf16)
        ginner_ref[:, at] = g
        vsum_ref[pl.ds(6 + c, 1), :] += total(g.astype(f32))
        acc_ref[...] += dot(g, wide_ref[:, w_at], NT)
        return carry

    lax.fori_loop(0, inner // step, down, 0)
    grad_first = acc_ref[...]
    normed = n1_ref[...]
    vsum_ref[1:2, :] += total(grad_first * normed)
    vsum_ref[2:3, :] += total(grad_first)
    grad_summed = row_back(grad_first, normed, rstdev1, vec(1))
    gsum_ref[...] = grad_summed
    grad_low = grad_summed.astype(bf16)
    gproj_ref[...] = grad_low
    vsum_ref[0:1, :] += total(grad_low.astype(f32))
    gatt_ref[...] = dot(grad_low, wide_ref[:, :width], NT).astype(bf16)


def layer(seq_index, own, their, x, upstream, wide):
    rows, width = x.shape
    inner = (wide.shape[1] - width - 128) // 2
    block = 512
    by_rows = lambda size: pl.BlockSpec((block, size), lambda i, *_: (i, 0))
    whole = lambda shape: pl.BlockSpec(shape, lambda i, *_: (0,) * len(shape), pipeline_mode=pl.Buffered(1))
    once = lambda shape: pl.BlockSpec(shape, lambda i, *_: (0, 0))
    spec = pltpu.PrefetchScalarGridSpec(
        num_scalar_prefetch=1,
        grid=(rows // block,),
        in_specs=[by_rows(width // 2)] * 2
        + [by_rows(width), by_rows(width), whole(wide.shape)],
        out_specs=[by_rows(width)] * 5
        + [by_rows(inner)] * 2
        + [by_rows(width)] * 2
        + [once((16, width))],
        scratch_shapes=[pltpu.VMEM((block, inner), jnp.float32)] + [pltpu.VMEM((block, width), jnp.float32)] * 3
        + [pltpu.VMEM((128, width), jnp.float32)],
    )
    shape = lambda size, dtype: jax.ShapeDtypeStruct((rows, size), dtype)
    low = jnp.bfloat16
    return pl.pallas_call(
        layer_kernel,
        grid_spec=spec,
        out_shape=[shape(width, low), shape(width, jnp.float32), shape(width, low), shape(width, low), shape(width, low)]
        + [shape(inner, low)] * 2
        + [shape(width, low)] * 2
        + [jax.ShapeDtypeStruct((16, width), jnp.float32)],
        compiler_params=pltpu.CompilerParams(dimension_semantics=("arbitrary",), vmem_limit_bytes=56 << 20),
        cost_estimate=pl.CostEstimate(
            flops=8 * rows * width * (width // 2 + inner), transcendentals=rows * inner, bytes_accessed=36 << 20
        ),
        name="layer",
    )(seq_index, own, their, x, upstream, wide)


def weights_kernel(s_ref, place_ref, vsum_ref, att_ref, first_ref, active_ref, gproj_ref, gouter_ref, ginner_ref,
                   wide_ref, mine_ref, their_ref):
    bf16 = jnp.bfloat16
    i, c = pl.program_id(0), pl.program_id(1)
    width = gproj_ref.shape[1]
    inner = width * pl.num_programs(1)
    owners, share = mine_ref.shape[0], mine_ref.shape[3]

    @pl.when(c == 0)
    def _():
        wide_ref[:, :width] = dot(att_ref[...], gproj_ref[...], TN).astype(bf16)
        sums = vsum_ref[...]
        sums = jnp.concatenate([sums, jnp.zeros((128 - sums.shape[0], sums.shape[1]), jnp.float32)], axis=0)
        wide_ref[:, width + inner :] = sums.T.astype(bf16)

    at = pl.ds(pl.multiple_of(width * (c + 1), 128), width)
    wide_ref[:, at] = dot(first_ref[...], ginner_ref[...], TN).astype(bf16)
    part = dot(active_ref[...], gouter_ref[...], TN)

    def place(out_ref):
        for k in range(owners):
            rows = part[k * share : (k + 1) * share].astype(bf16)
            for i in range(width // 128):
                out_ref[place_ref[k], i, c] = rows[:, i * 128 : (i + 1) * 128]

    @pl.when(i == s_ref[0])
    def _():
        place(mine_ref)

    @pl.when(i != s_ref[0])
    def _():
        place(their_ref)


def layer_weights(seq_index, places, sums, attended, first, active, gproj, gouter, ginner):
    rows, width = gproj.shape
    inner = ginner.shape[1]
    half = width // 2
    steps = inner // width
    owners = places.shape[0]
    blocks = (owners, width // 128, steps, half // owners, 128)
    spec = pltpu.PrefetchScalarGridSpec(
        num_scalar_prefetch=2,
        grid=(2, steps),
        in_specs=[
            pl.BlockSpec((sums.shape[0], half), lambda i, c, *_: (0, i)),
            pl.BlockSpec((rows, half), lambda i, c, *_: (0, i)),
            pl.BlockSpec((rows, half), lambda i, c, *_: (0, i)),
            pl.BlockSpec((rows, half), lambda i, c, *_: (0, 2 * c + i)),
            pl.BlockSpec((rows, width), lambda i, c, *_: (0, 0)),
            pl.BlockSpec((rows, width), lambda i, c, *_: (0, 0)),
            pl.BlockSpec((rows, width), lambda i, c, *_: (0, c)),
        ],
        out_specs=[
            pl.BlockSpec((half, width + inner + 128), lambda i, c, *_: (0, i)),
            pl.BlockSpec(blocks, lambda i, c, *_: (0, 0, 0, 0, 0)),
            pl.BlockSpec(blocks, lambda i, c, *_: (0, 0, 0, 0, 0)),
        ],
    )
    return pl.pallas_call(
        weights_kernel,
        grid_spec=spec,
        out_shape=[
            jax.ShapeDtypeStruct((half, 2 * (width + inner + 128)), jnp.bfloat16),
            jax.ShapeDtypeStruct(blocks, jnp.bfloat16),
            jax.ShapeDtypeStruct(blocks, jnp.bfloat16),
        ],
        compiler_params=pltpu.CompilerParams(dimension_semantics=("arbitrary", "arbitrary"), vmem_limit_bytes=56 << 20),
        cost_estimate=pl.CostEstimate(
            flops=4 * rows * width * (width // 2 + inner), transcendentals=0, bytes_accessed=32 << 20
        ),
        name="layer_weights",
    )(seq_index, places, sums, attended, first, active, gproj, gouter, ginner)


def matmul(left_side, right_side):
    return jnp.dot(left_side, right_side, preferred_element_type=jnp.float32)


def contract_rows(left_side, right_side):
    return jnp.einsum("rd,re->de", left_side, right_side, preferred_element_type=jnp.float32)


def times_transpose(left_side, right_side):
    return jnp.einsum("re,de->rd", left_side, right_side, preferred_element_type=jnp.float32)


def norm_forward(values, norm_gain, norm_shift):
    center = values - jnp.mean(values, axis=-1, keepdims=True)
    rstdev = lax.rsqrt(jnp.mean(center * center, axis=-1, keepdims=True) + EPSILON)
    normed = center * rstdev
    return (normed * norm_gain + norm_shift, normed, rstdev)


def norm_backward(gradient, normed, rstdev, norm_gain):
    scaled = gradient * norm_gain
    back = rstdev * (
        scaled
        - jnp.mean(scaled, axis=-1, keepdims=True)
        - normed * jnp.mean(scaled * normed, axis=-1, keepdims=True)
    )
    return (back, jnp.sum(gradient * normed, axis=0), jnp.sum(gradient, axis=0))


def swap_seq(value):
    return lax.ppermute(value, "seq", [(0, 1), (1, 0)])


def flip(value, axis, bit):
    return lax.ppermute(value, axis, [(i, i ^ bit) for i in range(lax.axis_size(axis))])


def row_steps():
    bits = [1 << i for i in range(1, lax.axis_size("row").bit_length() - 1)]
    return [("row", bit) for bit in bits], [("row", 1)]


def scatter_order():
    far, near = row_steps()
    return [("core", 1)] + near + far


def coordinates(owner):
    row_size = lax.axis_size("row")
    return {"seq": owner // (2 * row_size), "row": (owner // 2) % row_size, "core": owner % 2}


def places_of(order, count):
    owner = coordinates(jnp.arange(count, dtype=jnp.int32))
    place = jnp.zeros((count,), jnp.int32)
    for step, (axis, bit) in enumerate(order):
        place = place + ((((owner[axis] ^ lax.axis_index(axis)) // bit) & 1) << step)
    return place


def scatter_start(parts, axis, bit):
    half = parts[0].shape[0] // 2
    kept = [part[:half] for part in parts]
    sent = [part[half:] for part in parts]
    joined = lambda values: values[0] if len(values) == 1 else jnp.concatenate(values, axis=1)
    return joined(kept), flip(joined(sent), axis, bit)


def scatter_end(kept, arrived):
    return (kept.astype(jnp.float32) + arrived.astype(jnp.float32)).astype(jnp.bfloat16)


def body(
    incoming_activations,
    upstream_derivative,
    grid_coordinates,
    word_segment_ids,
    asking_matrix,
    asking_shift,
    lookup_matrix,
    content_matrix,
    content_shift,
    mixing_result_matrix,
    mixing_result_shift,
    post_mixing_scaling,
    post_mixing_offset,
    expand_matrix,
    expand_shift,
    contract_matrix,
    contract_shift,
    post_perceptron_scaling,
    post_perceptron_offset,
    pair_gate_scores,
    gate_random_jitter,
    softening_scale,
):
    f32, bf16 = jnp.float32, jnp.bfloat16
    heads = softening_scale.shape[0]
    width = incoming_activations.shape[2]
    rows = incoming_activations.shape[1]
    inner = expand_matrix.shape[1]
    tsize = pair_gate_scores.shape[2]
    score_scale = 1.0 / math.sqrt(width // heads)
    half_width, half_heads = width // 2, heads // 2
    pairs = half_heads // 2
    seq_index = lax.axis_index("seq")
    dp_size = 2 * lax.axis_size("row")
    dp_index = 2 * lax.axis_index("row") + lax.axis_index("core")
    owner = seq_index * dp_size + dp_index
    first_seq = seq_index == 0
    inputs = incoming_activations[0]
    share = asking_matrix.shape[0]
    inner_share = expand_shift.shape[0]
    mask_rows = tsize // (2 * dp_size)
    lanes = tsize // 128

    def seq_ordered(mine, others):
        return jnp.stack([jnp.where(first_seq, mine, others), jnp.where(first_seq, others, mine)])


    packed = jnp.stack(
        [part.reshape(share, 2, pairs, 128) for part in (asking_matrix, lookup_matrix, content_matrix)], axis=3
    )
    packed = packed.transpose(1, 2, 3, 0, 4).reshape(2, 3 * pairs * share, 128)
    lines = jnp.stack([asking_shift, content_shift])
    lines = jnp.pad(lines, ((0, 6), (0, 128 - share)))[None]
    smoothed_gate = jax.nn.sigmoid(
        (pair_gate_scores + gate_random_jitter) / softening_scale[:, None, None]
    )
    mask_low = smoothed_gate.astype(bf16).reshape(2, half_heads, mask_rows, lanes, 128)
    mask_low = mask_low.transpose(0, 1, 3, 2, 4).reshape(2, -1, 128)
    packed = jnp.concatenate([packed, jnp.concatenate([lines, lines], axis=0), mask_low], axis=1)
    kept = lax.dynamic_index_in_dim(packed, seq_index, 0, keepdims=False)
    sent = lax.dynamic_index_in_dim(packed, 1 - seq_index, 0, keepdims=False)
    packed = seq_ordered(kept, swap_seq(sent))
    other_inputs = swap_seq(inputs)
    hidden_blocks = inner_share // share
    hidden = expand_matrix.reshape(share, 2 * dp_size, hidden_blocks, share)
    contract_blocks = contract_matrix.reshape(hidden_blocks, share, width)
    columns = jnp.stack(
        [
            mixing_result_shift,
            post_mixing_scaling,
            post_mixing_offset,
            contract_shift,
            post_perceptron_scaling,
            post_perceptron_offset,
        ]
        + [expand_shift[k * share : (k + 1) * share] for k in range(hidden_blocks)],
        axis=1,
    )
    wide_share = jnp.concatenate(
        [mixing_result_matrix, hidden.transpose(0, 2, 1, 3).reshape(share, inner)]
        + [contract_blocks[k] for k in range(hidden_blocks)]
        + [jnp.pad(columns, ((0, 0), (0, 128 - columns.shape[1])))],
        axis=1,
    )
    wide_share = seq_ordered(wide_share, swap_seq(wide_share))
    wide_share, unused = lax.optimization_barrier((wide_share, packed))
    gathered = lax.all_gather(packed, ("row", "core"), axis=1, tiled=True)
    wide_matrix = lax.all_gather(wide_share, ("row", "core"), axis=1, tiled=True).reshape(width, -1)
    both_inputs = jnp.concatenate([inputs, other_inputs], axis=0)
    start = grid_coordinates[0, 0]
    turned = (jnp.arange(tsize, dtype=jnp.int32) + start) % tsize
    turn = (turned[:, None] == jnp.arange(tsize, dtype=jnp.int32)[None, :]).astype(bf16)
    row = jnp.arange(mask_rows, dtype=jnp.int32)
    table_order = scatter_order()
    table_places = places_of(table_order[::-1], dp_size)
    own_seq = (jnp.arange(2, dtype=jnp.int32) ^ seq_index)[:, None, None]
    input_spots = ((table_places[None, :] * 2 + own_seq[:, :, 0]) * share)[:, :, None] + jnp.arange(share)
    turned_inputs = matmul(
        both_inputs,
        (input_spots.reshape(-1)[:, None] == jnp.arange(width, dtype=jnp.int32)[None, :]).astype(bf16),
    ).astype(bf16)
    table_spots = ((table_places[None, :] * 2 + own_seq[:, :, 0]) * mask_rows)[:, :, None] + row
    table_spots = table_spots.reshape(-1)
    spot_turn = jnp.sum(jnp.where(turn > 0, table_spots[None, :], 0), axis=1)
    turn_back = (jnp.arange(tsize, dtype=jnp.int32)[:, None] == spot_turn[None, :]).astype(bf16)

    gathered, turned_inputs = lax.optimization_barrier((gathered, turned_inputs))
    gathered = gathered.reshape(2, dp_size, -1, 128)
    weight_lines = 3 * pairs * share
    heads_matrix = gathered[:, :, :weight_lines].reshape(2, dp_size, 3 * pairs, share, 128)
    heads_matrix = heads_matrix.transpose(0, 1, 3, 2, 4).reshape(width, 3 * half_width)
    shifts = lax.dynamic_index_in_dim(gathered, seq_index, 0, keepdims=False)
    shifts = shifts[:, weight_lines : weight_lines + 2, :share].astype(f32).transpose(1, 0, 2).reshape(2, pairs, 128)
    own_mask = gathered[:, :, weight_lines + 8 :].reshape(2 * dp_size, half_heads, lanes, mask_rows, 128)
    own_mask = own_mask.transpose(1, 0, 3, 2, 4).reshape(half_heads, tsize, tsize)

    segments = word_segment_ids[0]
    values_range = jnp.arange(8, dtype=jnp.int32)[:, None]
    segment_ends = jnp.sum((segments[None, :] <= values_range).astype(jnp.int32), axis=1)
    row_end = jnp.sum(jnp.where(segments[None, :] == values_range, segment_ends[:, None], 0), axis=0)
    counts = (row_end.reshape(-1, TILE)[:, -1] + (TILE - 1)) // TILE
    tables = jnp.einsum("hab,cb->hca", own_mask, turn, preferred_element_type=f32).astype(bf16)
    tables = jnp.einsum("hca,da->hcd", tables, turn, preferred_element_type=f32) * (4.0 * LOG2E)

    heads_shift = jnp.stack([shifts[0], jnp.zeros_like(shifts[0]), shifts[1]], axis=1)
    heads_rows = (matmul(both_inputs, heads_matrix) + heads_shift.reshape(-1)).astype(bf16)
    seq_scalar = seq_index[None].astype(jnp.int32)
    items = work_items(counts, row_end.reshape(-1, TILE)[:, 0] // TILE)
    scalars = (seq_scalar, counts, items)
    back_scalars = (seq_scalar, items)
    row_end = row_end[None]
    own_attended, wide_attended, logsum = attend(heads_rows, tables, row_end, scalars, score_scale)
    their_attended = swap_seq(own_attended[rows:])

    their_columns = swap_seq(heads_matrix[:, (pairs - 1) * 384 :])

    (layer_out, grad_summed, grad_attended, attended, first_low, active_low, grad_inner_low, grad_outer_low,
     grad_proj_low, vector_sums) = layer(
        seq_scalar,
        own_attended,
        their_attended,
        inputs,
        upstream_derivative[0],
        wide_matrix,
    )
    grad_attended, their_columns = lax.optimization_barrier((grad_attended, their_columns))
    low, high = grad_attended[:, :half_width], grad_attended[:, half_width:]
    arrived = swap_seq(jnp.where(first_seq, high, low))
    grads_all = jnp.concatenate([jnp.where(first_seq, low, high), arrived], axis=0)
    table_places_here = places_of(table_order[::-1], dp_size)
    wide_grad, outer_mine, outer_theirs = layer_weights(
        seq_scalar, table_places_here, vector_sums, attended, first_low, active_low,
        grad_proj_low, grad_outer_low, grad_inner_low,
    )
    wide_grad, grads_all, outer_mine, outer_theirs = lax.optimization_barrier(
        (wide_grad, grads_all, outer_mine, outer_theirs)
    )
    wide_half = lax.psum_scatter(wide_grad, ("row", "core"), scatter_dimension=0, tiled=True)
    wide_half = wide_half.reshape(share, 2, -1)
    outer_arrived = swap_seq(outer_theirs)

    split = pairs - 1
    back = lambda first, count, grads: attend_back(
        first, count, 2 * dp_size, heads_rows, grads, wide_attended, tables, row_end, logsum,
        turned_inputs, turn_back, turn, back_scalars, score_scale,
    )
    heads_columns = lambda first, last: heads_matrix[:, first * 384 : last * 384]
    early_heads, early_parts = back(0, split, grads_all)
    flat = lambda parts: parts.reshape(dp_size, -1, 128)
    early_heads, early_parts, outer_arrived = lax.optimization_barrier((early_heads, early_parts, outer_arrived))
    outer_parts = scatter_end(outer_mine, outer_arrived)
    parts = scatter_end(*scatter_start([flat(early_parts), flat(outer_parts)], *table_order[0]))
    early_sent = times_transpose(early_heads[rows:], heads_columns(0, split)).astype(bf16)
    grads_all, parts, early_sent = lax.optimization_barrier((grads_all, parts, early_sent))
    early_theirs = swap_seq(early_sent)
    parts, parts_flip = scatter_start([parts], *table_order[1])
    late_heads, late_parts = back(split, 1, grads_all)
    late_heads, late_parts, parts_flip, early_theirs, wide_half, early_heads = lax.optimization_barrier(
        (late_heads, late_parts, parts_flip, early_theirs, wide_half, early_heads)
    )
    late_theirs = swap_seq(late_heads[rows:])
    late_parts = flat(late_parts)
    parts = scatter_end(parts, parts_flip)
    own_half = lax.dynamic_index_in_dim(wide_half, seq_index, 1, keepdims=False)
    their_half = lax.dynamic_index_in_dim(wide_half, 1 - seq_index, 1, keepdims=False)
    wide_sum = own_half.astype(f32) + swap_seq(their_half).astype(f32)
    late_parts = scatter_end(*scatter_start([late_parts], *table_order[0]))
    late_parts, wide_sum, early_heads = lax.optimization_barrier((late_parts, wide_sum, early_heads))
    for step in table_order[1:]:
        late_parts = scatter_end(*scatter_start([late_parts], *step))
    for step in table_order[2:]:
        parts = scatter_end(*scatter_start([parts], *step))
    lines = late_parts.shape[1] // 2
    outer_parts = parts[0, 2 * split * lines :]
    all_parts = jnp.concatenate(
        [parts[0, : 2 * split * lines].reshape(split, 2, lines, 128), late_parts[0].reshape(1, 2, lines, 128)], axis=0
    )
    own_sums, their_sums = all_parts[:, 0], swap_seq(all_parts[:, 1])
    input_grad = (
        grad_summed
        + times_transpose(early_heads[:rows], heads_columns(0, split))
        + times_transpose(late_heads[:rows], heads_columns(split, pairs))
        + early_theirs.astype(f32)
        + times_transpose(late_theirs, their_columns)
    )

    both_sums = jnp.stack(
        [jnp.where(first_seq, own_sums, their_sums), jnp.where(first_seq, their_sums, own_sums)]
    ).astype(f32)
    table_lines = 2 * mask_rows * lanes
    table_grad = both_sums[:, :, :table_lines].reshape(2, pairs, 2, lanes, mask_rows, 128)
    table_grad = table_grad.transpose(0, 1, 2, 4, 3, 5).reshape(heads, mask_rows, tsize)
    mask_logits_gradient = (
        4.0 * table_grad * smoothed_gate * (1.0 - smoothed_gate) / softening_scale[:, None, None]
    )
    heads_lines = both_sums[:, :, table_lines:].reshape(2, pairs, 3, LINES, 128)
    heads_grad = heads_lines[:, :, :, :share].transpose(2, 3, 0, 1, 4).reshape(3, share, width)
    head_bias = own_sums[:, table_lines:].reshape(pairs, 3, LINES, 128)[:, :, share].astype(f32)

    vector_columns = wide_sum[:, width + inner :]
    piece = lambda index: vector_columns[:, index]

    def bias_piece(index):
        return lax.dynamic_slice_in_dim(head_bias[:, index].reshape(half_width), dp_index * share, share)

    inner_sum = wide_sum[:, width : width + inner].reshape(share, hidden_blocks, 2 * dp_size, share)
    inner_sum = inner_sum.transpose(0, 2, 1, 3).reshape(share, inner)
    outer_sum = outer_parts.reshape(width // 128, inner_share, 128).transpose(1, 0, 2).reshape(inner_share, width)
    outer_sum = outer_sum.astype(f32)
    inner_piece = vector_columns[:, 6 : 6 + hidden_blocks].T.reshape(inner_share)
    return (
        layer_out[None],
        input_grad[None],
        heads_grad[0],
        bias_piece(0),
        heads_grad[1],
        heads_grad[2],
        bias_piece(2),
        wide_sum[:, :width],
        piece(0),
        piece(1),
        piece(2),
        inner_sum,
        inner_piece,
        outer_sum,
        piece(3),
        piece(4),
        piece(5),
        mask_logits_gradient,
    )


def solution(mesh):
    split = jax.sharding.Mesh(
        mesh.devices.reshape(2, -1, 2), ("seq", "row", "core")
    )
    return jax.shard_map(
        body,
        mesh=split,
        in_specs=(
            P(("row", "core"), "seq", None),
            P(("row", "core"), "seq", None),
            P(("row", "core"), None),
            P(("row", "core"), None),
            P(("seq", "row", "core"), None),
            P(("seq", "row", "core")),
            P(("seq", "row", "core"), None),
            P(("seq", "row", "core"), None),
            P(("seq", "row", "core")),
            P(("seq", "row", "core"), None),
            P(("seq", "row", "core")),
            P(("seq", "row", "core")),
            P(("seq", "row", "core")),
            P(("seq", "row", "core"), None),
            P(("seq", "row", "core")),
            P(("seq", "row", "core"), None),
            P(("seq", "row", "core")),
            P(("seq", "row", "core")),
            P(("seq", "row", "core")),
            P(None, ("seq", "row", "core"), None),
            P(None, ("seq", "row", "core"), None),
            P(),
        ),
        out_specs=(
            P(("row", "core"), "seq", None),
            P(("row", "core"), "seq", None),
            P(("seq", "row", "core"), None),
            P(("seq", "row", "core")),
            P(("seq", "row", "core"), None),
            P(("seq", "row", "core"), None),
            P(("seq", "row", "core")),
            P(("seq", "row", "core"), None),
            P(("seq", "row", "core")),
            P(("seq", "row", "core")),
            P(("seq", "row", "core")),
            P(("seq", "row", "core"), None),
            P(("seq", "row", "core")),
            P(("seq", "row", "core"), None),
            P(("seq", "row", "core")),
            P(("seq", "row", "core")),
            P(("seq", "row", "core")),
            P(None, ("seq", "row", "core"), None),
        ),
        check_vma=False,
    )
```

```python
import functools
import math

import jax
import jax.numpy as jnp
from jax import lax
from jax.experimental import pallas as pl
from jax.experimental.pallas import tpu as pltpu
from jax.sharding import PartitionSpec as P

EPSILON = 1e-06
LOG2E = math.log2(math.e)
MASKED = -1e30
TILE = 256
NT = (((1,), (1,)), ((), ()))
NN = (((1,), (0,)), ((), ()))
TN = (((0,), (0,)), ((), ()))


def dot(a, b, dims=NN):
    return lax.dot_general(a, b, dims, preferred_element_type=jnp.float32)


def local_row(block, seq_index, half_blocks):
    return ((block // half_blocks) ^ seq_index) * (half_blocks * TILE) + (block % half_blocks) * TILE


def split_pair(rows):
    lane = lax.broadcasted_iota(jnp.int32, rows.shape, 1)
    zero = jnp.zeros_like(rows)
    return jnp.where(lane < 64, rows, zero), jnp.where(lane < 64, zero, rows)


CHUNK = 256
UNROLL = 4
BACK = 256
BACK_UNROLL = 4
LINES = 32


def chunk_row(block, seq_index, half_blocks):
    return pl.multiple_of(local_row(block, seq_index, half_blocks), TILE)


def attend_kernel(half_blocks, scale, s_ref, nk_ref, items_ref, qkv_ref, tab_ref, end_ref, att_ref, o32_ref, lse_ref, vt_ref, st_ref, acc_ref, even_ref, odd_ref):
    seq_index = s_ref[0]
    table_size = tab_ref.shape[1]
    per = CHUNK // TILE
    rows = qkv_ref.shape[0]
    pick = split_pair(jnp.ones((128, 128), jnp.bfloat16))
    reach = jnp.zeros((1, 1), jnp.float32)
    for half in pick:
        longest = []
        for at in (0, 128):
            part = qkv_ref[:, at : at + 128].astype(jnp.float32)
            squares = dot((part * part).astype(jnp.bfloat16), half, NT)
            longest.append(jnp.max(squares, keepdims=True))
        reach = jnp.maximum(reach, jnp.sqrt(longest[0]) * jnp.sqrt(longest[1]) * scale)
    small = reach[0, 0] < 80.0
    vt = qkv_ref[:, 256:384].astype(jnp.float32).T
    sub = lax.broadcasted_iota(jnp.int32, vt.shape, 0)
    vt_ref[0, 0:128] = jnp.where(sub < 64, vt, 0.0).astype(jnp.bfloat16)
    vt_ref[1, 0:128] = jnp.where(sub < 64, 0.0, vt).astype(jnp.bfloat16)
    sub = lax.broadcasted_iota(jnp.int32, (16, vt.shape[1]), 0)
    vt_ref[0, 128:144] = jnp.where(sub < 8, 1.0, 0.0).astype(jnp.bfloat16)
    vt_ref[1, 128:144] = jnp.where(sub < 8, 0.0, 1.0).astype(jnp.bfloat16)
    sub = lax.broadcasted_iota(jnp.int32, (CHUNK, TILE), 0)

    def products(block, j):
        queries = split_pair(qkv_ref[pl.ds(chunk_row(block, seq_index, half_blocks), TILE), 0:128])
        keys = qkv_ref[pl.ds(chunk_row((j * per) % (2 * half_blocks), seq_index, half_blocks), CHUNK), 128:256]
        return [dot(keys, queries[h], NT) for h in range(2)]

    def logits(block, j, raw, masked=True):
        row_end = end_ref[0:1, pl.ds(pl.multiple_of(block * TILE, TILE), TILE)]
        lane0 = pl.multiple_of((block * TILE) % table_size, TILE)
        trow = pl.multiple_of((j * CHUNK) % table_size, CHUNK)
        allowed = sub < row_end - j * CHUNK
        out = [raw[h] * scale + tab_ref[h, pl.ds(trow, CHUNK), pl.ds(lane0, TILE)] for h in range(2)]
        return [jnp.where(allowed, x, MASKED) for x in out] if masked else out

    def accumulate(block, j, probs):
        there = chunk_row((j * per) % (2 * half_blocks), seq_index, half_blocks)
        values = jnp.concatenate([vt_ref[h, :, pl.ds(there, CHUNK)] for h in range(2)], axis=1)
        acc_ref[block] += dot(values, jnp.concatenate([p.astype(jnp.bfloat16) for p in probs], axis=0))

    def finish(block, peak):
        here = chunk_row(block, seq_index, half_blocks)
        at = pl.multiple_of(block * TILE, TILE)
        acc = acc_ref[block]
        sums = [acc[128:129], acc[136:137]]
        out = jnp.concatenate([acc[0:64] / sums[0], acc[64:128] / sums[1]], axis=0).T
        o32_ref[pl.ds(here, TILE), :] = out
        att_ref[pl.ds(here, TILE), :] = out.astype(jnp.bfloat16)
        for h in range(2):
            lse_ref[0, h : h + 1, pl.ds(at, TILE)] = peak[h] + jnp.log2(sums[h])

    acc_ref[...] = jnp.zeros_like(acc_ref)

    @pl.when(small)
    def _():
        last = nk_ref.shape[0] - 1
        buffers = (even_ref, odd_ref)

        def prepare(t, to_ref):
            for h, raw in enumerate(products(jnp.minimum(items_ref[0, t], last), items_ref[1, t])):
                to_ref[h] = raw

        def use(t, from_ref, masked):
            block, j = jnp.minimum(items_ref[0, t], last), items_ref[1, t]
            accumulate(block, j, [jnp.exp2(x) for x in logits(block, j, [from_ref[h] for h in range(2)], masked)])

        prepare(0, even_ref)

        def step(masked, i, carry):
            for u in range(0, UNROLL, 2):
                t = UNROLL * i + u
                prepare(t + 1, odd_ref)
                use(t, even_ref, masked)
                prepare(t + 2, even_ref)
                use(t + 1, odd_ref, masked)
            return carry

        plain = items_ref[2, 1] // UNROLL
        lax.fori_loop(0, plain, functools.partial(step, False), 0)
        lax.fori_loop(plain, (items_ref[2, 0] + UNROLL - 1) // UNROLL, functools.partial(step, True), 0)

        def close(block, carry):
            finish(block, [0.0, 0.0])
            return carry

        lax.fori_loop(0, last + 1, close, 0)

    @pl.when(jnp.logical_not(small))
    def _():
        def query_block(block, carry):
            count = (nk_ref[block] + per - 1) // per

            def score(j, peaks):
                out = []
                for h, x in enumerate(logits(block, j, products(block, j))):
                    st_ref[h, pl.ds(pl.multiple_of(j * CHUNK, CHUNK), CHUNK), :] = x
                    out.append(jnp.maximum(peaks[h], jnp.max(x.reshape(CHUNK // 8, 8, TILE), axis=0)))
                return tuple(out)

            start = jnp.full((8, TILE), MASKED, jnp.float32)
            peaks = lax.fori_loop(0, count, score, (start, start))
            peak = [jnp.max(p, axis=0, keepdims=True) for p in peaks]

            def mix(j, carry):
                at_chunk = pl.ds(pl.multiple_of(j * CHUNK, CHUNK), CHUNK)
                accumulate(block, j, [jnp.exp2(st_ref[h, at_chunk, :] - peak[h]) for h in range(2)])
                return carry

            lax.fori_loop(0, count, mix, 0)
            finish(block, peak)
            return carry

        lax.fori_loop(0, nk_ref.shape[0], query_block, 0)


def work_items(counts, full):
    blocks = counts.shape[0]
    full = jnp.minimum(full, counts)
    parts = jnp.concatenate([full, counts - full])
    order = jnp.arange(2 * blocks, dtype=jnp.int32)
    ends = jnp.sum(jnp.where(order[:, None] >= order[None, :], parts[None, :], 0), axis=1)
    step = jnp.arange(blocks * blocks + 32, dtype=jnp.int32)
    part = jnp.sum((step[:, None] >= ends[None, :]).astype(jnp.int32), axis=1)
    first = jnp.sum(jnp.where(order[None, :] < part[:, None], parts[None, :], 0), axis=1)
    block = part % blocks
    before = jnp.sum(jnp.where(order[None, :blocks] == block[:, None], full[None, :], 0), axis=1)
    chunk = step - first + jnp.where(part >= blocks, before, 0)
    inside = part < 2 * blocks
    numbers = jnp.where(step == 0, ends[-1], ends[blocks - 1])
    rows = [jnp.where(inside, block, blocks), jnp.where(inside, chunk, blocks), numbers]
    return jnp.stack(rows).astype(jnp.int32)


def attend(qkv, tables, row_end, scalars, score_scale):
    rows = qkv.shape[0]
    pairs = qkv.shape[1] // 384
    tsize = tables.shape[1]
    spec = pltpu.PrefetchScalarGridSpec(
        num_scalar_prefetch=len(scalars),
        grid=(pairs,),
        in_specs=[
            pl.BlockSpec((rows, 384), lambda p, *_: (0, p)),
            pl.BlockSpec((2, tsize, tsize), lambda p, *_: (p, 0, 0)),
            pl.BlockSpec((1, rows), lambda p, *_: (0, 0)),
        ],
        out_specs=[
            pl.BlockSpec((rows, 128), lambda p, *_: (0, p)),
            pl.BlockSpec((rows, 128), lambda p, *_: (0, p)),
            pl.BlockSpec((1, 8, rows), lambda p, *_: (p, 0, 0)),
        ],
        scratch_shapes=[
            pltpu.VMEM((2, 144, rows), jnp.bfloat16),
            pltpu.VMEM((2, rows, TILE), jnp.float32),
            pltpu.VMEM((rows // TILE, 144, TILE), jnp.float32),
            pltpu.VMEM((2, CHUNK, TILE), jnp.float32),
            pltpu.VMEM((2, CHUNK, TILE), jnp.float32),
        ],
    )
    return pl.pallas_call(
        functools.partial(attend_kernel, rows // TILE // 2, score_scale * LOG2E),
        grid_spec=spec,
        out_shape=[
            jax.ShapeDtypeStruct((rows, pairs * 128), jnp.bfloat16),
            jax.ShapeDtypeStruct((rows, pairs * 128), jnp.float32),
            jax.ShapeDtypeStruct((pairs, 8, rows), jnp.float32),
        ],
        compiler_params=pltpu.CompilerParams(dimension_semantics=("arbitrary",), vmem_limit_bytes=40 << 20),
        cost_estimate=pl.CostEstimate(flops=40 * rows * rows * 128, transcendentals=2 * rows * rows, bytes_accessed=8 << 20),
        name="attend",
    )(*scalars, qkv, tables, row_end)


def attend_back_kernel(half_blocks, scale, score_scale, s_ref, items_ref, qkv_ref, grad_ref, o32_ref, tab_ref, end_ref, lse_ref,
                       turned_ref, back_ref, turn_ref, dqkv_ref, parts_ref, gtab_ref, kt_ref, dk_ref, dv_ref,
                       dq_ref, delta_ref, even_ref, odd_ref):
    seq_index = s_ref[0]
    table_size = tab_ref.shape[1]
    per = BACK // TILE
    blocks = 2 * half_blocks
    kt = qkv_ref[:, 128:256].astype(jnp.float32).T
    sub = lax.broadcasted_iota(jnp.int32, kt.shape, 0)
    kt_ref[0] = jnp.where(sub < 64, kt, 0.0).astype(jnp.bfloat16)
    kt_ref[1] = jnp.where(sub < 64, 0.0, kt).astype(jnp.bfloat16)
    dk_ref[...] = jnp.zeros_like(dk_ref)
    dv_ref[...] = jnp.zeros_like(dv_ref)
    dq_ref[...] = jnp.zeros_like(dq_ref)
    gtab_ref[...] = jnp.zeros_like(gtab_ref)
    inner = (grad_ref[...].astype(jnp.float32) * o32_ref[...]).T
    delta_ref[0:1, :] = jnp.sum(inner[0:64], axis=0, keepdims=True)
    delta_ref[1:2, :] = jnp.sum(inner[64:128], axis=0, keepdims=True)
    sub = lax.broadcasted_iota(jnp.int32, (BACK, TILE), 0)

    def item(t):
        block, j = jnp.minimum(items_ref[0, t], blocks - 1), items_ref[1, t]
        here = pl.ds(chunk_row(block, seq_index, half_blocks), TILE)
        there = pl.ds(chunk_row((j * per) % blocks, seq_index, half_blocks), BACK)
        return block, j, here, there

    def prepare(t, to_ref):
        block, j, here, there = item(t)
        queries, grads = split_pair(qkv_ref[here, 0:128]), split_pair(grad_ref[here, :])
        keys, values = qkv_ref[there, 128:256], qkv_ref[there, 256:384]
        for h in range(2):
            to_ref[h] = dot(keys, queries[h], NT)
            to_ref[2 + h] = dot(values, grads[h], NT)

    def use(t, from_ref, masked):
        block, j, here, there = item(t)
        at = pl.ds(pl.multiple_of(block * TILE, TILE), TILE)
        lane0 = pl.ds(pl.multiple_of((block * TILE) % table_size, TILE), TILE)
        trow = pl.ds(pl.multiple_of((j * BACK) % table_size, BACK), BACK)
        allowed = sub < end_ref[0:1, at] - j * BACK
        probs, scores = [], []
        for h in range(2):
            x = from_ref[h] * scale + tab_ref[h, trow, lane0] - lse_ref[0, h : h + 1, at]
            p = jnp.exp2(jnp.where(allowed, x, MASKED) if masked else x)
            d = p * (from_ref[2 + h] - delta_ref[h : h + 1, here])
            gtab_ref[h, trow, lane0] += d
            probs.append(p.astype(jnp.bfloat16))
            scores.append(d.astype(jnp.bfloat16))
        queries, grads = split_pair(qkv_ref[here, 0:128]), split_pair(grad_ref[here, :])
        dv_ref[there, :] += dot(jnp.concatenate(probs, axis=1), jnp.concatenate(grads, axis=0))
        dk_ref[there, :] += dot(jnp.concatenate(scores, axis=1), jnp.concatenate(queries, axis=0))
        kt = jnp.concatenate([kt_ref[h, :, there] for h in range(2)], axis=1)
        dq_ref[block] += dot(kt, jnp.concatenate(scores, axis=0))

    prepare(0, even_ref)

    def step(masked, i, carry):
        for u in range(0, BACK_UNROLL, 2):
            t = BACK_UNROLL * i + u
            prepare(t + 1, odd_ref)
            use(t, even_ref, masked)
            prepare(t + 2, even_ref)
            use(t + 1, odd_ref, masked)
        return carry

    plain = items_ref[2, 1] // BACK_UNROLL
    lax.fori_loop(0, plain, functools.partial(step, False), 0)
    lax.fori_loop(plain, (items_ref[2, 0] + BACK_UNROLL - 1) // BACK_UNROLL, functools.partial(step, True), 0)

    def close(block, carry):
        here = pl.ds(chunk_row(block, seq_index, half_blocks), TILE)
        dqkv_ref[here, 0:128] = (dq_ref[block] * score_scale).T.astype(jnp.bfloat16)
        return carry

    lax.fori_loop(0, blocks, close, 0)
    dqkv_ref[:, 128:256] = (dk_ref[...] * score_scale).astype(jnp.bfloat16)
    dqkv_ref[:, 256:384] = dv_ref[...].astype(jnp.bfloat16)
    owners, lines = 2 * parts_ref.shape[0], parts_ref.shape[3]
    mask_rows = table_size // owners
    share = turned_ref.shape[1] // owners
    table_lines = lines - 3 * LINES
    for h in range(2):
        table = dot(back_ref[...], gtab_ref[h].astype(jnp.bfloat16), NT).astype(jnp.bfloat16)
        table = dot(table, turn_ref[...])
        for i in range(table_size // 128):
            at = (h * (table_size // 128) + i) * mask_rows
            part = table[:, i * 128 : (i + 1) * 128].reshape(owners // 2, 2, mask_rows, 128)
            parts_ref[:, 0, :, at : at + mask_rows, :] = part.astype(jnp.bfloat16)
    bias = jnp.sum(dqkv_ref[...].astype(jnp.float32), axis=0, keepdims=True)
    step = 384 // share
    for i in range(owners // step):
        part = dot(turned_ref[:, i * 384 : (i + 1) * 384], dqkv_ref[...], TN)
        for c in range(3):
            lanes = slice(c * 128, (c + 1) * 128)
            sums = jnp.broadcast_to(bias[:, lanes], (step * (LINES - share), 128))
            block = jnp.concatenate(
                [part[:, lanes].reshape(step, share, 128), sums.reshape(step, LINES - share, 128)], axis=1
            )
            at = table_lines + c * LINES
            block = block.reshape(step // 2, 2, LINES, 128)
            parts_ref[i * step // 2 : (i + 1) * step // 2, 0, :, at : at + LINES, :] = block.astype(jnp.bfloat16)


def attend_back(first, pairs, owners, qkv, grads, o32, tables, row_end, lse, turned, back, turn, scalars, score_scale):
    rows = qkv.shape[0]
    tsize = tables.shape[1]
    width = turned.shape[1]
    lines = 2 * (tsize // owners) * (tsize // 128) + 3 * LINES
    spec = pltpu.PrefetchScalarGridSpec(
        num_scalar_prefetch=len(scalars),
        grid=(pairs,),
        in_specs=[
            pl.BlockSpec((rows, 384), lambda p, *_: (0, first + p)),
            pl.BlockSpec((rows, 128), lambda p, *_: (0, first + p)),
            pl.BlockSpec((rows, 128), lambda p, *_: (0, first + p)),
            pl.BlockSpec((2, tsize, tsize), lambda p, *_: (first + p, 0, 0)),
            pl.BlockSpec((1, rows), lambda p, *_: (0, 0)),
            pl.BlockSpec((1, 8, rows), lambda p, *_: (first + p, 0, 0)),
            pl.BlockSpec((rows, width), lambda p, *_: (0, 0), pipeline_mode=pl.Buffered(1)),
            pl.BlockSpec((tsize, tsize), lambda p, *_: (0, 0), pipeline_mode=pl.Buffered(1)),
            pl.BlockSpec((tsize, tsize), lambda p, *_: (0, 0), pipeline_mode=pl.Buffered(1)),
        ],
        out_specs=[
            pl.BlockSpec((rows, 384), lambda p, *_: (0, p)),
            pl.BlockSpec((owners // 2, 1, 2, lines, 128), lambda p, *_: (0, p, 0, 0, 0)),
        ],
        scratch_shapes=[
            pltpu.VMEM((2, tsize, tsize), jnp.float32),
            pltpu.VMEM((2, 128, rows), jnp.bfloat16),
            pltpu.VMEM((rows, 128), jnp.float32),
            pltpu.VMEM((rows, 128), jnp.float32),
            pltpu.VMEM((rows // TILE, 128, TILE), jnp.float32),
            pltpu.VMEM((8, rows), jnp.float32),
            pltpu.VMEM((4, BACK, TILE), jnp.float32),
            pltpu.VMEM((4, BACK, TILE), jnp.float32),
        ],
    )
    return pl.pallas_call(
        functools.partial(attend_back_kernel, rows // TILE // 2, score_scale * LOG2E, score_scale),
        grid_spec=spec,
        out_shape=[
            jax.ShapeDtypeStruct((rows, pairs * 384), jnp.bfloat16),
            jax.ShapeDtypeStruct((owners // 2, pairs, 2, lines, 128), jnp.bfloat16),
        ],
        compiler_params=pltpu.CompilerParams(dimension_semantics=("arbitrary",), vmem_limit_bytes=56 << 20),
        cost_estimate=pl.CostEstimate(
            flops=pairs * rows * rows, transcendentals=rows * rows // 64, bytes_accessed=1 << 20
        ),
        name="attend_back",
    )(*scalars, qkv, grads, o32, tables, row_end, lse, turned, back, turn)


GELU_A = math.sqrt(2.0 / math.pi)
GELU_B = 0.044715


def row_stats(values):
    center = values - jnp.mean(values, axis=-1, keepdims=True)
    rstdev = lax.rsqrt(jnp.mean(center * center, axis=-1, keepdims=True) + EPSILON)
    return center * rstdev, rstdev


def row_back(gradient, normed, rstdev, gain):
    scaled = gradient * gain
    return rstdev * (
        scaled
        - jnp.mean(scaled, axis=-1, keepdims=True)
        - normed * jnp.mean(scaled * normed, axis=-1, keepdims=True)
    )


def layer_kernel(s_ref, *refs):
    f32, bf16 = jnp.float32, jnp.bfloat16
    (own_ref, their_ref, x_ref, up_ref, wide_ref,
     out_ref, gsum_ref, gatt_ref, att_ref, first_ref, active_ref, ginner_ref, gouter_ref, gproj_ref,
     vsum_ref, slope_ref, acc_ref, n1_ref, f1_ref, vec_ref) = refs
    width = x_ref.shape[1]
    inner = active_ref.shape[1]
    step = width
    vec = lambda i: vec_ref[i : i + 1, :]
    total = lambda value: jnp.sum(value, axis=0, keepdims=True)

    def outer_rows(c):
        return wide_ref[:, pl.ds(pl.multiple_of(width + inner + c * step, 128), width)]

    @pl.when(pl.program_id(0) == 0)
    def _():
        vsum_ref[...] = jnp.zeros_like(vsum_ref)
        vec_ref[...] = wide_ref[:, width + 2 * inner :].astype(f32).T

    first_seq = s_ref[0] == 0
    mine, others = own_ref[...], their_ref[...]

    @pl.when(first_seq)
    def _():
        att_ref[:, : width // 2] = mine
        att_ref[:, width // 2 :] = others

    @pl.when(jnp.logical_not(first_seq))
    def _():
        att_ref[:, : width // 2] = others
        att_ref[:, width // 2 :] = mine

    summed = x_ref[...].astype(f32) + (dot(att_ref[...], wide_ref[:, :width]) + vec(0))
    normed, rstdev1 = row_stats(summed)
    n1_ref[...] = normed
    first = normed * vec(1) + vec(2)
    f1_ref[...] = first
    first_ref[...] = first.astype(bf16)
    acc_ref[...] = jnp.zeros_like(acc_ref)

    def up(c, carry):
        at = pl.ds(pl.multiple_of(c * step, 128), step)
        w_at = pl.ds(pl.multiple_of(width + c * step, 128), step)
        u = dot(first_ref[...], wide_ref[:, w_at]) + vec_ref[pl.ds(6 + c, 1), :]
        square = u * u
        t = jnp.tanh(GELU_A * (u + GELU_B * (square * u)))
        half = 0.5 * (1.0 + t)
        slope_ref[:, at] = half + 0.5 * u * (1.0 - t * t) * (GELU_A * (1.0 + 3.0 * GELU_B * square))
        active = (u * half).astype(bf16)
        active_ref[:, at] = active
        acc_ref[...] += dot(active, outer_rows(c))
        return carry

    lax.fori_loop(0, inner // step, up, 0)
    normed, rstdev = row_stats(f1_ref[...] + (acc_ref[...] + vec(3)))
    out_ref[...] = (normed * vec(4) + vec(5)).astype(bf16)
    gradient = up_ref[...].astype(f32)
    vsum_ref[4:5, :] += total(gradient * normed)
    vsum_ref[5:6, :] += total(gradient)
    grad_sum = row_back(gradient, normed, rstdev, vec(4))
    grad_low = grad_sum.astype(bf16)
    gouter_ref[...] = grad_low
    vsum_ref[3:4, :] += total(grad_low.astype(f32))
    acc_ref[...] = grad_sum

    def down(c, carry):
        at = pl.ds(pl.multiple_of(c * step, 128), step)
        w_at = pl.ds(pl.multiple_of(width + c * step, 128), step)
        g = (dot(gouter_ref[...], outer_rows(c), NT) * slope_ref[:, at]).astype(bf16)
        ginner_ref[:, at] = g
        vsum_ref[pl.ds(6 + c, 1), :] += total(g.astype(f32))
        acc_ref[...] += dot(g, wide_ref[:, w_at], NT)
        return carry

    lax.fori_loop(0, inner // step, down, 0)
    grad_first = acc_ref[...]
    normed = n1_ref[...]
    vsum_ref[1:2, :] += total(grad_first * normed)
    vsum_ref[2:3, :] += total(grad_first)
    grad_summed = row_back(grad_first, normed, rstdev1, vec(1))
    gsum_ref[...] = grad_summed
    grad_low = grad_summed.astype(bf16)
    gproj_ref[...] = grad_low
    vsum_ref[0:1, :] += total(grad_low.astype(f32))
    gatt_ref[...] = dot(grad_low, wide_ref[:, :width], NT).astype(bf16)


def layer(seq_index, own, their, x, upstream, wide):
    rows, width = x.shape
    inner = (wide.shape[1] - width - 128) // 2
    block = 512
    by_rows = lambda size: pl.BlockSpec((block, size), lambda i, *_: (i, 0))
    whole = lambda shape: pl.BlockSpec(shape, lambda i, *_: (0,) * len(shape), pipeline_mode=pl.Buffered(1))
    once = lambda shape: pl.BlockSpec(shape, lambda i, *_: (0, 0))
    spec = pltpu.PrefetchScalarGridSpec(
        num_scalar_prefetch=1,
        grid=(rows // block,),
        in_specs=[by_rows(width // 2)] * 2
        + [by_rows(width), by_rows(width), whole(wide.shape)],
        out_specs=[by_rows(width)] * 5
        + [by_rows(inner)] * 2
        + [by_rows(width)] * 2
        + [once((16, width))],
        scratch_shapes=[pltpu.VMEM((block, inner), jnp.float32)] + [pltpu.VMEM((block, width), jnp.float32)] * 3
        + [pltpu.VMEM((128, width), jnp.float32)],
    )
    shape = lambda size, dtype: jax.ShapeDtypeStruct((rows, size), dtype)
    low = jnp.bfloat16
    return pl.pallas_call(
        layer_kernel,
        grid_spec=spec,
        out_shape=[shape(width, low), shape(width, jnp.float32), shape(width, low), shape(width, low), shape(width, low)]
        + [shape(inner, low)] * 2
        + [shape(width, low)] * 2
        + [jax.ShapeDtypeStruct((16, width), jnp.float32)],
        compiler_params=pltpu.CompilerParams(dimension_semantics=("arbitrary",), vmem_limit_bytes=56 << 20),
        cost_estimate=pl.CostEstimate(
            flops=8 * rows * width * (width // 2 + inner), transcendentals=rows * inner, bytes_accessed=36 << 20
        ),
        name="layer",
    )(seq_index, own, their, x, upstream, wide)


def weights_kernel(s_ref, place_ref, vsum_ref, att_ref, first_ref, active_ref, gproj_ref, gouter_ref, ginner_ref,
                   wide_ref, mine_ref, their_ref):
    bf16 = jnp.bfloat16
    i, c = pl.program_id(0), pl.program_id(1)
    width = gproj_ref.shape[1]
    inner = width * pl.num_programs(1)
    owners, share = mine_ref.shape[0], mine_ref.shape[3]

    @pl.when(c == 0)
    def _():
        wide_ref[:, :width] = dot(att_ref[...], gproj_ref[...], TN).astype(bf16)
        sums = vsum_ref[...]
        sums = jnp.concatenate([sums, jnp.zeros((128 - sums.shape[0], sums.shape[1]), jnp.float32)], axis=0)
        wide_ref[:, width + inner :] = sums.T.astype(bf16)

    at = pl.ds(pl.multiple_of(width * (c + 1), 128), width)
    wide_ref[:, at] = dot(first_ref[...], ginner_ref[...], TN).astype(bf16)
    part = dot(active_ref[...], gouter_ref[...], TN)

    def place(out_ref):
        for k in range(owners):
            rows = part[k * share : (k + 1) * share].astype(bf16)
            for i in range(width // 128):
                out_ref[place_ref[k], i, c] = rows[:, i * 128 : (i + 1) * 128]

    @pl.when(i == s_ref[0])
    def _():
        place(mine_ref)

    @pl.when(i != s_ref[0])
    def _():
        place(their_ref)


def layer_weights(seq_index, places, sums, attended, first, active, gproj, gouter, ginner):
    rows, width = gproj.shape
    inner = ginner.shape[1]
    half = width // 2
    steps = inner // width
    owners = places.shape[0]
    blocks = (owners, width // 128, steps, half // owners, 128)
    spec = pltpu.PrefetchScalarGridSpec(
        num_scalar_prefetch=2,
        grid=(2, steps),
        in_specs=[
            pl.BlockSpec((sums.shape[0], half), lambda i, c, *_: (0, i)),
            pl.BlockSpec((rows, half), lambda i, c, *_: (0, i)),
            pl.BlockSpec((rows, half), lambda i, c, *_: (0, i)),
            pl.BlockSpec((rows, half), lambda i, c, *_: (0, 2 * c + i)),
            pl.BlockSpec((rows, width), lambda i, c, *_: (0, 0)),
            pl.BlockSpec((rows, width), lambda i, c, *_: (0, 0)),
            pl.BlockSpec((rows, width), lambda i, c, *_: (0, c)),
        ],
        out_specs=[
            pl.BlockSpec((half, width + inner + 128), lambda i, c, *_: (0, i)),
            pl.BlockSpec(blocks, lambda i, c, *_: (0, 0, 0, 0, 0)),
            pl.BlockSpec(blocks, lambda i, c, *_: (0, 0, 0, 0, 0)),
        ],
    )
    return pl.pallas_call(
        weights_kernel,
        grid_spec=spec,
        out_shape=[
            jax.ShapeDtypeStruct((half, 2 * (width + inner + 128)), jnp.bfloat16),
            jax.ShapeDtypeStruct(blocks, jnp.bfloat16),
            jax.ShapeDtypeStruct(blocks, jnp.bfloat16),
        ],
        compiler_params=pltpu.CompilerParams(dimension_semantics=("arbitrary", "arbitrary"), vmem_limit_bytes=56 << 20),
        cost_estimate=pl.CostEstimate(
            flops=4 * rows * width * (width // 2 + inner), transcendentals=0, bytes_accessed=32 << 20
        ),
        name="layer_weights",
    )(seq_index, places, sums, attended, first, active, gproj, gouter, ginner)


def matmul(left_side, right_side):
    return jnp.dot(left_side, right_side, preferred_element_type=jnp.float32)


def contract_rows(left_side, right_side):
    return jnp.einsum("rd,re->de", left_side, right_side, preferred_element_type=jnp.float32)


def times_transpose(left_side, right_side):
    return jnp.einsum("re,de->rd", left_side, right_side, preferred_element_type=jnp.float32)


def norm_forward(values, norm_gain, norm_shift):
    center = values - jnp.mean(values, axis=-1, keepdims=True)
    rstdev = lax.rsqrt(jnp.mean(center * center, axis=-1, keepdims=True) + EPSILON)
    normed = center * rstdev
    return (normed * norm_gain + norm_shift, normed, rstdev)


def norm_backward(gradient, normed, rstdev, norm_gain):
    scaled = gradient * norm_gain
    back = rstdev * (
        scaled
        - jnp.mean(scaled, axis=-1, keepdims=True)
        - normed * jnp.mean(scaled * normed, axis=-1, keepdims=True)
    )
    return (back, jnp.sum(gradient * normed, axis=0), jnp.sum(gradient, axis=0))


def swap_seq(value):
    return lax.ppermute(value, "seq", [(0, 1), (1, 0)])


def flip(value, axis, bit):
    return lax.ppermute(value, axis, [(i, i ^ bit) for i in range(lax.axis_size(axis))])


def row_steps():
    bits = [1 << i for i in range(1, lax.axis_size("row").bit_length() - 1)]
    return [("row", bit) for bit in bits], [("row", 1)]


def scatter_order():
    far, near = row_steps()
    return [("core", 1)] + near + far


def coordinates(owner):
    row_size = lax.axis_size("row")
    return {"seq": owner // (2 * row_size), "row": (owner // 2) % row_size, "core": owner % 2}


def places_of(order, count):
    owner = coordinates(jnp.arange(count, dtype=jnp.int32))
    place = jnp.zeros((count,), jnp.int32)
    for step, (axis, bit) in enumerate(order):
        place = place + ((((owner[axis] ^ lax.axis_index(axis)) // bit) & 1) << step)
    return place


def scatter_start(parts, axis, bit):
    half = parts[0].shape[0] // 2
    kept = [part[:half] for part in parts]
    sent = [part[half:] for part in parts]
    joined = lambda values: values[0] if len(values) == 1 else jnp.concatenate(values, axis=1)
    return joined(kept), flip(joined(sent), axis, bit)


def scatter_end(kept, arrived):
    return (kept.astype(jnp.float32) + arrived.astype(jnp.float32)).astype(jnp.bfloat16)


def body(
    incoming_activations,
    upstream_derivative,
    grid_coordinates,
    word_segment_ids,
    asking_matrix,
    asking_shift,
    lookup_matrix,
    content_matrix,
    content_shift,
    mixing_result_matrix,
    mixing_result_shift,
    post_mixing_scaling,
    post_mixing_offset,
    expand_matrix,
    expand_shift,
    contract_matrix,
    contract_shift,
    post_perceptron_scaling,
    post_perceptron_offset,
    pair_gate_scores,
    gate_random_jitter,
    softening_scale,
):
    f32, bf16 = jnp.float32, jnp.bfloat16
    heads = softening_scale.shape[0]
    width = incoming_activations.shape[2]
    rows = incoming_activations.shape[1]
    inner = expand_matrix.shape[1]
    tsize = pair_gate_scores.shape[2]
    score_scale = 1.0 / math.sqrt(width // heads)
    half_width, half_heads = width // 2, heads // 2
    pairs = half_heads // 2
    seq_index = lax.axis_index("seq")
    dp_size = 2 * lax.axis_size("row")
    dp_index = 2 * lax.axis_index("row") + lax.axis_index("core")
    owner = seq_index * dp_size + dp_index
    first_seq = seq_index == 0
    inputs = incoming_activations[0]
    share = asking_matrix.shape[0]
    inner_share = expand_shift.shape[0]
    mask_rows = tsize // (2 * dp_size)
    lanes = tsize // 128

    def seq_ordered(mine, others):
        return jnp.stack([jnp.where(first_seq, mine, others), jnp.where(first_seq, others, mine)])


    parts = (asking_matrix, lookup_matrix, content_matrix)
    packed = jnp.stack(
        [
            jnp.concatenate([part[:, at * 128 : (at + 1) * 128] for at in range(first, first + pairs) for part in parts])
            for first in (0, pairs)
        ]
    )
    lines = jnp.stack([asking_shift, content_shift])
    lines = jnp.pad(lines, ((0, 6), (0, 128 - share)))[None]
    smoothed_gate = jax.nn.sigmoid(
        (pair_gate_scores + gate_random_jitter) / softening_scale[:, None, None]
    )
    mask_low = smoothed_gate.astype(bf16).reshape(2, half_heads, mask_rows, lanes, 128)
    mask_low = mask_low.transpose(0, 1, 3, 2, 4).reshape(2, -1, 128)
    packed = jnp.concatenate([packed, jnp.concatenate([lines, lines], axis=0), mask_low], axis=1)
    kept = lax.dynamic_index_in_dim(packed, seq_index, 0, keepdims=False)
    sent = lax.dynamic_index_in_dim(packed, 1 - seq_index, 0, keepdims=False)
    packed = seq_ordered(kept, swap_seq(sent))
    other_inputs = swap_seq(inputs)
    hidden_blocks = inner_share // share
    hidden = expand_matrix.reshape(share, 2 * dp_size, hidden_blocks, share)
    contract_blocks = contract_matrix.reshape(hidden_blocks, share, width)
    columns = jnp.stack(
        [
            mixing_result_shift,
            post_mixing_scaling,
            post_mixing_offset,
            contract_shift,
            post_perceptron_scaling,
            post_perceptron_offset,
        ]
        + [expand_shift[k * share : (k + 1) * share] for k in range(hidden_blocks)],
        axis=1,
    )
    wide_share = jnp.concatenate(
        [mixing_result_matrix, hidden.transpose(0, 2, 1, 3).reshape(share, inner)]
        + [contract_blocks[k] for k in range(hidden_blocks)]
        + [jnp.pad(columns, ((0, 0), (0, 128 - columns.shape[1])))],
        axis=1,
    )
    wide_share = seq_ordered(wide_share, swap_seq(wide_share))
    wide_share, unused = lax.optimization_barrier((wide_share, packed))
    gathered = lax.all_gather(packed, ("row", "core"), axis=1, tiled=True)
    wide_matrix = lax.all_gather(wide_share, ("row", "core"), axis=1, tiled=True).reshape(width, -1)
    both_inputs = jnp.concatenate([inputs, other_inputs], axis=0)
    start = grid_coordinates[0, 0]
    turned = (jnp.arange(tsize, dtype=jnp.int32) + start) % tsize
    turn = (turned[:, None] == jnp.arange(tsize, dtype=jnp.int32)[None, :]).astype(bf16)
    row = jnp.arange(mask_rows, dtype=jnp.int32)
    table_order = scatter_order()
    table_places = places_of(table_order[::-1], dp_size)
    own_seq = (jnp.arange(2, dtype=jnp.int32) ^ seq_index)[:, None, None]
    input_spots = ((table_places[None, :] * 2 + own_seq[:, :, 0]) * share)[:, :, None] + jnp.arange(share)
    turned_inputs = matmul(
        both_inputs,
        (input_spots.reshape(-1)[:, None] == jnp.arange(width, dtype=jnp.int32)[None, :]).astype(bf16),
    ).astype(bf16)
    table_spots = ((table_places[None, :] * 2 + own_seq[:, :, 0]) * mask_rows)[:, :, None] + row
    table_spots = table_spots.reshape(-1)
    spot_turn = jnp.sum(jnp.where(turn > 0, table_spots[None, :], 0), axis=1)
    turn_back = (jnp.arange(tsize, dtype=jnp.int32)[:, None] == spot_turn[None, :]).astype(bf16)

    gathered, turned_inputs = lax.optimization_barrier((gathered, turned_inputs))
    gathered = gathered.reshape(2, dp_size, -1, 128)
    weight_lines = 3 * pairs * share
    heads_matrix = gathered[:, :, :weight_lines].reshape(2, dp_size, 3 * pairs, share, 128)
    heads_matrix = heads_matrix.transpose(0, 1, 3, 2, 4).reshape(width, 3 * half_width)
    shifts = lax.dynamic_index_in_dim(gathered, seq_index, 0, keepdims=False)
    shifts = shifts[:, weight_lines : weight_lines + 2, :share].astype(f32).transpose(1, 0, 2).reshape(2, pairs, 128)
    own_mask = gathered[:, :, weight_lines + 8 :].reshape(2 * dp_size, half_heads, lanes, mask_rows, 128)
    own_mask = own_mask.transpose(1, 0, 3, 2, 4).reshape(half_heads, tsize, tsize)

    segments = word_segment_ids[0]
    values_range = jnp.arange(8, dtype=jnp.int32)[:, None]
    segment_ends = jnp.sum((segments[None, :] <= values_range).astype(jnp.int32), axis=1)
    row_end = jnp.sum(jnp.where(segments[None, :] == values_range, segment_ends[:, None], 0), axis=0)
    counts = (row_end.reshape(-1, TILE)[:, -1] + (TILE - 1)) // TILE
    tables = jnp.einsum("hab,cb->hca", own_mask, turn, preferred_element_type=f32).astype(bf16)
    tables = jnp.einsum("hca,da->hcd", tables, turn, preferred_element_type=f32) * (4.0 * LOG2E)

    heads_shift = jnp.stack([shifts[0], jnp.zeros_like(shifts[0]), shifts[1]], axis=1)
    heads_rows = (matmul(both_inputs, heads_matrix) + heads_shift.reshape(-1)).astype(bf16)
    seq_scalar = seq_index[None].astype(jnp.int32)
    items = work_items(counts, row_end.reshape(-1, TILE)[:, 0] // TILE)
    scalars = (seq_scalar, counts, items)
    back_scalars = (seq_scalar, items)
    row_end = row_end[None]
    own_attended, wide_attended, logsum = attend(heads_rows, tables, row_end, scalars, score_scale)
    their_attended = swap_seq(own_attended[rows:])

    their_columns = swap_seq(heads_matrix[:, (pairs - 1) * 384 :])

    (layer_out, grad_summed, grad_attended, attended, first_low, active_low, grad_inner_low, grad_outer_low,
     grad_proj_low, vector_sums) = layer(
        seq_scalar,
        own_attended,
        their_attended,
        inputs,
        upstream_derivative[0],
        wide_matrix,
    )
    grad_attended, their_columns = lax.optimization_barrier((grad_attended, their_columns))
    low, high = grad_attended[:, :half_width], grad_attended[:, half_width:]
    arrived = swap_seq(jnp.where(first_seq, high, low))
    grads_all = jnp.concatenate([jnp.where(first_seq, low, high), arrived], axis=0)
    table_places_here = places_of(table_order[::-1], dp_size)
    wide_grad, outer_mine, outer_theirs = layer_weights(
        seq_scalar, table_places_here, vector_sums, attended, first_low, active_low,
        grad_proj_low, grad_outer_low, grad_inner_low,
    )
    wide_grad, grads_all, outer_mine, outer_theirs = lax.optimization_barrier(
        (wide_grad, grads_all, outer_mine, outer_theirs)
    )
    wide_half = lax.psum_scatter(wide_grad, ("row", "core"), scatter_dimension=0, tiled=True)
    wide_half = wide_half.reshape(share, 2, -1)
    outer_arrived = swap_seq(outer_theirs)

    split = pairs - 1
    back = lambda first, count, grads: attend_back(
        first, count, 2 * dp_size, heads_rows, grads, wide_attended, tables, row_end, logsum,
        turned_inputs, turn_back, turn, back_scalars, score_scale,
    )
    heads_columns = lambda first, last: heads_matrix[:, first * 384 : last * 384]
    early_heads, early_parts = back(0, split, grads_all)
    flat = lambda parts: parts.reshape(dp_size, -1, 128)
    early_heads, early_parts, outer_arrived = lax.optimization_barrier((early_heads, early_parts, outer_arrived))
    outer_parts = scatter_end(outer_mine, outer_arrived)
    parts = scatter_end(*scatter_start([flat(early_parts), flat(outer_parts)], *table_order[0]))
    early_sent = times_transpose(early_heads[rows:], heads_columns(0, split)).astype(bf16)
    grads_all, parts, early_sent = lax.optimization_barrier((grads_all, parts, early_sent))
    early_theirs = swap_seq(early_sent)
    parts, parts_flip = scatter_start([parts], *table_order[1])
    late_heads, late_parts = back(split, 1, grads_all)
    late_heads, late_parts, parts_flip, early_theirs, wide_half, early_heads = lax.optimization_barrier(
        (late_heads, late_parts, parts_flip, early_theirs, wide_half, early_heads)
    )
    late_theirs = swap_seq(late_heads[rows:])
    late_parts = flat(late_parts)
    parts = scatter_end(parts, parts_flip)
    own_half = lax.dynamic_index_in_dim(wide_half, seq_index, 1, keepdims=False)
    their_half = lax.dynamic_index_in_dim(wide_half, 1 - seq_index, 1, keepdims=False)
    wide_sum = own_half.astype(f32) + swap_seq(their_half).astype(f32)
    late_parts = scatter_end(*scatter_start([late_parts], *table_order[0]))
    late_parts, wide_sum, early_heads = lax.optimization_barrier((late_parts, wide_sum, early_heads))
    for step in table_order[1:]:
        late_parts = scatter_end(*scatter_start([late_parts], *step))
    for step in table_order[2:]:
        parts = scatter_end(*scatter_start([parts], *step))
    lines = late_parts.shape[1] // 2
    outer_parts = parts[0, 2 * split * lines :]
    all_parts = jnp.concatenate(
        [parts[0, : 2 * split * lines].reshape(split, 2, lines, 128), late_parts[0].reshape(1, 2, lines, 128)], axis=0
    )
    own_sums, their_sums = all_parts[:, 0], swap_seq(all_parts[:, 1])
    input_grad = (
        grad_summed
        + times_transpose(early_heads[:rows], heads_columns(0, split))
        + times_transpose(late_heads[:rows], heads_columns(split, pairs))
        + early_theirs.astype(f32)
        + times_transpose(late_theirs, their_columns)
    )

    both_sums = jnp.stack(
        [jnp.where(first_seq, own_sums, their_sums), jnp.where(first_seq, their_sums, own_sums)]
    ).astype(f32)
    table_lines = 2 * mask_rows * lanes
    table_grad = both_sums[:, :, :table_lines].reshape(2, pairs, 2, lanes, mask_rows, 128)
    table_grad = table_grad.transpose(0, 1, 2, 4, 3, 5).reshape(heads, mask_rows, tsize)
    mask_logits_gradient = (
        4.0 * table_grad * smoothed_gate * (1.0 - smoothed_gate) / softening_scale[:, None, None]
    )
    heads_lines = both_sums[:, :, table_lines:].reshape(2, pairs, 3, LINES, 128)
    heads_grad = heads_lines[:, :, :, :share].transpose(2, 3, 0, 1, 4).reshape(3, share, width)
    head_bias = own_sums[:, table_lines:].reshape(pairs, 3, LINES, 128)[:, :, share].astype(f32)

    vector_columns = wide_sum[:, width + inner :]
    piece = lambda index: vector_columns[:, index]

    def bias_piece(index):
        return lax.dynamic_slice_in_dim(head_bias[:, index].reshape(half_width), dp_index * share, share)

    inner_sum = wide_sum[:, width : width + inner].reshape(share, hidden_blocks, 2 * dp_size, share)
    inner_sum = inner_sum.transpose(0, 2, 1, 3).reshape(share, inner)
    outer_sum = outer_parts.reshape(width // 128, inner_share, 128).transpose(1, 0, 2).reshape(inner_share, width)
    outer_sum = outer_sum.astype(f32)
    inner_piece = vector_columns[:, 6 : 6 + hidden_blocks].T.reshape(inner_share)
    return (
        layer_out[None],
        input_grad[None],
        heads_grad[0],
        bias_piece(0),
        heads_grad[1],
        heads_grad[2],
        bias_piece(2),
        wide_sum[:, :width],
        piece(0),
        piece(1),
        piece(2),
        inner_sum,
        inner_piece,
        outer_sum,
        piece(3),
        piece(4),
        piece(5),
        mask_logits_gradient,
    )


def solution(mesh):
    split = jax.sharding.Mesh(
        mesh.devices.reshape(2, -1, 2), ("seq", "row", "core")
    )
    return jax.shard_map(
        body,
        mesh=split,
        in_specs=(
            P(("row", "core"), "seq", None),
            P(("row", "core"), "seq", None),
            P(("row", "core"), None),
            P(("row", "core"), None),
            P(("seq", "row", "core"), None),
            P(("seq", "row", "core")),
            P(("seq", "row", "core"), None),
            P(("seq", "row", "core"), None),
            P(("seq", "row", "core")),
            P(("seq", "row", "core"), None),
            P(("seq", "row", "core")),
            P(("seq", "row", "core")),
            P(("seq", "row", "core")),
            P(("seq", "row", "core"), None),
            P(("seq", "row", "core")),
            P(("seq", "row", "core"), None),
            P(("seq", "row", "core")),
            P(("seq", "row", "core")),
            P(("seq", "row", "core")),
            P(None, ("seq", "row", "core"), None),
            P(None, ("seq", "row", "core"), None),
            P(),
        ),
        out_specs=(
            P(("row", "core"), "seq", None),
            P(("row", "core"), "seq", None),
            P(("seq", "row", "core"), None),
            P(("seq", "row", "core")),
            P(("seq", "row", "core"), None),
            P(("seq", "row", "core"), None),
            P(("seq", "row", "core")),
            P(("seq", "row", "core"), None),
            P(("seq", "row", "core")),
            P(("seq", "row", "core")),
            P(("seq", "row", "core")),
            P(("seq", "row", "core"), None),
            P(("seq", "row", "core")),
            P(("seq", "row", "core"), None),
            P(("seq", "row", "core")),
            P(("seq", "row", "core")),
            P(("seq", "row", "core")),
            P(None, ("seq", "row", "core"), None),
        ),
        check_vma=False,
    )
```
